32 devices in a mesh: dp: 8 (over y, x, core), seq: 4 (over z).
Axes of the slice: x: 2, y: 2, z: 4, core: 2. Of those that a mesh axis runs over, the one named last changes fastest.
Arguments:
- tokens: bfloat16 [16, 1024, 2048], P('dp', 'seq'), may hold values from -6 to 6
- token_types: int32 [16, 1024], P('dp', 'seq'), may hold values from 0 to 3
- view_mask: int32 [16], P('dp'), may hold values from 0 to 1
- type_table: bfloat16 [4, 2048], P(None, 'seq'), may hold values from -3 to 3
- ln1_gain: bfloat16 [2048], P('seq'), may hold values from 0.25 to 1.75
- ln1_bias: bfloat16 [2048], P('seq'), may hold values from -2 to 2
- w_qkv: bfloat16 [2048, 6144], P('dp', 'seq'), may hold values from -0.125 to 0.125
- w_out: bfloat16 [2048, 2048], P('dp', 'seq'), may hold values from -1.5 to 1.5
- ln2_gain: bfloat16 [2048], P('seq'), may hold values from 0.25 to 1.75
- ln2_bias: bfloat16 [2048], P('seq'), may hold values from -2 to 2
- w_up: bfloat16 [2048, 8192], P('dp', 'seq'), may hold values from -0.125 to 0.125
- w_down: bfloat16 [8192, 2048], P('seq', 'dp'), may hold values from -0.0625 to 0.0625
- cotangent: bfloat16 [16, 1024, 2048], P('dp', 'seq'), may hold values from -6 to 6
Outputs:
- output: bfloat16 [16, 1024, 2048], P('dp', 'seq')
- input_grad: float32 [16, 1024, 2048], P('dp', 'seq')
- grad_type_table: float32 [4, 2048], P(None, ('dp', 'seq'))
- grad_ln1_gain: float32 [2048], P(('dp', 'seq'))
- grad_ln1_bias: float32 [2048], P(('dp', 'seq'))
- grad_w_qkv: float32 [2048, 6144], P('dp', 'seq')
- grad_w_out: float32 [2048, 2048], P('dp', 'seq')
- grad_ln2_gain: float32 [2048], P(('dp', 'seq'))
- grad_ln2_bias: float32 [2048], P(('dp', 'seq'))
- grad_w_up: float32 [2048, 8192], P('dp', 'seq')
- grad_w_down: float32 [8192, 2048], P('seq', 'dp')
The draws below stay inside these ranges and needn't reach their ends.
Inputs may be any that keep to these rules, and one draw needn't show every extreme that they name: `view_mask`: 1 marks a sequence whose timesteps hold two camera views; 0 one whose second view of 256 tokens in each timestep is padding.
All inputs are finite; a program needn't handle non-finite values.
Results may differ from the reference program's by a relative error of at most 0.019.
Values may be sent and summed in bfloat16 or wider, within the bound.
A program may use at most 256 MiB of HBM per device.

```python
import math
import jax
import jax.numpy as jnp
from jax import lax

D = 2048
HEADS = 16
HEAD_DIM = 128
FF = 8192
TYPES = 4
LEN = 1024
SEQUENCES = 16
STEP = 512
VIEW = 256


def plant(drawn, rng, smallest, high):
    longest = drawn.shape.index(max(drawn.shape))
    spots = []
    for shift in (0, 1):
        where = [jax.random.randint(jax.random.fold_in(rng, axis), (), 0, length) for axis, length in enumerate(drawn.shape)]
        where[longest] = (where[longest] + shift) % drawn.shape[longest]
        spots.append(tuple(where))
    return drawn.at[spots[0]].set(smallest).at[spots[1]].set(high)


def steps_of(own_key, extent, split, low, high):
    level = 1.0
    for axis_at, blocks in split:
        heights = jax.random.uniform(jax.random.fold_in(jax.random.fold_in(own_key, 6), axis_at), (blocks,), jnp.float32, low / len(split), high / len(split))
        level = level * jnp.repeat(jnp.exp(heights), extent[axis_at] // blocks).reshape((-1,) + (1,) * (len(extent) - 1 - axis_at))
    return level


def noise(key, dims, width, bound, pieces=(), held_as=jnp.bfloat16):
    level = steps_of(key, dims, pieces, -0.22, 0.18) if pieces else 1.0
    values = jax.random.normal(key, dims, jnp.float32) * width * level
    return jnp.minimum(jnp.maximum(values, -bound), bound).astype(held_as)


def setup_inputs(seed: int = 0) -> dict:
    splits = jax.random.split(jax.random.key(seed), 14)
    tokens = noise(splits[0], (SEQUENCES, LEN, D), 1.0, 6.0, ((0, 8), (1, 4)))
    token_types = plant(jax.random.randint(splits[1], (SEQUENCES, LEN), 0, TYPES), jax.random.fold_in(splits[1], 1), 0, TYPES - 1).astype(jnp.int32)
    view_mask = plant(jax.random.randint(splits[2], (SEQUENCES,), 0, 2), jax.random.fold_in(splits[2], 1), 0, 1).astype(jnp.int32)
    type_table = noise(splits[3], (TYPES, D), 0.5, 3.0, ((1, 4),))
    ln1_gain = jnp.clip(1.0 + 0.15 * jax.random.normal(splits[4], (D,), jnp.float32), 0.25, 1.75).astype(jnp.bfloat16)
    ln1_bias = noise(splits[5], (D,), 0.3, 2.0, ((0, 4),))
    w_qkv = noise(splits[6], (D, 3 * D), D ** -0.5, 0.125, ((0, 8), (1, 4)))
    w_out = noise(splits[7], (D, D), (D // 128) ** -0.5, 1.5, ((0, 8), (1, 4)))
    ln2_gain = jnp.clip(1.0 + 0.15 * jax.random.normal(splits[8], (D,), jnp.float32), 0.25, 1.75).astype(jnp.bfloat16)
    ln2_bias = noise(splits[9], (D,), 0.3, 2.0, ((0, 4),))
    w_up = noise(splits[10], (D, FF), D ** -0.5, 0.125, ((0, 8), (1, 4)))
    w_down = noise(splits[11], (FF, D), FF ** -0.5, 0.0625, ((0, 4), (1, 8)))
    cotangent = noise(splits[12], (SEQUENCES, LEN, D), 1.0, 6.0, ((0, 8), (1, 4)))
    return {"tokens": tokens, "token_types": token_types, "view_mask": view_mask, "type_table": type_table, "ln1_gain": ln1_gain, "ln1_bias": ln1_bias, "w_qkv": w_qkv, "w_out": w_out, "ln2_gain": ln2_gain, "ln2_bias": ln2_bias, "w_up": w_up, "w_down": w_down, "cotangent": cotangent}


EPS = 1e-05
NEGATIVE = -1e+30
HIGHEST_PRECISION = lax.Precision.HIGHEST

@jax.custom_vjp
def low(v):
    return lax.optimization_barrier(v.astype(jnp.bfloat16)).astype(jnp.float32)

@jax.custom_vjp
def low_back(v):
    return v

def low_keep(v):
    return (low(v), None)

def low_pass(kept, grad):
    return (grad,)

def back_keep(v):
    return (v, None)

def back_low(kept, grad):
    return (low(grad),)
low.defvjp(low_keep, low_pass)
low_back.defvjp(back_keep, back_low)

def layer_norm(hidden, gain, bias):
    average = lax.optimization_barrier(jnp.mean(hidden, axis=-1, keepdims=True))
    centered = hidden - average
    variance = lax.optimization_barrier(jnp.mean(centered * centered, axis=-1, keepdims=True))
    return centered * lax.rsqrt(variance + EPS) * gain + bias

def gelu_tanh(value):
    inner = math.sqrt(2.0 / math.pi) * (value + 0.044715 * value * value * value)
    return 0.5 * value * (1.0 + jnp.tanh(inner))

def product(left, right):
    return jnp.matmul(left, right, precision=HIGHEST_PRECISION)

def forward(hidden_in, onehot, allowed, table, gain_one, bias_one, qkv_weight, out_weight, gain_two, bias_two, up_weight, down_weight):
    group = hidden_in.shape[0]
    scale = 1.0 / math.sqrt(HEAD_DIM)
    start_hidden = hidden_in + product(onehot, table)
    normed_one = low(layer_norm(start_hidden, gain_one, bias_one))
    projected = low(low_back(product(normed_one, qkv_weight))).reshape(group, LEN, HEADS, 3, HEAD_DIM)
    query = projected[:, :, :, 0]
    keys = projected[:, :, :, 1]
    values = projected[:, :, :, 2]
    scores = low_back(jnp.einsum('gqhd,gkhd->ghqk', query, keys, precision=HIGHEST_PRECISION) * scale)
    scores = jnp.where(allowed, scores, NEGATIVE)
    top = lax.optimization_barrier(jnp.max(scores, axis=-1, keepdims=True))
    expd = jnp.exp(scores - top)
    probs = low(expd / lax.optimization_barrier(jnp.sum(expd, axis=-1, keepdims=True)))
    context = low(low_back(jnp.einsum('ghqk,gkhd->gqhd', probs, values, precision=HIGHEST_PRECISION)))
    context = context.reshape(group, LEN, HEADS * HEAD_DIM)
    mid_hidden = start_hidden + low_back(product(context, out_weight))
    normed_two = low(layer_norm(mid_hidden, gain_two, bias_two))
    activated = low(gelu_tanh(low_back(product(normed_two, up_weight))))
    return mid_hidden + low_back(product(activated, down_weight))

def reference(tokens, token_types, view_mask, type_table, ln1_gain, ln1_bias, w_qkv, w_out, ln2_gain, ln2_bias, w_up, w_down, cotangent):
    weights = tuple((w.astype(jnp.float32) for w in (type_table, ln1_gain, ln1_bias, w_qkv, w_out, ln2_gain, ln2_bias, w_up, w_down)))
    group = math.gcd(SEQUENCES, max(1, 4096 // LEN))
    count = SEQUENCES // group
    positions = jnp.arange(LEN, dtype=jnp.int32)
    causal = positions[None, :] <= positions[:, None]
    first_view = positions % STEP < VIEW

    def one(carry, item):
        hidden_in, types, views, cot = item
        onehot = (types[..., None] == jnp.arange(TYPES, dtype=jnp.int32)).astype(jnp.float32)
        seen = jnp.logical_or(views[:, None] == 1, first_view[None, :])
        allowed = jnp.logical_and(causal[None, None], seen[:, None, None, :])

        def run(hidden_f, *params):
            return forward(hidden_f, onehot, allowed, *params)
        result, pull = jax.vjp(run, hidden_in.astype(jnp.float32), *weights)
        grads = pull(cot.astype(jnp.float32))
        carry = tuple((total + grad for total, grad in zip(carry, grads[1:])))
        return (carry, (result.astype(jnp.bfloat16), grads[0]))
    items = (tokens.reshape(count, group, LEN, D), token_types.reshape(count, group, LEN), view_mask.reshape(count, group), cotangent.reshape(count, group, LEN, D))
    zeros = tuple((jnp.zeros(w.shape, jnp.float32) for w in weights))
    totals, (outputs, input_grads) = lax.scan(one, zeros, items)
    return (outputs.reshape(SEQUENCES, LEN, D), input_grads.reshape(SEQUENCES, LEN, D), totals[0], totals[1], totals[2], totals[3], totals[4], totals[5], totals[6], totals[7], totals[8])
```

```python
import math

import jax
import jax.numpy as jnp
from jax import lax
from jax.experimental import pallas as pl
from jax.experimental.pallas import tpu as pltpu
from jax.sharding import PartitionSpec as P

HEADS = 16
HEAD_DIM = 128
TYPES = 4


EPS = 1e-05
NEGATIVE = -1e30
HIGHEST_PRECISION = lax.Precision.HIGHEST


def layer_norm(hidden, gain, bias):
    average = jnp.mean(hidden, axis=-1, keepdims=True)
    centered = hidden - average
    variance = jnp.mean(centered * centered, axis=-1, keepdims=True)
    return centered * lax.rsqrt(variance + EPS) * gain + bias


def gelu_tanh(value):
    inner = math.sqrt(2.0 / math.pi) * (value + 0.044715 * value * value * value)
    return 0.5 * value * (1.0 + jnp.tanh(inner))


def key_allowed(first, count, full_len, view_flag):
    query_pos = first + jnp.arange(count, dtype=jnp.int32)
    key_pos = jnp.arange(full_len, dtype=jnp.int32)
    causal = key_pos[None, :] <= query_pos[:, None]
    seen = jnp.logical_or(view_flag == 1, key_pos % (full_len // 2) < full_len // 4)
    return jnp.logical_and(causal, seen[None, :])


def scores_of(query, keys, allowed, scale):
    plain = jnp.einsum("qhd,khd->hqk", query, keys, preferred_element_type=jnp.float32) * scale
    return jnp.where(allowed[None], plain, NEGATIVE)


def to_heads(values_in):
    return lax.all_to_all(values_in, "seq", split_axis=2, concat_axis=1, tiled=True)


def to_tokens(values_in):
    return lax.all_to_all(values_in, "seq", split_axis=1, concat_axis=2, tiled=True)


def plain_shards(
    tokens,
    token_types,
    view_mask,
    type_table,
    ln1_gain,
    ln1_bias,
    w_qkv,
    w_out,
    ln2_gain,
    ln2_bias,
    w_up,
    w_down,
    cotangent,
):
    seq_count, local_len, width = tokens.shape
    groups = lax.axis_size("seq")
    full_len = local_len * groups
    row_count = seq_count * local_len
    local_heads = HEADS // groups
    scale = 1.0 / math.sqrt(HEAD_DIM)
    block = min(512, full_len)
    f32 = jnp.float32
    bf16 = jnp.bfloat16
    out_part, table, gain_one, bias_one, gain_two, bias_two = (
        lax.all_gather(w_out, "seq", axis=1, tiled=True),
        lax.all_gather(type_table, "seq", axis=1, tiled=True),
        lax.all_gather(ln1_gain, "seq", axis=0, tiled=True),
        lax.all_gather(ln1_bias, "seq", axis=0, tiled=True),
        lax.all_gather(ln2_gain, "seq", axis=0, tiled=True),
        lax.all_gather(ln2_bias, "seq", axis=0, tiled=True),
    )
    qkv_full, out_full, up_full, down_full = (
        lax.all_gather(w_qkv, "dp", axis=0, tiled=True),
        lax.all_gather(out_part, "dp", axis=0, tiled=True),
        lax.all_gather(w_up, "dp", axis=0, tiled=True),
        lax.all_gather(w_down, "dp", axis=1, tiled=True),
    )
    onehot = (
        token_types.reshape(row_count)[:, None] == jnp.arange(TYPES, dtype=jnp.int32)[None, :]
    ).astype(f32)
    start_hidden = tokens.reshape(row_count, width).astype(f32) + jnp.dot(
        onehot, table.astype(f32), precision=HIGHEST_PRECISION
    )
    norm_one, pull_one = jax.vjp(
        layer_norm, start_hidden, gain_one.astype(f32), bias_one.astype(f32)
    )
    normed_one = norm_one.astype(bf16)
    normed_rows = lax.all_gather(
        normed_one.reshape(seq_count, local_len, width), "seq", axis=1, tiled=True
    )
    by_heads = jnp.einsum("std,de->ste", normed_rows, qkv_full, preferred_element_type=f32).astype(
        bf16
    )
    by_heads = by_heads.reshape(seq_count, full_len, local_heads, 3, HEAD_DIM)
    contexts = []
    kept_lse = []
    for index in range(seq_count):
        keys = by_heads[index, :, :, 1]
        values = by_heads[index, :, :, 2]
        context_blocks = []
        lse_blocks = []
        for first in range(0, full_len, block):
            query = by_heads[index, first : first + block, :, 0]
            allowed = key_allowed(first, block, full_len, view_mask[index])
            scores = scores_of(query, keys, allowed, scale)
            top = jnp.max(scores, axis=-1, keepdims=True)
            expd = jnp.exp(scores - top)
            total = jnp.sum(expd, axis=-1, keepdims=True)
            probs_low = (expd / total).astype(bf16)
            context_blocks.append(
                jnp.einsum("hqk,khd->qhd", probs_low, values, preferred_element_type=f32).astype(
                    bf16
                )
            )
            lse_blocks.append(top + jnp.log(total))
        contexts.append(jnp.concatenate(context_blocks, axis=0))
        kept_lse.append(lse_blocks)
    context_heads = jnp.stack(contexts)
    context_rows = to_tokens(context_heads).reshape(row_count, width)
    mid_hidden = start_hidden + jnp.dot(context_rows, out_full, preferred_element_type=f32)
    norm_two, pull_two = jax.vjp(layer_norm, mid_hidden, gain_two.astype(f32), bias_two.astype(f32))
    normed_two = norm_two.astype(bf16)
    cot_rows = cotangent.reshape(row_count, width)
    ffn_input, grad_rows = (
        lax.all_gather(normed_two, "seq", axis=0, tiled=True),
        lax.all_gather(cot_rows, "seq", axis=0, tiled=True),
    )
    up_value = jnp.dot(ffn_input, up_full, preferred_element_type=f32)
    activated, gelu_pull = jax.vjp(gelu_tanh, up_value)
    activated_low = activated.astype(bf16)
    piece = activated_low
    ffn_out = lax.psum_scatter(
        jnp.dot(piece, down_full, preferred_element_type=f32).astype(jnp.bfloat16),
        "seq",
        scatter_dimension=0,
        tiled=True,
    ).astype(jnp.float32)
    output = (mid_hidden + ffn_out).astype(bf16).reshape(seq_count, local_len, width)
    grad_down = jnp.einsum("ti,td->id", activated_low, grad_rows, preferred_element_type=f32)
    grad_act = jnp.einsum("td,id->ti", grad_rows, down_full, preferred_element_type=f32)
    grad_up_value = gelu_pull(grad_act)[0].astype(bf16)
    grad_up = jnp.einsum("td,ti->di", ffn_input, grad_up_value, preferred_element_type=f32)
    piece = grad_up_value
    grad_normed_two = lax.psum_scatter(
        jnp.einsum("ti,di->td", piece, up_full, preferred_element_type=f32).astype(jnp.bfloat16),
        "seq",
        scatter_dimension=0,
        tiled=True,
    ).astype(jnp.float32)
    grad_mid_norm, grad_gain_two, grad_bias_two = pull_two(grad_normed_two)
    grad_mid = cot_rows.astype(f32) + grad_mid_norm
    grad_mid_low = grad_mid.astype(bf16)
    grad_out_weight = jnp.einsum(
        "td,te->de", context_rows, grad_mid_low, preferred_element_type=f32
    )
    grad_context = jnp.einsum(
        "te,de->td", grad_mid_low, out_full, preferred_element_type=f32
    ).astype(bf16)
    grad_context = grad_context.reshape(seq_count, local_len, HEADS, HEAD_DIM)
    grad_by_heads = to_heads(grad_context)
    grad_parts = []
    for index in range(seq_count):
        keys = by_heads[index, :, :, 1]
        values = by_heads[index, :, :, 2]
        grad_keys = jnp.zeros(keys.shape, f32)
        grad_values = jnp.zeros(values.shape, f32)
        grad_query_blocks = []
        for number, first in enumerate(range(0, full_len, block)):
            query = by_heads[index, first : first + block, :, 0]
            allowed = key_allowed(first, block, full_len, view_mask[index])
            scores = scores_of(query, keys, allowed, scale)
            probs = jnp.exp(scores - kept_lse[index][number])
            probs_low = probs.astype(bf16)
            grad_block = grad_by_heads[index, first : first + block]
            grad_values = grad_values + jnp.einsum(
                "hqk,qhd->khd", probs_low, grad_block, preferred_element_type=f32
            )
            grad_probs = jnp.einsum("qhd,khd->hqk", grad_block, values, preferred_element_type=f32)
            weighted = jnp.sum(probs * grad_probs, axis=-1, keepdims=True)
            grad_scores = (probs * (grad_probs - weighted)).astype(bf16)
            grad_query_blocks.append(
                jnp.einsum("hqk,khd->qhd", grad_scores, keys, preferred_element_type=f32) * scale
            )
            grad_keys = (
                grad_keys
                + jnp.einsum("hqk,qhd->khd", grad_scores, query, preferred_element_type=f32) * scale
            )
        grad_parts.append(
            jnp.stack([jnp.concatenate(grad_query_blocks, axis=0), grad_keys, grad_values], axis=2)
        )
    grad_projected = jnp.stack(grad_parts).astype(bf16)
    columns = qkv_full.shape[1]
    grad_flat = grad_projected.reshape(seq_count, full_len, columns)
    grad_qkv_weight = jnp.einsum("std,ste->de", normed_rows, grad_flat, preferred_element_type=f32)
    position_major = jnp.transpose(grad_flat, (1, 0, 2)).reshape(full_len * seq_count, columns)
    piece = position_major
    summed_rows = lax.psum_scatter(
        jnp.einsum("te,de->td", piece, qkv_full, preferred_element_type=f32).astype(jnp.bfloat16),
        "seq",
        scatter_dimension=0,
        tiled=True,
    ).astype(jnp.float32)
    grad_normed_one = jnp.transpose(
        summed_rows.reshape(local_len, seq_count, width), (1, 0, 2)
    ).reshape(row_count, width)
    grad_start_norm, grad_gain_one, grad_bias_one = pull_one(grad_normed_one)
    grad_start = grad_mid + grad_start_norm
    input_grad = grad_start.reshape(seq_count, local_len, width)
    grad_table = jnp.einsum("tk,td->kd", onehot, grad_start, precision=HIGHEST_PRECISION)
    (
        sum_qkv,
        sum_out,
        sum_up,
        sum_down,
        sum_table,
        sum_gain_one,
        sum_bias_one,
        sum_gain_two,
        sum_bias_two,
    ) = (
        lax.psum_scatter(
            grad_qkv_weight.astype(jnp.bfloat16), "dp", scatter_dimension=0, tiled=True
        ).astype(jnp.float32),
        lax.psum_scatter(
            grad_out_weight.astype(jnp.bfloat16), "dp", scatter_dimension=0, tiled=True
        ).astype(jnp.float32),
        lax.psum_scatter(
            grad_up.astype(jnp.bfloat16), "dp", scatter_dimension=0, tiled=True
        ).astype(jnp.float32),
        lax.psum_scatter(
            grad_down.astype(jnp.bfloat16), "dp", scatter_dimension=1, tiled=True
        ).astype(jnp.float32),
        lax.psum_scatter(
            grad_table.astype(jnp.bfloat16), "dp", scatter_dimension=1, tiled=True
        ).astype(jnp.float32),
        lax.psum_scatter(
            grad_gain_one.astype(jnp.bfloat16), "dp", scatter_dimension=0, tiled=True
        ).astype(jnp.float32),
        lax.psum_scatter(
            grad_bias_one.astype(jnp.bfloat16), "dp", scatter_dimension=0, tiled=True
        ).astype(jnp.float32),
        lax.psum_scatter(
            grad_gain_two.astype(jnp.bfloat16), "dp", scatter_dimension=0, tiled=True
        ).astype(jnp.float32),
        lax.psum_scatter(
            grad_bias_two.astype(jnp.bfloat16), "dp", scatter_dimension=0, tiled=True
        ).astype(jnp.float32),
    )
    final_out, final_table, final_gain_one, final_bias_one, final_gain_two, final_bias_two = (
        lax.psum_scatter(
            sum_out.astype(jnp.bfloat16), "seq", scatter_dimension=1, tiled=True
        ).astype(jnp.float32),
        lax.psum_scatter(
            sum_table.astype(jnp.bfloat16), "seq", scatter_dimension=1, tiled=True
        ).astype(jnp.float32),
        lax.psum_scatter(
            sum_gain_one.astype(jnp.bfloat16), "seq", scatter_dimension=0, tiled=True
        ).astype(jnp.float32),
        lax.psum_scatter(
            sum_bias_one.astype(jnp.bfloat16), "seq", scatter_dimension=0, tiled=True
        ).astype(jnp.float32),
        lax.psum_scatter(
            sum_gain_two.astype(jnp.bfloat16), "seq", scatter_dimension=0, tiled=True
        ).astype(jnp.float32),
        lax.psum_scatter(
            sum_bias_two.astype(jnp.bfloat16), "seq", scatter_dimension=0, tiled=True
        ).astype(jnp.float32),
    )
    return (
        output,
        input_grad,
        final_table,
        final_gain_one,
        final_bias_one,
        sum_qkv,
        final_out,
        final_gain_two,
        final_bias_two,
        sum_up,
        sum_down,
    )


PLANE = 8
QUAD = 4
F32 = jnp.float32
BF16 = jnp.bfloat16
MESH_ID = pl.DeviceIdType.MESH
CORE, X_WAY, Y_WAY = 1, 2, 4
FAR_FIRST = (6, 7, 2, 3, 4, 5, 1)


def swap(value, mask):
    dp = lax.axis_size("dp")
    return lax.ppermute(value, "dp", [(i, i ^ mask) for i in range(dp)])


def after(value, *earlier):
    return lax.optimization_barrier((value, earlier))[0]


def at_plane(d, z):
    return dict(device_id=(d, z), device_id_type=MESH_ID)


class Moves:
    def __init__(self, send_sem, recv_sem, local_sem=None):
        self.sems = (send_sem, recv_sem, local_sem)
        self.count = [0, 0]
        self.open = []

    def far(self, source, target, d, z, sends=None, receives=None, lands=None):
        number = self.count[0]
        self.count[0] += 1

        def copy(landing):
            return pltpu.make_async_remote_copy(
                src_ref=source,
                dst_ref=target,
                send_sem=self.sems[0].at[number],
                recv_sem=self.sems[1].at[landing],
                **at_plane(d, z),
            )

        out = copy(number if lands is None else lands)
        when(sends, out.start)
        move = [(out, copy(number)), sends, receives, False]
        self.open.append(move)
        return move

    def here(self, source, target, sends=None):
        number = self.count[1]
        self.count[1] += 1
        copy = pltpu.make_async_copy(source, target, self.sems[2].at[number])
        when(sends, copy.start)
        move = [copy, sends, None, False]
        self.open.append(move)
        return move

    def landed(self, move):
        copy, sends, receives, done = move
        assert not done
        move[3] = True
        if isinstance(copy, tuple):
            when(receives, copy[1].wait_recv)
        else:
            when(sends, copy.wait)

    def finish(self):
        for move in self.open:
            if not move[3]:
                self.landed(move)
            if isinstance(move[0], tuple):
                when(move[1], move[0][0].wait_send)


def when(condition, do):
    if condition is None:
        do()
    else:
        pl.when(condition)(do)


def meet_all(masks, lines=True, peers=False):
    d = lax.axis_index("dp")
    z = lax.axis_index("seq")
    groups = lax.axis_size("seq")
    barrier = pltpu.get_barrier_semaphore()
    count = len(masks)
    for mask in masks:
        pl.semaphore_signal(barrier, inc=1, **at_plane(d ^ mask, z))
    if lines:
        count = count + groups - 1
        for step in range(1, groups):
            pl.semaphore_signal(barrier, inc=1, **at_plane(d, (z + step) % groups))
    if peers:
        for number in range(2):
            to_d, to_z, itself = peer_of(number)
            away = jnp.logical_not(itself)

            def signal(to_d=to_d, to_z=to_z):
                pl.semaphore_signal(barrier, inc=1, **at_plane(to_d, to_z))

            when(away, signal)
            count = count + jnp.where(itself, 0, 1)
    pl.semaphore_wait(barrier, count)


def peer_of(number):
    d = lax.axis_index("dp")
    z = lax.axis_index("seq")
    core = d & 1
    to_d = (d - core) + (z >> 1)
    to_z = 2 * core + number
    return to_d, to_z, jnp.logical_and(to_d == d, to_z == z)


def exchange_along_z(moves, number, source, target, base=None):
    z = lax.axis_index("seq")
    base = moves.count[0] - number if base is None else base
    to_d, to_z, itself = peer_of(number)
    away = jnp.logical_not(itself)
    far = moves.far(source, target(z & 1), to_d, to_z, away, away, base + (z & 1))
    near = moves.here(source, target(z & 1), itself)
    return far, near


def all_landed(moves, landing):
    for move in landing:
        moves.landed(move)


def intake_kernel(small_ref, mark_ref, qkv_ref, whole_ref, marks_ref, half_ref, *sems):
    moves = Moves(*sems)
    d = lax.axis_index("dp")
    z = lax.axis_index("seq")
    groups = lax.axis_size("seq")
    meet_all(range(1, PLANE))
    moves.here(small_ref, whole_ref.at[z])
    for step in range(1, groups):
        moves.far(small_ref, whole_ref.at[z], d, (z + step) % groups)
    moves.here(mark_ref, marks_ref.at[0])
    for mask in range(1, PLANE):
        moves.far(mark_ref, marks_ref.at[mask], d ^ mask, z)
    spread_columns(moves, qkv_ref, half_ref)
    moves.finish()


def spread_columns(moves, shard, half):
    d = lax.axis_index("dp")
    z = lax.axis_index("seq")
    part, width = half.shape[0], shard.shape[1]
    target = half.at[:, pl.ds(pl.multiple_of(d * width, 128), width)]

    def rows(mask):
        return shard.at[pl.ds(pl.multiple_of((d ^ mask) * part, 64), part)]

    moves.here(rows(0), target)
    for mask in FAR_FIRST:
        moves.far(rows(mask), target, d ^ mask, z)


def kernel_call(
    kernel, inputs, outputs, far, here, number, name, traffic, spaces=None, scratch=(), late=()
):
    count = len(inputs)

    def body(*refs):
        kernel(*refs[:count], *refs[count + len(late) :])

    return pl.pallas_call(
        body,
        out_shape=outputs,
        in_specs=[pl.BlockSpec(memory_space=space) for space in spaces or [pltpu.VMEM] * count]
        + [pl.BlockSpec(memory_space=pl.ANY)] * len(late),
        out_specs=[pl.BlockSpec(memory_space=pl.ANY)] * len(outputs),
        scratch_shapes=[
            *scratch,
            pltpu.SemaphoreType.DMA((far,)),
            pltpu.SemaphoreType.DMA((far,)),
            pltpu.SemaphoreType.DMA((here,)),
        ],
        compiler_params=pltpu.CompilerParams(
            collective_id=number, has_side_effects=True, vmem_limit_bytes=56 * 1024 * 1024
        ),
        cost_estimate=pl.CostEstimate(
            flops=0, bytes_accessed=traffic * 3 * 1024 * 1024, transcendentals=0
        ),
        name=name,
    )(*inputs, *late)


def shaped(*shape):
    return jax.ShapeDtypeStruct(shape, BF16)


def intake(small, mark, qkv_shard):
    groups = lax.axis_size("seq")
    units, width = qkv_shard.shape
    return kernel_call(
        intake_kernel,
        [small, mark, qkv_shard],
        [
            shaped(groups, *small.shape),
            jax.ShapeDtypeStruct((PLANE,) + mark.shape, mark.dtype),
            shaped(units // PLANE, width * PLANE),
        ],
        groups - 1 + 2 * (PLANE - 1),
        3,
        1,
        "intake",
        20,
    )


def gather_rows(moves, rows_ref, chips_ref, others_ref, ready=None, pieces=2):
    d = lax.axis_index("dp")
    z = lax.axis_index("seq")
    size = chips_ref.shape[1] // pieces
    parts = [pl.ds(number * size, size) for number in range(pieces)]
    order = [i + j for i in range(pieces // 2) for j in (0, pieces // 2)]

    def far(source, target, mask):
        return moves.far(source, target, d ^ mask, z)

    if ready is None:
        moves.here(rows_ref, chips_ref.at[0])
    over_x = {}
    over_y = {}
    for number in order:
        part = parts[number]
        if ready is None:
            source = rows_ref.at[part]
        else:
            ready(number)
            source = chips_ref.at[0, part]
        over_x[number] = far(source, chips_ref.at[1, part], X_WAY)
        over_y[number] = far(source, chips_ref.at[2, part], Y_WAY)
        far(source, others_ref.at[0, part], CORE)

    def pass_on(chip, number):
        part = parts[number]
        far(chips_ref.at[chip, part], others_ref.at[chip, part], CORE)

    corner = {}
    for number in order:
        yield
        part = parts[number]
        first = number < pieces // 2
        via, chip, mask = (over_y, 2, X_WAY) if first else (over_x, 1, Y_WAY)
        moves.landed(via[number])
        corner[number] = far(chips_ref.at[chip, part], chips_ref.at[3, part], mask)
        pass_on(chip, number)
        moves.landed((over_x if first else over_y)[number])
        pass_on(3 - chip, number)
    yield
    for number in order:
        moves.landed(corner[number])
        pass_on(3, number)


GATHER_COPIES = 14
FIRST_PIECES = 4


def gather_along_z(moves, shard_ref, place, target):
    d = lax.axis_index("dp")
    z = lax.axis_index("seq")
    own = moves.here(shard_ref, target.at[place(z)])
    arrivals = []
    for step in (2, -2, 1, -1):
        to, source = z + step, z - step
        inside = jnp.logical_and(to >= 0, to < 4)
        comes = jnp.logical_and(source >= 0, source < 4)
        arrivals.append(
            moves.far(shard_ref, target.at[place(z)], d, jnp.clip(to, 0, 3), inside, comes)
        )
    yield
    for arrival in arrivals:
        moves.landed(arrival)
    for end, via, to in ((0, 2, 3), (3, 1, 0)):
        arrivals.append(
            moves.far(target.at[place(end)], target.at[place(end)], d, to, z == via, z == to)
        )
    yield
    for arrival in arrivals[4:] + [own]:
        moves.landed(arrival)


Z_COPIES = 6


def first_kernel(rows_ref, qkv_ref, up_ref, down_ref, *refs):
    chips, others, heads, up_half, down_half = refs[:5]
    moves = Moves(*refs[5:])
    d = lax.axis_index("dp")
    core = d & 1
    half = rows_ref.shape[1]
    meet_all(range(1, PLANE), peers=True)
    size = 2 * half // FIRST_PIECES
    landing = {}
    for piece in range(FIRST_PIECES // 2):
        for number in range(2):
            landing[number * (FIRST_PIECES // 2) + piece] = exchange_along_z(
                moves,
                number,
                rows_ref.at[number, pl.ds(piece * size, size)],
                lambda at: chips.at[
                    0, pl.ds(pl.multiple_of(at * half + piece * size, size), size)
                ],
            )
    spread_columns(moves, up_ref, up_half)
    spread_columns(moves, down_ref, down_half)

    def place(at):
        own = (at >> 1) == core
        return jnp.where(own, (at & 1) * 2 + core, 4 + (at & 1))

    qkv = gather_along_z(moves, qkv_ref, place, heads)
    next(qkv)
    rows = gather_rows(
        moves,
        None,
        chips,
        others,
        lambda number: all_landed(moves, landing[number]),
        FIRST_PIECES,
    )
    for _ in range(FIRST_PIECES):
        next(rows)
    next(qkv)
    next(rows)
    next(qkv, None)
    z = lax.axis_index("seq")
    for number in range(2):
        moves.far(heads.at[4 + number], heads.at[number * 2 + core], d ^ CORE, z)
    next(rows, None)
    moves.finish()


def first_gather(rows, qkv_half, up_shard, down_shard):
    seqs, half, width = rows.shape
    spread = [shaped(w.shape[0] // PLANE, w.shape[1] * PLANE) for w in (up_shard, down_shard)]
    return kernel_call(
        first_kernel,
        [rows, qkv_half, up_shard, down_shard],
        [
            shaped(4, seqs * half, width),
            shaped(4, seqs * half, width),
            shaped(6, *qkv_half.shape),
            *spread,
        ],
        7 * FIRST_PIECES + Z_COPIES + FIRST_PIECES + 2 + 2 * (PLANE - 1),
        3 + FIRST_PIECES,
        2,
        "first_gather",
        110,
    )


def gather_kernel(rows_ref, chips, others, *sems):
    moves = Moves(*sems)
    meet_all((CORE, X_WAY, Y_WAY), lines=False)
    for _ in gather_rows(moves, rows_ref, chips, others):
        pass
    moves.finish()


def plane_gather_now(rows, number, late):
    count, width = rows.shape
    got = kernel_call(
        gather_kernel,
        [rows],
        [shaped(4, count, width)] * 2,
        GATHER_COPIES,
        1,
        number,
        "plane_gather",
        76,
        late=late,
    )
    return [part.reshape(4 * count, width) for part in got]


def scatter_rows(moves, natural, chips_ref, others_ref, out_ref, own, got, far, near, done):
    d = lax.axis_index("dp")
    z = lax.axis_index("seq")
    half = own.shape[1] // 2
    first, second = pl.ds(0, half), pl.ds(half, half)

    def send_to(source, target, mask):
        return moves.far(source, target, d ^ mask, z)

    order = (3, 1, 2, 0)
    from_core = [send_to(others_ref.at[c], got.at[i], CORE) for i, c in enumerate(order)]
    reads = [moves.here(chips_ref.at[c], own.at[i]) for i, c in enumerate(order)]
    step = 64

    def add(target, start, sources):
        @pl.loop(0, half // step)
        def _(i):
            total = None
            for ref, offset in sources:
                piece = ref[pl.ds(pl.multiple_of(offset + i * step, step), step), :].astype(F32)
                total = piece if total is None else total + piece
            target[pl.ds(pl.multiple_of(start + i * step, step), step), :] = total.astype(
                target.dtype
            )

    def ready(i):
        moves.landed(from_core[i])
        moves.landed(reads[i])

    yield
    ready(0)
    add(own.at[0], 0, [(own.at[0], 0), (got.at[0], 0)])
    to_x = send_to(own.at[0, first], far.at[0], X_WAY)
    add(own.at[0], half, [(own.at[0], half), (got.at[0], half)])
    to_y = send_to(own.at[0, second], far.at[1], Y_WAY)
    ready(1)
    add(own.at[1], 0, [(own.at[1], 0), (got.at[1], 0)])
    x_first = send_to(own.at[1, first], near.at[0, first], X_WAY)
    ready(2)
    add(own.at[2], half, [(own.at[2], half), (got.at[2], half)])
    y_second = send_to(own.at[2, second], near.at[1, second], Y_WAY)
    yield
    moves.landed(to_y)
    add(own.at[1], half, [(own.at[1], half), (got.at[1], half), (far.at[1], 0)])
    x_second = send_to(own.at[1, second], near.at[0, second], X_WAY)
    moves.landed(to_x)
    add(own.at[2], 0, [(own.at[2], 0), (got.at[2], 0), (far.at[0], 0)])
    y_first = send_to(own.at[2, first], near.at[1, first], Y_WAY)
    ready(3)
    yield
    moves.landed(x_first)
    moves.landed(y_second)
    for number, arrivals in ((0, (y_first,)), (1, (x_second,))):
        all_landed(moves, arrivals)
        start = number * half
        add(done, start, [(own.at[3], start), (got.at[3], start), (near.at[0], start), (near.at[1], start)])
        if natural:
            exchange_along_z(
                moves,
                number,
                done.at[pl.ds(start, half)],
                lambda at: out_ref.at[at],
            )
    if not natural:
        moves.here(done, out_ref)


SCATTER_COPIES = 10


def scatter_kernel(natural, united, *refs):
    count = len(natural)
    ins, refs = refs[: 2 * count], refs[2 * count :]
    held, refs = refs[:united], refs[united:]
    outs, refs = refs[:count], refs[count:]
    shard, refs = refs[:united], refs[united:]
    buffers = refs[: 5 * count]
    moves = Moves(*refs[5 * count :])
    meet_all(range(1, PLANE) if united else (CORE, X_WAY, Y_WAY), lines=False, peers=any(natural))
    if united:
        unite_columns(moves, held[0], shard[0])
    steps = [
        scatter_rows(
            moves, natural[i], *ins[2 * i : 2 * i + 2], outs[i], *buffers[5 * i : 5 * i + 5]
        )
        for i in range(count)
    ]
    for _ in range(4):
        for step in steps:
            next(step, None)
    moves.finish()


def plane_scatter_now(parts, shapes, natural, number, late=(), united=()):
    inputs = []
    scratch = []
    for pair in parts:
        total, width = pair[0].shape
        count = total // 4
        inputs += [part.reshape(4, count, width) for part in pair]
        for lead, rows in ((4, count), (4, count), (2, count // 2), (2, count)):
            scratch.append(pltpu.VMEM((lead, rows, width), BF16))
        scratch.append(pltpu.VMEM((count, width), BF16))
    count = len(united)
    return kernel_call(
        lambda *refs: scatter_kernel(natural, count, *refs),
        inputs + list(united),
        [shaped(*shape) for shape in shapes]
        + [shaped(s.shape[0] * PLANE, s.shape[1] // PLANE) for s in united],
        SCATTER_COPIES * len(parts) + 2 + count * (PLANE - 1),
        7 * len(parts) + count,
        number,
        "plane_scatter",
        100 if any(natural) else 76,
        [pl.ANY] * len(inputs) + [pltpu.VMEM] * count,
        scratch,
        late,
    )


def unite_columns(moves, half_ref, shard_ref):
    d = lax.axis_index("dp")
    z = lax.axis_index("seq")
    part, width = half_ref.shape[0], shard_ref.shape[1]
    target = shard_ref.at[pl.ds(pl.multiple_of(d * part, 64), part)]

    def columns(mask):
        return half_ref.at[:, pl.ds(pl.multiple_of((d ^ mask) * width, 128), width)]

    moves.here(columns(0), target)
    for mask in FAR_FIRST:
        moves.far(columns(mask), target, d ^ mask, z)


def along_z(value):
    return lax.all_gather(value, "seq", axis=0, tiled=True)


def sum_along_z(grad):
    return lax.psum_scatter(grad, "seq", scatter_dimension=0, tiled=True)


def shared_heads(grad):
    heads = HEADS // PLANE
    held = grad.reshape(heads, 2, -1, grad.shape[-1])
    second = lax.axis_index("dp") % 2 == 1
    keep = jnp.where(second, held[:, 1], held[:, 0])
    other = swap(jnp.where(second, held[:, 0], held[:, 1]), CORE)
    whole = jnp.concatenate([jnp.where(second, other, keep), jnp.where(second, keep, other)])
    return whole.reshape(-1, grad.shape[-1])


def plane_gather(rows, second, third):
    half = rows.shape[0] // 2
    x_rows = swap(rows, X_WAY)
    y_rows = swap(rows, Y_WAY)
    corner_first = swap(after(y_rows[:half], second), X_WAY)
    corner_second = swap(after(x_rows[half:], second), Y_WAY)
    chips = jnp.concatenate([rows, x_rows, y_rows, after(corner_first, third), corner_second])
    return chips, swap(chips, CORE)


def plane_scatter(chips, others):
    count = chips.shape[0] // 4
    half = count // 2
    got = swap(others, CORE)

    def both(start, size):
        return chips[start : start + size].astype(F32) + got[start : start + size].astype(F32)

    far_first = swap(both(3 * count, half).astype(BF16), X_WAY)
    far_second = swap(both(3 * count + half, half).astype(BF16), Y_WAY)
    x_first = swap(both(count, half).astype(BF16), X_WAY)
    y_second = swap(both(2 * count + half, half).astype(BF16), Y_WAY)
    x_second = swap((both(count + half, half) + far_second.astype(F32)).astype(BF16), X_WAY)
    y_first = swap((both(2 * count, half) + far_first.astype(F32)).astype(BF16), Y_WAY)
    first = both(0, half) + x_first.astype(F32) + y_first.astype(F32)
    second = both(half, half) + x_second.astype(F32) + y_second.astype(F32)
    return jnp.concatenate([first, second])


def place_of(mask):
    return (mask & 1) * (PLANE // 2) + (mask >> 1)


def column_of(holder, member, number):
    head = (2 * (member & 1) + number) * (PLANE // 2) + (member >> 1)
    place = place_of(holder ^ (head >> 1))
    return pl.ds(pl.multiple_of((2 * place + (head & 1)) * HEAD_DIM, HEAD_DIM), HEAD_DIM)


def meet_heads(masks):
    d = lax.axis_index("dp")
    z = lax.axis_index("seq")
    core = d & 1
    groups = lax.axis_size("seq")
    inside = (z >> 1) == core
    barrier = pltpu.get_barrier_semaphore()

    def greet(to_d, to_z, maybe_itself):
        def signal():
            pl.semaphore_signal(barrier, inc=1, **at_plane(to_d, to_z))

        when(jnp.logical_or(to_d != d, to_z != z) if maybe_itself else None, signal)

    for line in range(PLANE // 2):
        for to_z in range(groups):
            greet(((d >> 1) ^ line) * 2 + (z >> 1), to_z, line == 0)
    for mask in range(PLANE):
        for j in range(2):
            greet(d ^ mask, 2 * core + j, mask == 0)
    for mask in masks:
        greet(d ^ mask, z, False)
    pl.semaphore_wait(barrier, 4 * PLANE + len(masks) - jnp.where(inside, 2, 0))


def contexts_home_kernel(chip_ref, other_ref, rows_ref, out_ref, out_chips, out_others, *sems):
    moves = Moves(*sems)
    d = lax.axis_index("dp")
    z = lax.axis_index("seq")
    core = d & 1
    heads = HEADS // PLANE
    half = out_ref.shape[1]
    meet_heads((CORE, X_WAY, Y_WAY))
    comes = []
    for j in range(2):
        comes += [2 * core + j != z] * heads + [None] * ((PLANE - 1) * heads)
    for line in (3, 1, 2, 0):
        to_d = ((d >> 1) ^ line) * 2 + (z >> 1)
        for slot, source in ((0, chip_ref), (1, other_ref)):
            for part in range(2):
                to_z = 2 * (core ^ slot) + part
                itself = jnp.logical_and(to_d == d, to_z == z)
                for number in range(heads):
                    here = source.at[
                        line, pl.ds(part * half, half), pl.ds(number * HEAD_DIM, HEAD_DIM)
                    ]
                    there = out_ref.at[z & 1, :, column_of(to_d, d, number)]
                    moves.far(
                        here,
                        there,
                        to_d,
                        to_z,
                        jnp.logical_not(itself) if line == 0 else None,
                        comes[moves.count[0]],
                        ((z & 1) * PLANE + (d ^ to_d)) * heads + number,
                    )
                    if line == 0:
                        moves.here(here, there, itself)
    for _ in gather_rows(moves, rows_ref, out_chips, out_others):
        pass
    moves.finish()


def contexts_home(context, out_rows):
    lines, rows, columns = context[0].shape
    count, width = out_rows.shape
    heads = HEADS // PLANE
    out, chips, others = kernel_call(
        contexts_home_kernel,
        [*context, out_rows],
        [shaped(2, rows // 2, width), shaped(4, count, width), shaped(4, count, width)],
        2 * PLANE * heads + GATHER_COPIES,
        4 * heads + 1,
        3,
        "contexts_home",
        60,
    )
    return out.reshape(rows, width), chips.reshape(-1, width), others.reshape(-1, width)


def gradients_out_kernel(count, in_ref, *refs):
    sums, out_ref, shards = refs[:count], refs[count], refs[count + 1 : 2 * count + 1]
    moves = Moves(*refs[2 * count + 1 :])
    d = lax.axis_index("dp")
    z = lax.axis_index("seq")
    core = d & 1
    heads = HEADS // PLANE
    half = in_ref.shape[1]
    meet_heads(range(1, PLANE))
    comes = []
    for side in range(2):
        for line in range(PLANE // 2):
            for part in range(2):
                itself = jnp.logical_and((z >> 1) == core, 2 * (core ^ side) + part == z)
                comes += [jnp.logical_not(itself) if line == 0 else None] * heads
    for mask in FAR_FIRST + (0,):
        for j in range(2):
            to_d = d ^ mask
            to_z = 2 * core + j
            line = mask >> 1
            side = (to_d & 1) ^ (z >> 1)
            for number in range(heads):
                here = in_ref.at[j, :, column_of(d, to_d, number)]
                there = out_ref.at[
                    side,
                    line,
                    pl.ds(pl.multiple_of((z & 1) * half, half), half),
                    pl.ds(number * HEAD_DIM, HEAD_DIM),
                ]
                moves.far(
                    here,
                    there,
                    to_d,
                    to_z,
                    to_z != z if mask == 0 else None,
                    comes[moves.count[0]],
                    ((side * (PLANE // 2) + line) * 2 + (z & 1)) * heads + number,
                )
                if mask == 0:
                    moves.here(here, there, to_z == z)
    for held, shard in zip(sums, shards):
        unite_columns(moves, held, shard)
    moves.finish()


def gradients_out(grad, sums):
    rows, width = grad.shape
    heads = HEADS // PLANE
    count = len(sums)
    return kernel_call(
        lambda *refs: gradients_out_kernel(count, *refs),
        [grad.reshape(2, rows // 2, width), *sums],
        [shaped(2, PLANE // 2, rows, heads * HEAD_DIM)]
        + [shaped(s.shape[0] * PLANE, s.shape[1] // PLANE) for s in sums],
        2 * PLANE * heads + count * (PLANE - 1),
        2 * heads + count,
        4,
        "gradients_out",
        50,
    )


SEQS = 4


def masked_scores(left, right, first_row, first_column, row_axis, flag, full_len):
    plain = lax.dot_general(
        left, right, (((1,), (1,)), ((), ())), preferred_element_type=F32
    ) * (1.0 / math.sqrt(HEAD_DIM))
    rows = first_row + lax.broadcasted_iota(jnp.int32, plain.shape, row_axis)
    columns = first_column + lax.broadcasted_iota(jnp.int32, plain.shape, 1 - row_axis)
    seen = jnp.logical_or(flag == 1, columns % (full_len // 2) < full_len // 4)
    return jnp.where(jnp.logical_and(columns <= rows, seen), plain, NEGATIVE)


def attend_kernel(half, block, core, flag, qkv, context, lse):
    for part in range(2):
        here = part ^ core
        for first in range(0, half, block):
            query = qkv[here][0, first : first + block, :HEAD_DIM]
            spans = [(here, part, first + block)]
            if part == 1:
                spans = [(core, 0, half)] + spans
            scores = []
            for slot, place, length in spans:
                keys = qkv[slot][0, :length, HEAD_DIM : 2 * HEAD_DIM]
                scores.append(
                    masked_scores(
                        query, keys, part * half + first, place * half, 0, flag, 2 * half
                    )
                )
            top = jnp.max(scores[0], axis=-1, keepdims=True)
            for more in scores[1:]:
                top = jnp.maximum(top, jnp.max(more, axis=-1, keepdims=True))
            expd = [jnp.exp(piece - top) for piece in scores]
            total = sum(jnp.sum(piece, axis=-1, keepdims=True) for piece in expd)
            result = 0.0
            for (slot, _, length), piece in zip(spans, expd):
                values = qkv[slot][0, :length, 2 * HEAD_DIM :]
                result = result + jnp.dot(
                    (piece / total).astype(BF16), values, preferred_element_type=F32
                )
            context[here][0, first : first + block, :] = result.astype(BF16)
            wide = jnp.broadcast_to(top + jnp.log(total), (block, HEAD_DIM))
            lse[here][0, 0, :, first : first + block] = jnp.transpose(wide)[:8]


def attend(qkv, flags, heads):
    half = qkv[0].shape[1]
    spot = lambda s, h: (s, 0, h)

    def kernel(flags_ref, *refs):
        for core in range(2):

            @pl.when(flags_ref[SEQS] == core)
            def _():
                flag = flags_ref[pl.program_id(0)]
                attend_kernel(half, half // 2, core, flag, refs[:2], refs[2:4], refs[4:])

    out = pl.pallas_call(
        kernel,
        grid=(SEQS, heads),
        in_specs=[pl.BlockSpec(memory_space=pltpu.SMEM)]
        + [pl.BlockSpec((1, half, 3 * HEAD_DIM), spot)] * 2,
        out_specs=[pl.BlockSpec((1, half, HEAD_DIM), spot)] * 2
        + [pl.BlockSpec((1, 1, 8, half), lambda s, h: (s, h, 0, 0))] * 2,
        out_shape=[jax.ShapeDtypeStruct((SEQS, half, heads * HEAD_DIM), BF16)] * 2
        + [jax.ShapeDtypeStruct((SEQS, heads, 8, half), F32)] * 2,
        cost_estimate=pl.CostEstimate(
            flops=48 * heads * half * half * HEAD_DIM,
            bytes_accessed=64 * heads * half * HEAD_DIM,
            transcendentals=16 * heads * half * half,
        ),
        name="attend",
    )(flags, *qkv)
    return out[:2], out[2:]


def attend_back_kernel(half, block, core, flag, qkv, grads, lse, out, grad_keys, grad_values):
    scale = 1.0 / math.sqrt(HEAD_DIM)
    grad_keys[...] = jnp.zeros_like(grad_keys)
    grad_values[...] = jnp.zeros_like(grad_values)
    for part in range(2):
        here = part ^ core
        for first in range(0, half, block):
            query = qkv[here][0, first : first + block, :HEAD_DIM]
            grad = grads[here, 0, first : first + block, :]
            level = lse[here][0, 0, 0:1, first : first + block]
            spans = [(here, part, first + block)]
            if part == 1:
                spans = [(core, 0, half)] + spans
            held = []
            weighted = 0.0
            for slot, place, length in spans:
                keys = qkv[slot][0, :length, HEAD_DIM : 2 * HEAD_DIM]
                values = qkv[slot][0, :length, 2 * HEAD_DIM :]
                scores = masked_scores(
                    keys, query, part * half + first, place * half, 1, flag, 2 * half
                )
                probs = jnp.exp(scores - level)
                grad_values[place, :length, :] += jnp.dot(
                    probs.astype(BF16), grad, preferred_element_type=F32
                )
                grad_probs = lax.dot_general(
                    values, grad, (((1,), (1,)), ((), ())), preferred_element_type=F32
                )
                weighted = weighted + jnp.sum(probs * grad_probs, axis=0, keepdims=True)
                held.append((probs, grad_probs, keys))
            grad_query = 0.0
            for (_, place, length), (probs, grad_probs, keys) in zip(spans, held):
                grad_scores = (probs * (grad_probs - weighted)).astype(BF16)
                grad_keys[place, :length, :] += jnp.dot(
                    grad_scores, query, preferred_element_type=F32
                )
                grad_query = grad_query + lax.dot_general(
                    grad_scores, keys, (((0,), (0,)), ((), ())), preferred_element_type=F32
                )
            out[here][0, first : first + block, :HEAD_DIM] = (grad_query * scale).astype(BF16)
    for part in range(2):
        target = out[part ^ core]
        target[0, :, HEAD_DIM : 2 * HEAD_DIM] = (grad_keys[part] * scale).astype(BF16)
        target[0, :, 2 * HEAD_DIM :] = grad_values[part].astype(BF16)


def attend_back(qkv, grads, lse, flags, heads):
    half = qkv[0].shape[1]
    spot = lambda s, h: (s, 0, h)

    def kernel(flags_ref, *refs):
        for core in range(2):

            @pl.when(flags_ref[SEQS] == core)
            def _():
                flag = flags_ref[pl.program_id(0)]
                attend_back_kernel(
                    half, half // 2, core, flag, refs[:2], refs[2], refs[3:5], refs[5:7], *refs[7:]
                )

    return pl.pallas_call(
        kernel,
        grid=(SEQS, heads),
        in_specs=[pl.BlockSpec(memory_space=pltpu.SMEM)]
        + [pl.BlockSpec((1, half, 3 * HEAD_DIM), spot)] * 2
        + [pl.BlockSpec((2, 1, half, HEAD_DIM), lambda s, h: (0, s, 0, h))]
        + [pl.BlockSpec((1, 1, 8, half), lambda s, h: (s, h, 0, 0))] * 2,
        out_specs=[pl.BlockSpec((1, half, 3 * HEAD_DIM), spot)] * 2,
        out_shape=[jax.ShapeDtypeStruct(qkv[0].shape, BF16)] * 2,
        scratch_shapes=[
            pltpu.VMEM((2, half, HEAD_DIM), F32),
            pltpu.VMEM((2, half, HEAD_DIM), F32),
        ],
        cost_estimate=pl.CostEstimate(
            flops=128 * heads * half * half * HEAD_DIM,
            bytes_accessed=128 * heads * half * HEAD_DIM,
            transcendentals=16 * heads * half * half,
        ),
        name="attend_back",
    )(flags, *qkv, grads, *lse)


def sum_everywhere(sums, late):
    dp = lax.axis_size("dp")
    seq = lax.axis_size("seq")
    count = dp * seq
    kinds, width = sums.shape
    piece = width // count
    lanes = 128
    pieces = jnp.transpose(sums.reshape(kinds, count, piece), (1, 0, 2))
    pieces = pieces.reshape(count, kinds * piece // lanes, lanes)

    def kernel(in_ref, late_ref, out_ref, got, send_sem, got_sem):
        d = lax.axis_index("dp")
        z = lax.axis_index("seq")
        me = d * seq + z
        mesh_id = pl.DeviceIdType.MESH
        barrier = pltpu.get_barrier_semaphore()
        for far in range(1, count):
            to = (me + far) % count
            pl.semaphore_signal(
                barrier, inc=1, device_id=(to // seq, to % seq), device_id_type=mesh_id
            )
        pl.semaphore_wait(barrier, count - 1)
        copies = []
        for far in range(1, count):
            to = (me + far) % count
            copy = pltpu.make_async_remote_copy(
                src_ref=in_ref.at[to],
                dst_ref=got.at[far],
                send_sem=send_sem.at[far],
                recv_sem=got_sem.at[far],
                device_id=(to // seq, to % seq),
                device_id_type=mesh_id,
            )
            copy.start()
            copies.append(copy)
        total = in_ref[me]
        for far in range(1, count):
            copies[far - 1].wait()
            total = total + got[far]
        out_ref[...] = total

    summed = pl.pallas_call(
        kernel,
        out_shape=jax.ShapeDtypeStruct(pieces.shape[1:], F32),
        in_specs=[pl.BlockSpec(memory_space=pltpu.VMEM), pl.BlockSpec(memory_space=pl.ANY)],
        out_specs=pl.BlockSpec(memory_space=pltpu.VMEM),
        scratch_shapes=[
            pltpu.VMEM(pieces.shape, F32),
            pltpu.SemaphoreType.DMA((count,)),
            pltpu.SemaphoreType.DMA((count,)),
        ],
        compiler_params=pltpu.CompilerParams(collective_id=0, has_side_effects=True),
        name="sum_everywhere",
    )(pieces, late)
    return summed.reshape(kinds, piece)


def grouped_shards(
    tokens,
    token_types,
    view_mask,
    type_table,
    ln1_gain,
    ln1_bias,
    w_qkv,
    w_out,
    ln2_gain,
    ln2_bias,
    w_up,
    w_down,
    cotangent,
):
    seq_count, local_len, width = tokens.shape
    groups = lax.axis_size("seq")
    rows = seq_count * local_len
    heads = HEADS // PLANE
    d = lax.axis_index("dp")
    z = lax.axis_index("seq")

    small = jnp.concatenate(
        [type_table, jnp.stack([ln1_gain, ln1_bias, ln2_gain, ln2_bias])], axis=0
    )
    mark = jnp.broadcast_to(view_mask[:, None, None], (seq_count, 4, 128)).reshape(8, 128)
    out_columns = along_z(jnp.transpose(w_out))
    small, marks, qkv_half = intake(small, mark, jnp.transpose(w_qkv))
    small = jnp.swapaxes(small, 0, 1).reshape(2 * TYPES, width).astype(F32)
    table = small[:TYPES]
    gain_one, bias_one, gain_two, bias_two = (small[TYPES + i] for i in range(4))
    marks = lax.dynamic_index_in_dim(marks[:, ::4, 0], z & 1, 1, keepdims=False)
    marks = lax.dynamic_index_in_dim(
        marks.reshape(SEQS, 2), (d & 1) ^ (z >> 1), 1, keepdims=False
    )
    flags = jnp.concatenate([marks, (d & 1)[None]])

    types = token_types.reshape(rows)
    onehot = (types[:, None] == jnp.arange(TYPES, dtype=jnp.int32)[None, :]).astype(F32)
    start_hidden = tokens.reshape(rows, width).astype(F32) + jnp.dot(
        onehot, table, precision=HIGHEST_PRECISION
    )
    cot = cotangent.reshape(rows, width)
    norm_one, pull_one = jax.vjp(layer_norm, start_hidden, gain_one, bias_one)
    chips, others, qkv_full, up_half, down_half = first_gather(
        norm_one.astype(BF16).reshape(tokens.shape),
        qkv_half,
        jnp.transpose(w_up),
        w_down,
    )
    up_full = along_z(up_half)
    down_full = along_z(down_half)
    normed = [part.reshape(4 * rows, width) for part in (chips, others)]
    qkv_full = qkv_full[:4].reshape(-1, width)
    qkv = [
        jnp.einsum("td,ed->te", part, qkv_full, preferred_element_type=F32)
        .astype(BF16)
        .reshape(SEQS, rows, 3 * heads * HEAD_DIM)
        for part in normed
    ]
    context, lse = attend(qkv, flags, heads)
    context_rows, out_chips, out_others = contexts_home(
        context, jnp.transpose(out_columns)
    )
    cots = plane_gather(after(cot, chips), context, context_rows)
    mid_hidden = (
        start_hidden
        + jnp.dot(context_rows[:, : width // 2], out_chips, preferred_element_type=F32)
        + jnp.dot(context_rows[:, width // 2 :], out_others, preferred_element_type=F32)
    )
    norm_two, pull_two = jax.vjp(layer_norm, mid_hidden, gain_two, bias_two)
    ffn_input = plane_gather_now(norm_two.astype(BF16), 5, cots)
    def weight_grad(left, right):
        return sum(
            jnp.einsum("ti,td->id", a, b, preferred_element_type=F32)
            for a, b in zip(left, right)
        ).astype(BF16)

    def times(parts, weight):
        return [jnp.dot(part, weight, preferred_element_type=F32).astype(BF16) for part in parts]

    ups = [
        jnp.einsum("td,id->ti", part, up_full, preferred_element_type=F32) for part in ffn_input
    ]
    acts = [gelu_tanh(up_value).astype(BF16) for up_value in ups]
    ffn_out = plane_scatter(*times(acts, down_full))
    grad_ups = []
    for cot_part, up_value in zip(cots, ups):
        grad_act = jnp.einsum("td,id->ti", cot_part, down_full, preferred_element_type=F32)
        grad_ups.append(jax.vjp(gelu_tanh, up_value)[1](grad_act)[0].astype(BF16))
    down_grad = weight_grad(acts, cots)
    up_grad = weight_grad(grad_ups, ffn_input)
    down_sum = sum_along_z(down_grad)
    up_sum = sum_along_z(up_grad)
    grad_parts = times(grad_ups, up_full)
    (grad_normed_two,) = plane_scatter_now(
        [grad_parts], [(rows, width)], [False], 6, [down_sum, up_grad, ffn_out]
    )
    grad_normed_two = grad_normed_two.astype(F32)
    grad_mid_norm, grad_gain_two, grad_bias_two = pull_two(grad_normed_two)
    grad_mid = cot.astype(F32) + grad_mid_norm
    grad_mid_low = grad_mid.astype(BF16)
    grad_context = jnp.concatenate(
        [
            jnp.einsum("te,de->td", grad_mid_low, part, preferred_element_type=F32).astype(BF16)
            for part in (out_chips, out_others)
        ],
        axis=1,
    )
    output = (mid_hidden + ffn_out).astype(BF16).reshape(tokens.shape)
    grad_by_heads, up_shard, down_shard = gradients_out(grad_context, [up_sum, down_sum])
    grad_qkv = attend_back(qkv, grad_by_heads, lse, flags, heads)
    grad_qkv = [part.reshape(SEQS * rows, 3 * heads * HEAD_DIM) for part in grad_qkv]
    grad_out_weight = [
        jnp.einsum("td,te->de", part, grad_mid_low, preferred_element_type=F32).astype(BF16)
        for part in jnp.split(context_rows, 2, axis=1)
    ]
    qkv_grad = shared_heads(weight_grad(grad_qkv, normed))
    qkv_sum = sum_along_z(qkv_grad)
    out_sum = plane_scatter(*grad_out_weight).astype(BF16)
    grad_normed_one, qkv_shard = plane_scatter_now(
        [times(grad_qkv, qkv_full)], [tokens.shape], [True], 7, [out_sum], [qkv_sum]
    )
    grad_normed_one = grad_normed_one.astype(F32)
    out_sum = sum_along_z(jnp.transpose(out_sum))
    sum_qkv = jnp.transpose(qkv_shard)
    sum_up = jnp.transpose(up_shard)
    sum_down = down_shard
    grad_start_norm, grad_gain_one, grad_bias_one = pull_one(grad_normed_one.reshape(rows, width))
    grad_start = grad_mid + grad_start_norm
    grad_table = jnp.einsum("tk,td->kd", onehot, grad_start, precision=HIGHEST_PRECISION)
    sums = jnp.concatenate(
        [
            grad_table,
            jnp.stack([grad_gain_one, grad_bias_one, grad_gain_two, grad_bias_two]),
        ],
        axis=0,
    )
    sums = sum_everywhere(sums, out_sum)
    return (
        output,
        grad_start.reshape(tokens.shape),
        sums[:TYPES],
        sums[TYPES],
        sums[TYPES + 1],
        sum_qkv.astype(F32),
        jnp.transpose(out_sum).astype(F32),
        sums[TYPES + 2],
        sums[TYPES + 3],
        sum_up.astype(F32),
        sum_down.astype(F32),
    )


def solution(mesh):
    placed = (
        P("dp", "seq", None),
        P("dp", "seq"),
        P("dp"),
        P(None, "seq"),
        P("seq"),
        P("seq"),
        P("dp", "seq"),
        P("dp", "seq"),
        P("seq"),
        P("seq"),
        P("dp", "seq"),
        P("seq", "dp"),
        P("dp", "seq", None),
    )
    fits = mesh.shape["dp"] == 8 and mesh.shape["seq"] == 4
    return jax.shard_map(
        grouped_shards if fits else plain_shards,
        mesh=mesh,
        in_specs=placed,
        out_specs=(
            P("dp", "seq", None),
            P("dp", "seq", None),
            P(None, ("dp", "seq")),
            P(("dp", "seq")),
            P(("dp", "seq")),
            P("dp", "seq"),
            P("dp", "seq"),
            P(("dp", "seq")),
            P(("dp", "seq")),
            P("dp", "seq"),
            P("seq", "dp"),
        ),
        check_vma=False,
    )
```

```python
import math

import jax
import jax.numpy as jnp
from jax import lax
from jax.experimental import pallas as pl
from jax.experimental.pallas import tpu as pltpu
from jax.sharding import PartitionSpec as P

HEADS = 16
HEAD_DIM = 128
TYPES = 4


EPS = 1e-05
NEGATIVE = -1e30
HIGHEST_PRECISION = lax.Precision.HIGHEST


def layer_norm(hidden, gain, bias):
    average = jnp.mean(hidden, axis=-1, keepdims=True)
    centered = hidden - average
    variance = jnp.mean(centered * centered, axis=-1, keepdims=True)
    return centered * lax.rsqrt(variance + EPS) * gain + bias


def gelu_tanh(value):
    inner = math.sqrt(2.0 / math.pi) * (value + 0.044715 * value * value * value)
    return 0.5 * value * (1.0 + jnp.tanh(inner))


def key_allowed(first, count, full_len, view_flag):
    query_pos = first + jnp.arange(count, dtype=jnp.int32)
    key_pos = jnp.arange(full_len, dtype=jnp.int32)
    causal = key_pos[None, :] <= query_pos[:, None]
    seen = jnp.logical_or(view_flag == 1, key_pos % (full_len // 2) < full_len // 4)
    return jnp.logical_and(causal, seen[None, :])


def scores_of(query, keys, allowed, scale):
    plain = jnp.einsum("qhd,khd->hqk", query, keys, preferred_element_type=jnp.float32) * scale
    return jnp.where(allowed[None], plain, NEGATIVE)


def to_heads(values_in):
    return lax.all_to_all(values_in, "seq", split_axis=2, concat_axis=1, tiled=True)


def to_tokens(values_in):
    return lax.all_to_all(values_in, "seq", split_axis=1, concat_axis=2, tiled=True)


def plain_shards(
    tokens,
    token_types,
    view_mask,
    type_table,
    ln1_gain,
    ln1_bias,
    w_qkv,
    w_out,
    ln2_gain,
    ln2_bias,
    w_up,
    w_down,
    cotangent,
):
    seq_count, local_len, width = tokens.shape
    groups = lax.axis_size("seq")
    full_len = local_len * groups
    row_count = seq_count * local_len
    local_heads = HEADS // groups
    scale = 1.0 / math.sqrt(HEAD_DIM)
    block = min(512, full_len)
    f32 = jnp.float32
    bf16 = jnp.bfloat16
    out_part, table, gain_one, bias_one, gain_two, bias_two = (
        lax.all_gather(w_out, "seq", axis=1, tiled=True),
        lax.all_gather(type_table, "seq", axis=1, tiled=True),
        lax.all_gather(ln1_gain, "seq", axis=0, tiled=True),
        lax.all_gather(ln1_bias, "seq", axis=0, tiled=True),
        lax.all_gather(ln2_gain, "seq", axis=0, tiled=True),
        lax.all_gather(ln2_bias, "seq", axis=0, tiled=True),
    )
    qkv_full, out_full, up_full, down_full = (
        lax.all_gather(w_qkv, "dp", axis=0, tiled=True),
        lax.all_gather(out_part, "dp", axis=0, tiled=True),
        lax.all_gather(w_up, "dp", axis=0, tiled=True),
        lax.all_gather(w_down, "dp", axis=1, tiled=True),
    )
    onehot = (
        token_types.reshape(row_count)[:, None] == jnp.arange(TYPES, dtype=jnp.int32)[None, :]
    ).astype(f32)
    start_hidden = tokens.reshape(row_count, width).astype(f32) + jnp.dot(
        onehot, table.astype(f32), precision=HIGHEST_PRECISION
    )
    norm_one, pull_one = jax.vjp(
        layer_norm, start_hidden, gain_one.astype(f32), bias_one.astype(f32)
    )
    normed_one = norm_one.astype(bf16)
    normed_rows = lax.all_gather(
        normed_one.reshape(seq_count, local_len, width), "seq", axis=1, tiled=True
    )
    by_heads = jnp.einsum("std,de->ste", normed_rows, qkv_full, preferred_element_type=f32).astype(
        bf16
    )
    by_heads = by_heads.reshape(seq_count, full_len, local_heads, 3, HEAD_DIM)
    contexts = []
    kept_lse = []
    for index in range(seq_count):
        keys = by_heads[index, :, :, 1]
        values = by_heads[index, :, :, 2]
        context_blocks = []
        lse_blocks = []
        for first in range(0, full_len, block):
            query = by_heads[index, first : first + block, :, 0]
            allowed = key_allowed(first, block, full_len, view_mask[index])
            scores = scores_of(query, keys, allowed, scale)
            top = jnp.max(scores, axis=-1, keepdims=True)
            expd = jnp.exp(scores - top)
            total = jnp.sum(expd, axis=-1, keepdims=True)
            probs_low = (expd / total).astype(bf16)
            context_blocks.append(
                jnp.einsum("hqk,khd->qhd", probs_low, values, preferred_element_type=f32).astype(
                    bf16
                )
            )
            lse_blocks.append(top + jnp.log(total))
        contexts.append(jnp.concatenate(context_blocks, axis=0))
        kept_lse.append(lse_blocks)
    context_heads = jnp.stack(contexts)
    context_rows = to_tokens(context_heads).reshape(row_count, width)
    mid_hidden = start_hidden + jnp.dot(context_rows, out_full, preferred_element_type=f32)
    norm_two, pull_two = jax.vjp(layer_norm, mid_hidden, gain_two.astype(f32), bias_two.astype(f32))
    normed_two = norm_two.astype(bf16)
    cot_rows = cotangent.reshape(row_count, width)
    ffn_input, grad_rows = (
        lax.all_gather(normed_two, "seq", axis=0, tiled=True),
        lax.all_gather(cot_rows, "seq", axis=0, tiled=True),
    )
    up_value = jnp.dot(ffn_input, up_full, preferred_element_type=f32)
    activated, gelu_pull = jax.vjp(gelu_tanh, up_value)
    activated_low = activated.astype(bf16)
    piece = activated_low
    ffn_out = lax.psum_scatter(
        jnp.dot(piece, down_full, preferred_element_type=f32).astype(jnp.bfloat16),
        "seq",
        scatter_dimension=0,
        tiled=True,
    ).astype(jnp.float32)
    output = (mid_hidden + ffn_out).astype(bf16).reshape(seq_count, local_len, width)
    grad_down = jnp.einsum("ti,td->id", activated_low, grad_rows, preferred_element_type=f32)
    grad_act = jnp.einsum("td,id->ti", grad_rows, down_full, preferred_element_type=f32)
    grad_up_value = gelu_pull(grad_act)[0].astype(bf16)
    grad_up = jnp.einsum("td,ti->di", ffn_input, grad_up_value, preferred_element_type=f32)
    piece = grad_up_value
    grad_normed_two = lax.psum_scatter(
        jnp.einsum("ti,di->td", piece, up_full, preferred_element_type=f32).astype(jnp.bfloat16),
        "seq",
        scatter_dimension=0,
        tiled=True,
    ).astype(jnp.float32)
    grad_mid_norm, grad_gain_two, grad_bias_two = pull_two(grad_normed_two)
    grad_mid = cot_rows.astype(f32) + grad_mid_norm
    grad_mid_low = grad_mid.astype(bf16)
    grad_out_weight = jnp.einsum(
        "td,te->de", context_rows, grad_mid_low, preferred_element_type=f32
    )
    grad_context = jnp.einsum(
        "te,de->td", grad_mid_low, out_full, preferred_element_type=f32
    ).astype(bf16)
    grad_context = grad_context.reshape(seq_count, local_len, HEADS, HEAD_DIM)
    grad_by_heads = to_heads(grad_context)
    grad_parts = []
    for index in range(seq_count):
        keys = by_heads[index, :, :, 1]
        values = by_heads[index, :, :, 2]
        grad_keys = jnp.zeros(keys.shape, f32)
        grad_values = jnp.zeros(values.shape, f32)
        grad_query_blocks = []
        for number, first in enumerate(range(0, full_len, block)):
            query = by_heads[index, first : first + block, :, 0]
            allowed = key_allowed(first, block, full_len, view_mask[index])
            scores = scores_of(query, keys, allowed, scale)
            probs = jnp.exp(scores - kept_lse[index][number])
            probs_low = probs.astype(bf16)
            grad_block = grad_by_heads[index, first : first + block]
            grad_values = grad_values + jnp.einsum(
                "hqk,qhd->khd", probs_low, grad_block, preferred_element_type=f32
            )
            grad_probs = jnp.einsum("qhd,khd->hqk", grad_block, values, preferred_element_type=f32)
            weighted = jnp.sum(probs * grad_probs, axis=-1, keepdims=True)
            grad_scores = (probs * (grad_probs - weighted)).astype(bf16)
            grad_query_blocks.append(
                jnp.einsum("hqk,khd->qhd", grad_scores, keys, preferred_element_type=f32) * scale
            )
            grad_keys = (
                grad_keys
                + jnp.einsum("hqk,qhd->khd", grad_scores, query, preferred_element_type=f32) * scale
            )
        grad_parts.append(
            jnp.stack([jnp.concatenate(grad_query_blocks, axis=0), grad_keys, grad_values], axis=2)
        )
    grad_projected = jnp.stack(grad_parts).astype(bf16)
    columns = qkv_full.shape[1]
    grad_flat = grad_projected.reshape(seq_count, full_len, columns)
    grad_qkv_weight = jnp.einsum("std,ste->de", normed_rows, grad_flat, preferred_element_type=f32)
    position_major = jnp.transpose(grad_flat, (1, 0, 2)).reshape(full_len * seq_count, columns)
    piece = position_major
    summed_rows = lax.psum_scatter(
        jnp.einsum("te,de->td", piece, qkv_full, preferred_element_type=f32).astype(jnp.bfloat16),
        "seq",
        scatter_dimension=0,
        tiled=True,
    ).astype(jnp.float32)
    grad_normed_one = jnp.transpose(
        summed_rows.reshape(local_len, seq_count, width), (1, 0, 2)
    ).reshape(row_count, width)
    grad_start_norm, grad_gain_one, grad_bias_one = pull_one(grad_normed_one)
    grad_start = grad_mid + grad_start_norm
    input_grad = grad_start.reshape(seq_count, local_len, width)
    grad_table = jnp.einsum("tk,td->kd", onehot, grad_start, precision=HIGHEST_PRECISION)
    (
        sum_qkv,
        sum_out,
        sum_up,
        sum_down,
        sum_table,
        sum_gain_one,
        sum_bias_one,
        sum_gain_two,
        sum_bias_two,
    ) = (
        lax.psum_scatter(
            grad_qkv_weight.astype(jnp.bfloat16), "dp", scatter_dimension=0, tiled=True
        ).astype(jnp.float32),
        lax.psum_scatter(
            grad_out_weight.astype(jnp.bfloat16), "dp", scatter_dimension=0, tiled=True
        ).astype(jnp.float32),
        lax.psum_scatter(
            grad_up.astype(jnp.bfloat16), "dp", scatter_dimension=0, tiled=True
        ).astype(jnp.float32),
        lax.psum_scatter(
            grad_down.astype(jnp.bfloat16), "dp", scatter_dimension=1, tiled=True
        ).astype(jnp.float32),
        lax.psum_scatter(
            grad_table.astype(jnp.bfloat16), "dp", scatter_dimension=1, tiled=True
        ).astype(jnp.float32),
        lax.psum_scatter(
            grad_gain_one.astype(jnp.bfloat16), "dp", scatter_dimension=0, tiled=True
        ).astype(jnp.float32),
        lax.psum_scatter(
            grad_bias_one.astype(jnp.bfloat16), "dp", scatter_dimension=0, tiled=True
        ).astype(jnp.float32),
        lax.psum_scatter(
            grad_gain_two.astype(jnp.bfloat16), "dp", scatter_dimension=0, tiled=True
        ).astype(jnp.float32),
        lax.psum_scatter(
            grad_bias_two.astype(jnp.bfloat16), "dp", scatter_dimension=0, tiled=True
        ).astype(jnp.float32),
    )
    final_out, final_table, final_gain_one, final_bias_one, final_gain_two, final_bias_two = (
        lax.psum_scatter(
            sum_out.astype(jnp.bfloat16), "seq", scatter_dimension=1, tiled=True
        ).astype(jnp.float32),
        lax.psum_scatter(
            sum_table.astype(jnp.bfloat16), "seq", scatter_dimension=1, tiled=True
        ).astype(jnp.float32),
        lax.psum_scatter(
            sum_gain_one.astype(jnp.bfloat16), "seq", scatter_dimension=0, tiled=True
        ).astype(jnp.float32),
        lax.psum_scatter(
            sum_bias_one.astype(jnp.bfloat16), "seq", scatter_dimension=0, tiled=True
        ).astype(jnp.float32),
        lax.psum_scatter(
            sum_gain_two.astype(jnp.bfloat16), "seq", scatter_dimension=0, tiled=True
        ).astype(jnp.float32),
        lax.psum_scatter(
            sum_bias_two.astype(jnp.bfloat16), "seq", scatter_dimension=0, tiled=True
        ).astype(jnp.float32),
    )
    return (
        output,
        input_grad,
        final_table,
        final_gain_one,
        final_bias_one,
        sum_qkv,
        final_out,
        final_gain_two,
        final_bias_two,
        sum_up,
        sum_down,
    )


PLANE = 8
QUAD = 4
F32 = jnp.float32
BF16 = jnp.bfloat16
MESH_ID = pl.DeviceIdType.MESH
CORE, X_WAY, Y_WAY = 1, 2, 4
FAR_FIRST = (6, 7, 2, 3, 4, 5, 1)


def swap(value, mask):
    dp = lax.axis_size("dp")
    return lax.ppermute(value, "dp", [(i, i ^ mask) for i in range(dp)])


def after(value, *earlier):
    return lax.optimization_barrier((value, earlier))[0]


def at_plane(d, z):
    return dict(device_id=(d, z), device_id_type=MESH_ID)


class Moves:
    def __init__(self, send_sem, recv_sem, local_sem=None):
        self.sems = (send_sem, recv_sem, local_sem)
        self.count = [0, 0]
        self.open = []
        self.done = []

    def far(self, source, target, d, z, sends=None, receives=None, lands=None, own=None):
        number = self.count[0] if own is None else own
        self.count[0] += own is None

        def copy(landing):
            return pltpu.make_async_remote_copy(
                src_ref=source,
                dst_ref=target,
                send_sem=self.sems[0].at[number],
                recv_sem=self.sems[1].at[landing],
                **at_plane(d, z),
            )

        out = copy(number if lands is None else lands)
        when(sends, out.start)
        move = [(out, copy(number)), sends, receives, False]
        self.open.append(move)
        return move

    def here(self, source, target, sends=None):
        number = self.count[1]
        self.count[1] += 1
        copy = pltpu.make_async_copy(source, target, self.sems[2].at[number])
        when(sends, copy.start)
        move = [copy, sends, None, False]
        self.open.append(move)
        return move

    def landed(self, move):
        copy, sends, receives, done = move
        assert not done
        move[3] = True
        if isinstance(copy, tuple):
            when(receives, copy[1].wait_recv)
        else:
            when(sends, copy.wait)

    def sent(self, move):
        when(move[1], move[0][0].wait_send)
        self.done.append(id(move))

    def finish(self):
        for move in self.open:
            if not move[3]:
                self.landed(move)
            if isinstance(move[0], tuple) and id(move) not in self.done:
                self.sent(move)


def when(condition, do):
    if condition is None:
        do()
    else:
        pl.when(condition)(do)


def meet_all(masks, lines=True, peers=False):
    d = lax.axis_index("dp")
    z = lax.axis_index("seq")
    groups = lax.axis_size("seq")
    barrier = pltpu.get_barrier_semaphore()
    count = len(masks)
    for mask in masks:
        pl.semaphore_signal(barrier, inc=1, **at_plane(d ^ mask, z))
    if lines:
        count = count + groups - 1
        for step in range(1, groups):
            pl.semaphore_signal(barrier, inc=1, **at_plane(d, (z + step) % groups))
    if peers:
        for number in range(2):
            to_d, to_z, itself = peer_of(number)
            away = jnp.logical_not(itself)

            def signal(to_d=to_d, to_z=to_z):
                pl.semaphore_signal(barrier, inc=1, **at_plane(to_d, to_z))

            when(away, signal)
            count = count + jnp.where(itself, 0, 1)
    pl.semaphore_wait(barrier, count)


def peer_of(number):
    d = lax.axis_index("dp")
    z = lax.axis_index("seq")
    core = d & 1
    to_d = (d - core) + (z >> 1)
    to_z = 2 * core + number
    return to_d, to_z, jnp.logical_and(to_d == d, to_z == z)


def exchange_along_z(moves, number, source, target, base=None):
    z = lax.axis_index("seq")
    own = None if base is None else base + number
    base = moves.count[0] - number if base is None else base
    to_d, to_z, itself = peer_of(number)
    away = jnp.logical_not(itself)
    far = moves.far(source, target(z & 1), to_d, to_z, away, away, base + (z & 1), own)
    near = moves.here(source, target(z & 1), itself)
    return far, near


def all_landed(moves, landing):
    for move in landing:
        moves.landed(move)


def intake_kernel(small_ref, mark_ref, whole_ref, marks_ref, *sems):
    moves = Moves(*sems)
    d = lax.axis_index("dp")
    z = lax.axis_index("seq")
    groups = lax.axis_size("seq")
    meet_all(range(1, PLANE))
    moves.here(small_ref, whole_ref.at[z])
    for step in range(1, groups):
        moves.far(small_ref, whole_ref.at[z], d, (z + step) % groups)
    moves.here(mark_ref, marks_ref.at[0])
    for mask in range(1, PLANE):
        moves.far(mark_ref, marks_ref.at[mask], d ^ mask, z)
    moves.finish()


def spread_columns(moves, shard, half):
    d = lax.axis_index("dp")
    z = lax.axis_index("seq")
    part, width = shard.shape[0] // PLANE, shard.shape[1]
    target = half.at[:, pl.ds(pl.multiple_of(d * width, 128), width)]

    def rows(mask):
        return shard.at[pl.ds(pl.multiple_of((d ^ mask) * part, 64), part)]

    return [moves.here(rows(0), target)] + [
        moves.far(rows(mask), target, d ^ mask, z) for mask in FAR_FIRST
    ]


def kernel_call(
    kernel, inputs, outputs, far, here, number, name, traffic, spaces=None, scratch=(), late=()
):
    count = len(inputs)

    def body(*refs):
        kernel(*refs[:count], *refs[count + len(late) :])

    return pl.pallas_call(
        body,
        out_shape=outputs,
        in_specs=[pl.BlockSpec(memory_space=space) for space in spaces or [pltpu.VMEM] * count]
        + [pl.BlockSpec(memory_space=pl.ANY)] * len(late),
        out_specs=[pl.BlockSpec(memory_space=pl.ANY)] * len(outputs),
        scratch_shapes=[
            *scratch,
            pltpu.SemaphoreType.DMA((far,)),
            pltpu.SemaphoreType.DMA((far,)),
            pltpu.SemaphoreType.DMA((here,)),
        ],
        compiler_params=pltpu.CompilerParams(
            collective_id=number, has_side_effects=True, vmem_limit_bytes=56 * 1024 * 1024
        ),
        cost_estimate=pl.CostEstimate(
            flops=0, bytes_accessed=traffic * 3 * 1024 * 1024, transcendentals=0
        ),
        name=name,
    )(*inputs, *late)


def shaped(*shape):
    return jax.ShapeDtypeStruct(shape, BF16)


def intake(small, mark):
    groups = lax.axis_size("seq")
    return kernel_call(
        intake_kernel,
        [small, mark],
        [
            shaped(groups, *small.shape),
            jax.ShapeDtypeStruct((PLANE,) + mark.shape, mark.dtype),
        ],
        groups - 1 + PLANE - 1,
        2,
        1,
        "intake",
        10,
    )


def gather_rows(moves, rows_ref, chips_ref, others_ref, ready=None, pieces=2):
    d = lax.axis_index("dp")
    z = lax.axis_index("seq")
    size = chips_ref.shape[1] // pieces
    parts = [pl.ds(number * size, size) for number in range(pieces)]
    order = [i + j for i in range(pieces // 2) for j in (0, pieces // 2)]

    def far(source, target, mask):
        return moves.far(source, target, d ^ mask, z)

    if ready is None:
        moves.here(rows_ref, chips_ref.at[0])
    over_x = {}
    over_y = {}
    for number in order:
        part = parts[number]
        if ready is None:
            source = rows_ref.at[part]
        else:
            ready(number)
            source = chips_ref.at[0, part]
        over_x[number] = far(source, chips_ref.at[1, part], X_WAY)
        over_y[number] = far(source, chips_ref.at[2, part], Y_WAY)
        far(source, others_ref.at[0, part], CORE)

    def pass_on(chip, number):
        part = parts[number]
        far(chips_ref.at[chip, part], others_ref.at[chip, part], CORE)

    corner = {}
    for number in order:
        yield
        part = parts[number]
        first = number < pieces // 2
        via, chip, mask = (over_y, 2, X_WAY) if first else (over_x, 1, Y_WAY)
        moves.landed(via[number])
        corner[number] = far(chips_ref.at[chip, part], chips_ref.at[3, part], mask)
        pass_on(chip, number)
        moves.landed((over_x if first else over_y)[number])
        pass_on(3 - chip, number)
    yield
    for number in order:
        moves.landed(corner[number])
        pass_on(3, number)


GATHER_COPIES = 14
FIRST_PIECES = 4


def gather_along_z(moves, shard_ref, place, target):
    d = lax.axis_index("dp")
    z = lax.axis_index("seq")
    own = moves.here(shard_ref, target.at[place(z)])
    arrivals = []
    for step in (2, -2, 1, -1):
        to, source = z + step, z - step
        inside = jnp.logical_and(to >= 0, to < 4)
        comes = jnp.logical_and(source >= 0, source < 4)
        arrivals.append(
            moves.far(shard_ref, target.at[place(z)], d, jnp.clip(to, 0, 3), inside, comes)
        )
    yield
    for arrival in arrivals:
        moves.landed(arrival)
    for end, via, to in ((0, 2, 3), (3, 1, 0)):
        arrivals.append(
            moves.far(target.at[place(end)], target.at[place(end)], d, to, z == via, z == to)
        )
    yield
    for arrival in arrivals[4:] + [own]:
        moves.landed(arrival)


Z_COPIES = 6


def first_kernel(rows_ref, qkv_ref, up_ref, down_ref, *refs):
    chips, others, heads, up_half, down_half, qkv_half = refs[:6]
    moves = Moves(*refs[6:])
    d = lax.axis_index("dp")
    core = d & 1
    half = rows_ref.shape[1]
    meet_all(range(1, PLANE), peers=True)
    size = 2 * half // FIRST_PIECES
    landing = {}
    for piece in range(FIRST_PIECES // 2):
        for number in range(2):
            landing[number * (FIRST_PIECES // 2) + piece] = exchange_along_z(
                moves,
                number,
                rows_ref.at[number, pl.ds(piece * size, size)],
                lambda at: chips.at[
                    0, pl.ds(pl.multiple_of(at * half + piece * size, size), size)
                ],
            )
    spread = spread_columns(moves, qkv_ref, qkv_half)
    spread_columns(moves, up_ref, up_half)
    spread_columns(moves, down_ref, down_half)
    all_landed(moves, spread)

    def place(at):
        own = (at >> 1) == core
        return jnp.where(own, (at & 1) * 2 + core, 4 + (at & 1))

    qkv = gather_along_z(moves, qkv_half, place, heads)
    next(qkv)
    rows = gather_rows(
        moves,
        None,
        chips,
        others,
        lambda number: all_landed(moves, landing[number]),
        FIRST_PIECES,
    )
    for _ in range(FIRST_PIECES):
        next(rows)
    next(qkv)
    next(rows)
    next(qkv, None)
    z = lax.axis_index("seq")
    for number in range(2):
        moves.far(heads.at[4 + number], heads.at[number * 2 + core], d ^ CORE, z)
    next(rows, None)
    moves.finish()


def first_gather(rows, qkv_shard, up_shard, down_shard, late):
    seqs, half, width = rows.shape
    part = qkv_shard.shape[0] // PLANE
    return kernel_call(
        first_kernel,
        [rows, qkv_shard, up_shard, down_shard],
        [
            shaped(4, seqs * half, width),
            shaped(4, seqs * half, width),
            shaped(6, part, width),
            shaped(up_shard.shape[0] // PLANE, width),
            shaped(down_shard.shape[0] // PLANE, width),
            shaped(part, width),
        ],
        7 * FIRST_PIECES + Z_COPIES + FIRST_PIECES + 2 + 3 * (PLANE - 1),
        4 + FIRST_PIECES,
        2,
        "first_gather",
        110,
        late=late,
    )[:5]


def gather_kernel(rows_ref, held_ref, chips, others, held_others, *sems):
    moves = Moves(*sems)
    d = lax.axis_index("dp")
    z = lax.axis_index("seq")
    meet_all((CORE, X_WAY, Y_WAY), lines=False)
    steps = gather_rows(moves, rows_ref, chips, others)
    next(steps)
    moves.far(held_ref, held_others, d ^ CORE, z)
    for _ in steps:
        pass
    moves.finish()


def plane_gather_now(rows, held, number, late):
    count, width = rows.shape
    chips, others, held_others = kernel_call(
        gather_kernel,
        [rows, held],
        [shaped(4, count, width), shaped(4, count, width), shaped(*held.shape)],
        GATHER_COPIES + 1,
        1,
        number,
        "plane_gather",
        76,
        [pltpu.VMEM, pl.ANY],
        late=late,
    )
    return [part.reshape(4 * count, width) for part in (chips, others)], held_others


def add_rows(target, start, sources, count, step=64):
    @pl.loop(0, count // step)
    def _(i):
        total = None
        for ref, offset in sources:
            piece = ref[pl.ds(pl.multiple_of(offset + i * step, step), step), :].astype(F32)
            total = piece if total is None else total + piece
        target[pl.ds(pl.multiple_of(start + i * step, step), step), :] = total.astype(target.dtype)


CHIP_ORDER = (3, 1, 2, 0)


def scatter_rows(moves, fill, last, own, got, far, near, done):
    d = lax.axis_index("dp")
    z = lax.axis_index("seq")
    half = own.shape[1] // 2
    first, second = pl.ds(0, half), pl.ds(half, half)

    def send_to(source, target, mask):
        return moves.far(source, target, d ^ mask, z)

    ready = fill(send_to)
    yield
    ready(0)
    add_rows(own.at[0], 0, [(own.at[0], 0), (got.at[0], 0)], half)
    to_x = send_to(own.at[0, first], far.at[0], X_WAY)
    add_rows(own.at[0], half, [(own.at[0], half), (got.at[0], half)], half)
    to_y = send_to(own.at[0, second], far.at[1], Y_WAY)
    ready(1)
    add_rows(own.at[1], 0, [(own.at[1], 0), (got.at[1], 0)], half)
    x_first = send_to(own.at[1, first], near.at[0, first], X_WAY)
    ready(2)
    yield
    moves.landed(to_x)
    add_rows(own.at[2], 0, [(own.at[2], 0), (got.at[2], 0), (far.at[0], 0)], half)
    y_first = send_to(own.at[2, first], near.at[1, first], Y_WAY)
    add_rows(own.at[2], half, [(own.at[2], half), (got.at[2], half)], half)
    y_second = send_to(own.at[2, second], near.at[1, second], Y_WAY)
    moves.landed(to_y)
    add_rows(own.at[1], half, [(own.at[1], half), (got.at[1], half), (far.at[1], 0)], half)
    x_second = send_to(own.at[1, second], near.at[0, second], X_WAY)
    ready(3)
    yield
    for number, arrivals in ((0, (x_first, y_first)), (1, (x_second, y_second))):
        all_landed(moves, arrivals)
        start = number * half
        add_rows(
            done,
            start,
            [(own.at[3], start), (got.at[3], start), (near.at[0], start), (near.at[1], start)],
            half,
        )
        last(number)
    for move in (to_x, to_y, x_first, x_second, y_first, y_second):
        moves.sent(move)


SCATTER_COPIES = 10


def sum_rows(target, sources, step=64):
    @pl.loop(0, target.shape[0] // step)
    def _(i):
        at = pl.ds(pl.multiple_of(i * step, step), step)
        total = sources[0][at, :].astype(F32)
        for ref in sources[1:]:
            total = total + ref[at, :].astype(F32)
        target[at, :] = total.astype(target.dtype)


def sum_along_line(moves, piece, got, target):
    d = lax.axis_index("dp")
    z = lax.axis_index("seq")
    groups = lax.axis_size("seq")
    arrivals = []
    for step in range(1, groups):
        to = (z + step) % groups
        arrivals.append(moves.far(piece(to), got.at[step - 1], d, to))
    yield
    all_landed(moves, arrivals)
    sum_rows(target, [piece(z)] + [got.at[step] for step in range(groups - 1)])


class Slots:
    def __init__(self, places, sems):
        self.places = places
        self.sems = sems
        self.copies = {}

    def load(self, slot, source):
        self.copies[slot] = pltpu.make_async_copy(source, self.places.at[slot], self.sems.at[slot])
        self.copies[slot].start()

    def store(self, slot, target):
        self.copies[slot] = pltpu.make_async_copy(self.places.at[slot], target, self.sems.at[slot])
        self.copies[slot].start()

    def wait(self, slot):
        if slot in self.copies:
            self.copies.pop(slot).wait()
        return self.places.at[slot]


def scatter_products(
    moves, sources, held, rows_in, weights_in, stage, side, last, follow=None, also=None
):
    count = held[0].shape[1]
    blocks = [(1, c) for c in CHIP_ORDER] + [(0, c) for c in CHIP_ORDER]

    def fill(send_to):
        def load(number):
            which, c = blocks[number]
            rows_in.load(number % 2, sources[which].at[pl.ds(c * count, count)])

        load(0)
        matrix = weights_in.wait(side)
        from_core = []
        for number, (which, c) in enumerate(blocks):
            if number + 1 < len(blocks):
                load(number + 1)
            if which == 1 and number >= 2:
                moves.sent(from_core[number - 2])
            place = stage.at[number % 2] if which == 1 else held[0].at[number - 4]
            block = rows_in.wait(number % 2)

            @pl.loop(0, count // 256)
            def _(i):
                at = pl.ds(pl.multiple_of(i * 256, 256), 256)
                place[at, :] = jnp.dot(
                    block[at, :], matrix[...], preferred_element_type=F32
                ).astype(BF16)
                if also is not None:
                    also(which, c, block, i)

            if which == 1:
                from_core.append(send_to(place, held[1].at[number], CORE))
        if follow is not None:
            follow()
        moves.sent(from_core[2])
        moves.sent(from_core[3])
        return lambda i: moves.landed(from_core[i])

    return scatter_rows(moves, fill, last, *held)


def last_kernel(
    chips_ref,
    others_ref,
    weights_ref,
    out_ref,
    held_ref,
    grad_ref,
    out_sum_ref,
    shard_ref,
    own,
    got,
    far,
    near,
    done,
    stage,
    rows_held,
    weights_held,
    out_got,
    out_sum,
    rows_sem,
    weights_sem,
    *sems,
):
    moves = Moves(*sems)
    rows_in = Slots(rows_held, rows_sem)
    weights_in = Slots(weights_held, weights_sem)
    columns = out_sum.shape[1]
    half, width = own.shape[2] // 2, own.shape[3]
    for side in range(2):
        weights_in.load(side, weights_ref.at[:, pl.ds(side * width, width)])
    meet_all(range(1, PLANE), peers=True)
    out = sum_along_line(
        moves,
        lambda at: out_ref.at[:, pl.ds(pl.multiple_of(at * columns, 128), columns)],
        out_got,
        out_sum,
    )
    next(out)

    def scatter(side):
        base = []

        def last(number):
            if number == 0:
                base.append(moves.count[0])
                moves.count[0] += 2
            exchange_along_z(
                moves,
                number,
                done.at[side, pl.ds(number * half, half)],
                lambda at: grad_ref.at[at, :, pl.ds(side * width, width)],
                base[0],
            )

        held = [ref.at[side] for ref in (own, got, far, near, done)]
        return scatter_products(
            moves, (chips_ref, others_ref), held, rows_in, weights_in, stage, side, last
        )

    low, high = scatter(0), scatter(1)
    next(low)
    next(low)
    next(high)
    next(low)
    next(high)
    next(out, None)
    moves.here(out_sum, out_sum_ref)
    next(low, None)
    next(high)
    unite_columns(moves, held_ref, shard_ref)
    next(high, None)
    moves.finish()


def last_scatter(parts, weights, out_grad, held, shape):
    total, units = parts[0].shape
    width = weights.shape[1]
    count, half = total // 4, width // 2
    groups = lax.axis_size("seq")
    rows, columns = out_grad.shape[0], width // groups
    sizes = ((4, count, half), (4, count, half), (2, count // 2, half), (2, count, half))
    return kernel_call(
        last_kernel,
        [*parts, weights, out_grad, held],
        [
            shaped(*shape),
            shaped(rows, columns),
            shaped(held.shape[0] * PLANE, width // PLANE),
        ],
        2 * SCATTER_COPIES + 4 + groups - 1 + PLANE - 1,
        6,
        7,
        "last_scatter",
        100,
        [pl.ANY, pl.ANY, pl.ANY, pltpu.VMEM, pltpu.VMEM],
        [pltpu.VMEM((2,) + size, BF16) for size in sizes + ((count, half),)]
        + [
            pltpu.VMEM((2, count, half), BF16),
            pltpu.VMEM((2, count, units), BF16),
            pltpu.VMEM((2, units, half), BF16),
            pltpu.VMEM((groups - 1, rows, columns), BF16),
            pltpu.VMEM((rows, columns), BF16),
            pltpu.SemaphoreType.DMA((2,)),
            pltpu.SemaphoreType.DMA((2,)),
        ],
    )


def feed_kernel(
    grad_chips,
    grad_others,
    act_chips,
    act_others,
    up_ref,
    down_ref,
    rows_chips,
    rows_others,
    cot_chips,
    cot_others,
    norm_ref,
    out_ref,
    up_parts_ref,
    down_grad_ref,
    left,
    rows_held,
    weights_held,
    own,
    got,
    far,
    near,
    done,
    stage,
    stream_held,
    result_held,
    rows_sem,
    weights_sem,
    stream_sem,
    result_sem,
    free_sem,
    send_sem,
    recv_sem,
    local_sem,
):
    moves = Moves(send_sem, recv_sem, local_sem)
    d = lax.axis_index("dp")
    z = lax.axis_index("seq")
    rows_in = Slots(rows_held, rows_sem)
    weights_in = Slots(weights_held, weights_sem)
    stream = Slots(stream_held, stream_sem)
    results = Slots(result_held, result_sem)
    count, width = own.shape[2], own.shape[3]
    columns = stream_held.shape[2]
    def load_weights(weights, side):
        weights_in.load(side, weights.at[:, pl.ds(side * width, width)])

    def scatter(sources, side, target, follow, keep):
        held = [ref.at[side] for ref in (own, got, far, near, done)]

        def transposed(which, c, block, i):
            tokens = pl.ds(pl.multiple_of(c * count + i * 256, 256), 256)
            for unit in range(0, block.shape[1], 256):
                left[which, unit : unit + 256, tokens] = jnp.transpose(
                    block[pl.ds(pl.multiple_of(i * 256, 256), 256), unit : unit + 256]
                )

        def last(number):
            if number == 1:
                moves.here(held[4], target.at[:, pl.ds(side * width, width)])

        return scatter_products(
            moves,
            sources,
            held,
            rows_in,
            weights_in,
            stage,
            side,
            last,
            follow,
            transposed if keep else None,
        )

    def end(work, side):
        next(work, None)
        all_landed(moves, moves.open[-1:])
        for mask in (CORE, X_WAY, Y_WAY):
            pl.semaphore_signal(free_sem.at[side], inc=1, **at_plane(d ^ mask, z))

    def weight_grad(rights, place):
        chunks = rights[0].shape[1] // columns
        gone = {}

        def load(chunk):
            for side in range(2):
                stream.load(
                    2 * (chunk % 2) + side, rights[side].at[:, pl.ds(chunk * columns, columns)]
                )

        load(0)
        for chunk in range(chunks):
            if chunk + 1 < chunks:
                load(chunk + 1)
            first, second = (stream.wait(2 * (chunk % 2) + side) for side in range(2))
            result = results.wait(chunk % 2)
            for move in gone.pop(chunk % 2, ()):
                moves.sent(move)

            @pl.loop(0, result.shape[0] // 256)
            def _(i):
                at = pl.ds(pl.multiple_of(i * 256, 256), 256)
                total = jnp.dot(left[0, at, :], first[...], preferred_element_type=F32)
                total += jnp.dot(left[1, at, :], second[...], preferred_element_type=F32)
                result[at, :] = total.astype(BF16)

            gone[chunk % 2] = place(result, chunk)
            yield
        for copies in gone.values():
            for move in copies:
                moves.sent(move)

    groups = lax.axis_size("seq")
    part = up_parts_ref.shape[1]

    def to_line(result, chunk):
        target = up_parts_ref.at[:, :, pl.ds(chunk * columns, columns)]
        copies = []
        for step in range(1, groups):
            to = (z + step) % groups
            piece = result.at[pl.ds(pl.multiple_of(to * part, 256), part)]
            copies.append(moves.far(piece, target.at[step], d, to))
        piece = result.at[pl.ds(pl.multiple_of(z * part, 256), part)]
        results.copies[chunk % 2] = pltpu.make_async_copy(
            piece, target.at[0], results.sems.at[chunk % 2]
        )
        results.copies[chunk % 2].start()
        return copies

    def to_memory(result, chunk):
        results.store(chunk % 2, down_grad_ref.at[:, pl.ds(chunk * columns, columns)])
        return ()

    def steps(work, number):
        for _ in range(number):
            next(work, None)

    nothing = lambda: None
    load_weights(up_ref, 0)
    load_weights(up_ref, 1)
    meet_all((CORE, X_WAY, Y_WAY))
    grads = (grad_chips, grad_others)
    acts = (act_chips, act_others)
    norm_low = scatter(grads, 0, norm_ref, lambda: load_weights(down_ref, 0), True)
    norm_high = scatter(grads, 1, norm_ref, lambda: load_weights(down_ref, 1), False)
    out_low = scatter(acts, 0, out_ref, nothing, False)
    out_high = scatter(acts, 1, out_ref, nothing, True)
    up_work = weight_grad((rows_chips, rows_others), to_line)
    down_work = weight_grad((cot_chips, cot_others), to_memory)
    next(norm_low)
    next(norm_low)
    steps(up_work, 3)
    next(norm_low)
    next(norm_high)
    next(norm_high)
    steps(up_work, 3)
    end(norm_low, 0)
    next(norm_high)
    pl.semaphore_wait(free_sem.at[0], 3)
    next(out_low)
    next(out_low)
    steps(up_work, 3)
    end(norm_high, 1)
    next(out_low)
    pl.semaphore_wait(free_sem.at[1], 3)
    next(out_high)
    next(out_high)
    steps(down_work, 4)
    next(out_low, None)
    next(out_high)
    steps(down_work, 5)
    next(out_high, None)
    for slot in range(2):
        results.wait(slot)
    moves.finish()


def feed_back(grads, acts, up_full, down_full, rows, cots):
    total, units = grads[0].shape
    width = up_full.shape[1]
    count = total // 4
    half = width // 2
    columns = 256
    copies = 4 * SCATTER_COPIES + 3 * width // columns
    groups = lax.axis_size("seq")
    ins = [*grads, *acts, up_full, down_full, *rows, *cots]
    return pl.pallas_call(
        feed_kernel,
        out_shape=[shaped(count, width)] * 2
        + [shaped(groups, units // groups, width), shaped(units, width)],
        in_specs=[pl.BlockSpec(memory_space=pl.ANY)] * len(ins),
        out_specs=[pl.BlockSpec(memory_space=pl.ANY)] * 4,
        scratch_shapes=[
            pltpu.VMEM((2, units, total), BF16),
            pltpu.VMEM((2, count, units), BF16),
            pltpu.VMEM((2, units, half), BF16),
            pltpu.VMEM((2, 4, count, half), BF16),
            pltpu.VMEM((2, 4, count, half), BF16),
            pltpu.VMEM((2, 2, count // 2, half), BF16),
            pltpu.VMEM((2, 2, count, half), BF16),
            pltpu.VMEM((2, count, half), BF16),
            pltpu.VMEM((2, count, half), BF16),
            pltpu.VMEM((4, total, columns), BF16),
            pltpu.VMEM((2, units, columns), BF16),
            pltpu.SemaphoreType.DMA((2,)),
            pltpu.SemaphoreType.DMA((2,)),
            pltpu.SemaphoreType.DMA((4,)),
            pltpu.SemaphoreType.DMA((2,)),
            pltpu.SemaphoreType.REGULAR((2,)),
            pltpu.SemaphoreType.DMA((copies,)),
            pltpu.SemaphoreType.DMA((copies,)),
            pltpu.SemaphoreType.DMA((4,)),
        ],
        compiler_params=pltpu.CompilerParams(
            collective_id=6, has_side_effects=True, vmem_limit_bytes=62 * 1024 * 1024
        ),
        cost_estimate=pl.CostEstimate(
            flops=8 * 2 * total * units * width, bytes_accessed=160 * 3 * 1024 * 1024, transcendentals=0
        ),
        name="feed_back",
    )(*ins)


def unite_columns(moves, half_ref, shard_ref):
    d = lax.axis_index("dp")
    z = lax.axis_index("seq")
    part, width = half_ref.shape[0], shard_ref.shape[1]
    target = shard_ref.at[pl.ds(pl.multiple_of(d * part, 64), part)]

    def columns(mask):
        return half_ref.at[:, pl.ds(pl.multiple_of((d ^ mask) * width, 128), width)]

    moves.here(columns(0), target)
    for mask in FAR_FIRST:
        moves.far(columns(mask), target, d ^ mask, z)


def along_z(value):
    return lax.all_gather(value, "seq", axis=0, tiled=True)


def sum_along_z(grad):
    return lax.psum_scatter(grad, "seq", scatter_dimension=0, tiled=True)


def shared_heads(grad):
    heads = HEADS // PLANE
    held = grad.reshape(heads, 2, -1, grad.shape[-1])
    second = lax.axis_index("dp") % 2 == 1
    keep = jnp.where(second, held[:, 1], held[:, 0])
    other = swap(jnp.where(second, held[:, 0], held[:, 1]), CORE)
    whole = jnp.concatenate([jnp.where(second, other, keep), jnp.where(second, keep, other)])
    return whole.reshape(-1, grad.shape[-1])


def chips_gather(rows, second):
    half = rows.shape[0] // 2
    x_rows = swap(rows, X_WAY)
    y_rows = swap(rows, Y_WAY)
    corner_first = swap(after(y_rows[:half], second), X_WAY)
    corner_second = swap(after(x_rows[half:], second), Y_WAY)
    return jnp.concatenate([rows, x_rows, y_rows, corner_first, corner_second])


class Scatter:
    def __init__(self, chips, others):
        self.chips = chips
        self.got = swap(others, CORE)
        self.count = chips.shape[0] // 4

    def both(self, start, size):
        return sum(part[start : start + size].astype(F32) for part in (self.chips, self.got))

    def corners(self, tied):
        half = self.count // 2
        self.got, tied = lax.optimization_barrier((self.got, tied))
        at = 3 * self.count
        self.far = (
            swap(self.both(at, half).astype(BF16), X_WAY),
            swap(self.both(at + half, half).astype(BF16), Y_WAY),
        )
        self.near = (
            swap(self.both(self.count, half).astype(BF16), X_WAY),
            swap(self.both(2 * self.count + half, half).astype(BF16), Y_WAY),
        )
        return tied

    def sides(self, tied):
        half = self.count // 2
        self.far, tied = lax.optimization_barrier((self.far, tied))
        x_second = self.both(self.count + half, half) + self.far[1].astype(F32)
        y_first = self.both(2 * self.count, half) + self.far[0].astype(F32)
        self.last = swap(x_second.astype(BF16), X_WAY), swap(y_first.astype(BF16), Y_WAY)
        return tied

    def result(self):
        half = self.count // 2
        first = self.both(0, half) + self.near[0].astype(F32) + self.last[1].astype(F32)
        second = self.both(half, half) + self.last[0].astype(F32) + self.near[1].astype(F32)
        return jnp.concatenate([first, second])


def place_of(mask):
    return (mask & 1) * (PLANE // 2) + (mask >> 1)


def column_of(holder, member, number):
    head = (2 * (member & 1) + number) * (PLANE // 2) + (member >> 1)
    place = place_of(holder ^ (head >> 1))
    return pl.ds(pl.multiple_of((2 * place + (head & 1)) * HEAD_DIM, HEAD_DIM), HEAD_DIM)


def meet_heads(masks):
    d = lax.axis_index("dp")
    z = lax.axis_index("seq")
    core = d & 1
    groups = lax.axis_size("seq")
    inside = (z >> 1) == core
    barrier = pltpu.get_barrier_semaphore()

    def greet(to_d, to_z, maybe_itself):
        def signal():
            pl.semaphore_signal(barrier, inc=1, **at_plane(to_d, to_z))

        when(jnp.logical_or(to_d != d, to_z != z) if maybe_itself else None, signal)

    for line in range(PLANE // 2):
        for to_z in range(groups):
            greet(((d >> 1) ^ line) * 2 + (z >> 1), to_z, line == 0)
    for mask in range(PLANE):
        for j in range(2):
            greet(d ^ mask, 2 * core + j, mask == 0)
    for mask in masks:
        greet(d ^ mask, z, False)
    pl.semaphore_wait(barrier, 4 * PLANE + len(masks) - jnp.where(inside, 2, 0))


def contexts_home_kernel(chip_ref, other_ref, rows_ref, out_ref, out_chips, out_others, *sems):
    moves = Moves(*sems)
    d = lax.axis_index("dp")
    z = lax.axis_index("seq")
    core = d & 1
    heads = HEADS // PLANE
    half = out_ref.shape[1]
    meet_heads((CORE, X_WAY, Y_WAY))
    comes = []
    for j in range(2):
        comes += [2 * core + j != z] * heads + [None] * ((PLANE - 1) * heads)
    for line in (3, 1, 2, 0):
        to_d = ((d >> 1) ^ line) * 2 + (z >> 1)
        for slot, source in ((0, chip_ref), (1, other_ref)):
            for part in range(2):
                to_z = 2 * (core ^ slot) + part
                itself = jnp.logical_and(to_d == d, to_z == z)
                for number in range(heads):
                    here = source.at[
                        line, pl.ds(part * half, half), pl.ds(number * HEAD_DIM, HEAD_DIM)
                    ]
                    there = out_ref.at[z & 1, :, column_of(to_d, d, number)]
                    moves.far(
                        here,
                        there,
                        to_d,
                        to_z,
                        jnp.logical_not(itself) if line == 0 else None,
                        comes[moves.count[0]],
                        ((z & 1) * PLANE + (d ^ to_d)) * heads + number,
                    )
                    if line == 0:
                        moves.here(here, there, itself)
    for _ in gather_rows(moves, rows_ref, out_chips, out_others):
        pass
    moves.finish()


def contexts_home(context, out_rows):
    lines, rows, columns = context[0].shape
    count, width = out_rows.shape
    heads = HEADS // PLANE
    out, chips, others = kernel_call(
        contexts_home_kernel,
        [*context, out_rows],
        [
            shaped(2, rows // 2, width),
            shaped(4, count, width),
            shaped(4, count, width),
        ],
        2 * PLANE * heads + GATHER_COPIES,
        4 * heads + 1,
        3,
        "contexts_home",
        60,
    )
    chips, others = (part.reshape(-1, width) for part in (chips, others))
    return out.reshape(rows, width), chips, others


def gradients_out_kernel(count, in_ref, *refs):
    sums, out_ref, shards = refs[:count], refs[count], refs[count + 1 : 2 * count + 1]
    moves = Moves(*refs[2 * count + 1 :])
    d = lax.axis_index("dp")
    z = lax.axis_index("seq")
    core = d & 1
    heads = HEADS // PLANE
    half = in_ref.shape[1]
    meet_heads(range(1, PLANE))
    comes = []
    for side in range(2):
        for line in range(PLANE // 2):
            for part in range(2):
                itself = jnp.logical_and((z >> 1) == core, 2 * (core ^ side) + part == z)
                comes += [jnp.logical_not(itself) if line == 0 else None] * heads
    for mask in FAR_FIRST + (0,):
        for j in range(2):
            to_d = d ^ mask
            to_z = 2 * core + j
            line = mask >> 1
            side = (to_d & 1) ^ (z >> 1)
            for number in range(heads):
                here = in_ref.at[j, :, column_of(d, to_d, number)]
                there = out_ref.at[
                    side,
                    line,
                    pl.ds(pl.multiple_of((z & 1) * half, half), half),
                    pl.ds(number * HEAD_DIM, HEAD_DIM),
                ]
                moves.far(
                    here,
                    there,
                    to_d,
                    to_z,
                    to_z != z if mask == 0 else None,
                    comes[moves.count[0]],
                    ((side * (PLANE // 2) + line) * 2 + (z & 1)) * heads + number,
                )
                if mask == 0:
                    moves.here(here, there, to_z == z)
    for held, shard in zip(sums, shards):
        unite_columns(moves, held, shard)
    moves.finish()


def gradients_out(grad, sums, late):
    rows, width = grad.shape
    heads = HEADS // PLANE
    count = len(sums)
    return kernel_call(
        lambda *refs: gradients_out_kernel(count, *refs),
        [grad.reshape(2, rows // 2, width), *sums],
        [shaped(2, PLANE // 2, rows, heads * HEAD_DIM)]
        + [shaped(s.shape[0] * PLANE, s.shape[1] // PLANE) for s in sums],
        2 * PLANE * heads + count * (PLANE - 1),
        2 * heads + count,
        4,
        "gradients_out",
        50,
        late=late,
    )


SEQS = 4


def masked_scores(left, right, first_row, first_column, row_axis, flag, full_len):
    plain = lax.dot_general(
        left, right, (((1,), (1,)), ((), ())), preferred_element_type=F32
    ) * (1.0 / math.sqrt(HEAD_DIM))
    rows = first_row + lax.broadcasted_iota(jnp.int32, plain.shape, row_axis)
    columns = first_column + lax.broadcasted_iota(jnp.int32, plain.shape, 1 - row_axis)
    seen = jnp.logical_or(flag == 1, columns % (full_len // 2) < full_len // 4)
    return jnp.where(jnp.logical_and(columns <= rows, seen), plain, NEGATIVE)


def attend_kernel(half, block, core, flag, qkv, context, lse):
    for part in range(2):
        here = part ^ core
        for first in range(0, half, block):
            query = qkv[here][0, first : first + block, :HEAD_DIM]
            spans = [(here, part, first + block)]
            if part == 1:
                spans = [(core, 0, half)] + spans
            scores = []
            for slot, place, length in spans:
                keys = qkv[slot][0, :length, HEAD_DIM : 2 * HEAD_DIM]
                scores.append(
                    masked_scores(
                        query, keys, part * half + first, place * half, 0, flag, 2 * half
                    )
                )
            top = jnp.max(scores[0], axis=-1, keepdims=True)
            for more in scores[1:]:
                top = jnp.maximum(top, jnp.max(more, axis=-1, keepdims=True))
            expd = [jnp.exp(piece - top) for piece in scores]
            total = sum(jnp.sum(piece, axis=-1, keepdims=True) for piece in expd)
            result = 0.0
            for (slot, _, length), piece in zip(spans, expd):
                values = qkv[slot][0, :length, 2 * HEAD_DIM :]
                result = result + jnp.dot(
                    (piece / total).astype(BF16), values, preferred_element_type=F32
                )
            context[here][0, first : first + block, :] = result.astype(BF16)
            wide = jnp.broadcast_to(top + jnp.log(total), (block, HEAD_DIM))
            lse[here][0, 0, :, first : first + block] = jnp.transpose(wide)[:8]


def attend(qkv, flags, heads):
    half = qkv[0].shape[1]
    spot = lambda s, h: (s, 0, h)

    def kernel(flags_ref, *refs):
        for core in range(2):

            @pl.when(flags_ref[SEQS] == core)
            def _():
                flag = flags_ref[pl.program_id(0)]
                attend_kernel(half, half // 2, core, flag, refs[:2], refs[2:4], refs[4:])

    out = pl.pallas_call(
        kernel,
        grid=(SEQS, heads),
        in_specs=[pl.BlockSpec(memory_space=pltpu.SMEM)]
        + [pl.BlockSpec((1, half, 3 * HEAD_DIM), spot)] * 2,
        out_specs=[pl.BlockSpec((1, half, HEAD_DIM), spot)] * 2
        + [pl.BlockSpec((1, 1, 8, half), lambda s, h: (s, h, 0, 0))] * 2,
        out_shape=[jax.ShapeDtypeStruct((SEQS, half, heads * HEAD_DIM), BF16)] * 2
        + [jax.ShapeDtypeStruct((SEQS, heads, 8, half), F32)] * 2,
        cost_estimate=pl.CostEstimate(
            flops=48 * heads * half * half * HEAD_DIM,
            bytes_accessed=64 * heads * half * HEAD_DIM,
            transcendentals=16 * heads * half * half,
        ),
        name="attend",
    )(flags, *qkv)
    return out[:2], out[2:]


def attend_back_kernel(half, block, core, flag, qkv, grads, lse, out, grad_keys, grad_values):
    scale = 1.0 / math.sqrt(HEAD_DIM)
    grad_keys[...] = jnp.zeros_like(grad_keys)
    grad_values[...] = jnp.zeros_like(grad_values)
    for part in range(2):
        here = part ^ core
        for first in range(0, half, block):
            query = qkv[here][0, first : first + block, :HEAD_DIM]
            grad = grads[here, 0, first : first + block, :]
            level = lse[here][0, 0, 0:1, first : first + block]
            spans = [(here, part, first + block)]
            if part == 1:
                spans = [(core, 0, half)] + spans
            held = []
            weighted = 0.0
            for slot, place, length in spans:
                keys = qkv[slot][0, :length, HEAD_DIM : 2 * HEAD_DIM]
                values = qkv[slot][0, :length, 2 * HEAD_DIM :]
                scores = masked_scores(
                    keys, query, part * half + first, place * half, 1, flag, 2 * half
                )
                probs = jnp.exp(scores - level)
                grad_values[place, :length, :] += jnp.dot(
                    probs.astype(BF16), grad, preferred_element_type=F32
                )
                grad_probs = lax.dot_general(
                    values, grad, (((1,), (1,)), ((), ())), preferred_element_type=F32
                )
                weighted = weighted + jnp.sum(probs * grad_probs, axis=0, keepdims=True)
                held.append((probs, grad_probs, keys))
            grad_query = 0.0
            for (_, place, length), (probs, grad_probs, keys) in zip(spans, held):
                grad_scores = (probs * (grad_probs - weighted)).astype(BF16)
                grad_keys[place, :length, :] += jnp.dot(
                    grad_scores, query, preferred_element_type=F32
                )
                grad_query = grad_query + lax.dot_general(
                    grad_scores, keys, (((0,), (0,)), ((), ())), preferred_element_type=F32
                )
            out[here][0, first : first + block, :HEAD_DIM] = (grad_query * scale).astype(BF16)
    for part in range(2):
        target = out[part ^ core]
        target[0, :, HEAD_DIM : 2 * HEAD_DIM] = (grad_keys[part] * scale).astype(BF16)
        target[0, :, 2 * HEAD_DIM :] = grad_values[part].astype(BF16)


def attend_back(qkv, grads, lse, flags, heads):
    half = qkv[0].shape[1]
    spot = lambda s, h: (s, 0, h)

    def kernel(flags_ref, *refs):
        for core in range(2):

            @pl.when(flags_ref[SEQS] == core)
            def _():
                flag = flags_ref[pl.program_id(0)]
                attend_back_kernel(
                    half, half // 2, core, flag, refs[:2], refs[2], refs[3:5], refs[5:7], *refs[7:]
                )

    return pl.pallas_call(
        kernel,
        grid=(SEQS, heads),
        in_specs=[pl.BlockSpec(memory_space=pltpu.SMEM)]
        + [pl.BlockSpec((1, half, 3 * HEAD_DIM), spot)] * 2
        + [pl.BlockSpec((2, 1, half, HEAD_DIM), lambda s, h: (0, s, 0, h))]
        + [pl.BlockSpec((1, 1, 8, half), lambda s, h: (s, h, 0, 0))] * 2,
        out_specs=[pl.BlockSpec((1, half, 3 * HEAD_DIM), spot)] * 2,
        out_shape=[jax.ShapeDtypeStruct(qkv[0].shape, BF16)] * 2,
        scratch_shapes=[
            pltpu.VMEM((2, half, HEAD_DIM), F32),
            pltpu.VMEM((2, half, HEAD_DIM), F32),
        ],
        cost_estimate=pl.CostEstimate(
            flops=128 * heads * half * half * HEAD_DIM,
            bytes_accessed=128 * heads * half * HEAD_DIM,
            transcendentals=16 * heads * half * half,
        ),
        name="attend_back",
    )(flags, *qkv, grads, *lse)


def sum_everywhere_kernel(number, in_ref, *refs):
    held, out_ref, shards = refs[:number], refs[number], refs[number + 1 : 2 * number + 1]
    got = refs[2 * number + 1]
    moves = Moves(*refs[2 * number + 2 :])
    d = lax.axis_index("dp")
    z = lax.axis_index("seq")
    groups = lax.axis_size("seq")
    count = in_ref.shape[0]
    me = d * groups + z
    barrier = pltpu.get_barrier_semaphore()
    for step in range(1, count):
        to = (me + step) % count
        pl.semaphore_signal(barrier, inc=1, **at_plane(to // groups, to % groups))
    pl.semaphore_wait(barrier, count - 1)
    arrivals = []
    for step in range(1, count):
        to = (me + step) % count
        arrivals.append(moves.far(in_ref.at[to], got.at[step - 1], to // groups, to % groups))
    for held_ref, shard_ref in zip(held, shards):
        unite_columns(moves, held_ref, shard_ref)
    total = in_ref[me]
    for step, arrival in enumerate(arrivals):
        moves.landed(arrival)
        total = total + got[step]
    out_ref[...] = total
    moves.finish()


def sum_everywhere(sums, held):
    count = lax.axis_size("dp") * lax.axis_size("seq")
    kinds, width = sums.shape
    piece = width // count
    lanes = 128
    pieces = jnp.transpose(sums.reshape(kinds, count, piece), (1, 0, 2))
    pieces = pieces.reshape(count, kinds * piece // lanes, lanes)
    number = len(held)
    far = count - 1 + number * (PLANE - 1)
    summed, *shards = pl.pallas_call(
        lambda *refs: sum_everywhere_kernel(number, *refs),
        out_shape=[jax.ShapeDtypeStruct(pieces.shape[1:], F32)]
        + [shaped(h.shape[0] * PLANE, h.shape[1] // PLANE) for h in held],
        in_specs=[pl.BlockSpec(memory_space=pltpu.VMEM)] * (1 + number),
        out_specs=[pl.BlockSpec(memory_space=pltpu.VMEM)]
        + [pl.BlockSpec(memory_space=pl.ANY)] * number,
        scratch_shapes=[
            pltpu.VMEM((count - 1,) + pieces.shape[1:], F32),
            pltpu.SemaphoreType.DMA((far,)),
            pltpu.SemaphoreType.DMA((far,)),
            pltpu.SemaphoreType.DMA((number,)),
        ],
        compiler_params=pltpu.CompilerParams(collective_id=0, has_side_effects=True),
        cost_estimate=pl.CostEstimate(
            flops=0, bytes_accessed=40 * 1024 * 1024, transcendentals=0
        ),
        name="sum_everywhere",
    )(pieces, *held)
    return summed.reshape(kinds, piece), shards


def grouped_shards(
    tokens,
    token_types,
    view_mask,
    type_table,
    ln1_gain,
    ln1_bias,
    w_qkv,
    w_out,
    ln2_gain,
    ln2_bias,
    w_up,
    w_down,
    cotangent,
):
    seq_count, local_len, width = tokens.shape
    groups = lax.axis_size("seq")
    rows = seq_count * local_len
    heads = HEADS // PLANE
    d = lax.axis_index("dp")
    z = lax.axis_index("seq")

    small = jnp.concatenate(
        [type_table, jnp.stack([ln1_gain, ln1_bias, ln2_gain, ln2_bias])], axis=0
    )
    mark = jnp.broadcast_to(view_mask[:, None, None], (seq_count, 4, 128)).reshape(8, 128)
    out_columns = along_z(jnp.transpose(w_out))
    small, marks = intake(small, mark)
    small = jnp.swapaxes(small, 0, 1).reshape(2 * TYPES, width).astype(F32)
    table = small[:TYPES]
    gain_one, bias_one, gain_two, bias_two = (small[TYPES + i] for i in range(4))
    marks = lax.dynamic_index_in_dim(marks[:, ::4, 0], z & 1, 1, keepdims=False)
    marks = lax.dynamic_index_in_dim(
        marks.reshape(SEQS, 2), (d & 1) ^ (z >> 1), 1, keepdims=False
    )
    flags = jnp.concatenate([marks, (d & 1)[None]])

    types = token_types.reshape(rows)
    onehot = (types[:, None] == jnp.arange(TYPES, dtype=jnp.int32)[None, :]).astype(F32)
    start_hidden = tokens.reshape(rows, width).astype(F32) + jnp.dot(
        onehot, table, precision=HIGHEST_PRECISION
    )
    cot = cotangent.reshape(rows, width)
    norm_one, pull_one = jax.vjp(layer_norm, start_hidden, gain_one, bias_one)
    chips, others, qkv_full, up_half, down_half = first_gather(
        norm_one.astype(BF16).reshape(tokens.shape),
        jnp.transpose(w_qkv),
        jnp.transpose(w_up),
        w_down,
        [out_columns],
    )
    up_full = along_z(up_half)
    down_full = along_z(down_half)
    normed = [part.reshape(4 * rows, width) for part in (chips, others)]
    qkv_full = qkv_full[:4].reshape(-1, width)
    qkv = [
        jnp.einsum("td,ed->te", part, qkv_full, preferred_element_type=F32)
        .astype(BF16)
        .reshape(SEQS, rows, 3 * heads * HEAD_DIM)
        for part in normed
    ]
    context, lse = attend(qkv, flags, heads)
    context_rows, out_chips, out_others = contexts_home(context, jnp.transpose(out_columns))
    cot_chips = chips_gather(after(cot, chips), context)
    mid_hidden = (
        start_hidden
        + jnp.dot(context_rows[:, : width // 2], out_chips, preferred_element_type=F32)
        + jnp.dot(context_rows[:, width // 2 :], out_others, preferred_element_type=F32)
    )
    norm_two, pull_two = jax.vjp(layer_norm, mid_hidden, gain_two, bias_two)
    ffn_input, cot_others = plane_gather_now(
        norm_two.astype(BF16), cot_chips, 5, []
    )
    cots = (cot_chips, cot_others)
    def weight_grad(left, right):
        return sum(
            jnp.einsum("ti,td->id", a, b, preferred_element_type=F32)
            for a, b in zip(left, right)
        ).astype(BF16)

    acts = []
    grad_ups = []
    for cot_part, input_part in zip(cots, ffn_input):
        grad_act = jnp.einsum("td,id->ti", cot_part, down_full, preferred_element_type=F32)
        up_value = jnp.einsum("td,id->ti", input_part, up_full, preferred_element_type=F32)
        activated, gelu_pull = jax.vjp(gelu_tanh, up_value)
        acts.append(activated.astype(BF16))
        grad_ups.append(gelu_pull(grad_act)[0].astype(BF16))
    grad_normed_two, ffn_out, up_parts, down_grad = feed_back(
        grad_ups, acts, up_full, down_full, ffn_input, cots
    )
    up_sum = jnp.sum(up_parts.astype(F32), axis=0).astype(BF16)
    grad_normed_two = grad_normed_two.astype(F32)
    grad_mid_norm, grad_gain_two, grad_bias_two = pull_two(grad_normed_two)
    grad_mid = cot.astype(F32) + grad_mid_norm
    grad_mid_low = grad_mid.astype(BF16)
    grad_context = jnp.concatenate(
        [
            jnp.einsum("te,de->td", grad_mid_low, part, preferred_element_type=F32).astype(BF16)
            for part in (out_chips, out_others)
        ],
        axis=1,
    )
    output = (mid_hidden + ffn_out.astype(F32)).astype(BF16).reshape(tokens.shape)
    grad_out_weight = [
        jnp.einsum("td,te->de", part, grad_mid_low, preferred_element_type=F32).astype(BF16)
        for part in jnp.split(context_rows, 2, axis=1)
    ]
    out_scatter = Scatter(*grad_out_weight)
    grad_by_heads, up_shard = gradients_out(grad_context, [up_sum], [])
    grad_by_heads, down_grad = lax.optimization_barrier((grad_by_heads, down_grad))
    down_sum = sum_along_z(down_grad)
    grad_by_heads = out_scatter.corners(grad_by_heads)
    grad_qkv = attend_back(qkv, grad_by_heads, lse, flags, heads)
    grad_qkv = [part.reshape(SEQS * rows, 3 * heads * HEAD_DIM) for part in grad_qkv]
    grad_qkv = out_scatter.sides(grad_qkv)
    qkv_grad = shared_heads(weight_grad(grad_qkv, normed))
    qkv_sum = sum_along_z(qkv_grad)
    grad_normed_one, out_sum, sum_down = last_scatter(
        grad_qkv, qkv_full, out_scatter.result().astype(BF16), down_sum, tokens.shape
    )
    grad_normed_one = grad_normed_one.astype(F32)
    grad_start_norm, grad_gain_one, grad_bias_one = pull_one(grad_normed_one.reshape(rows, width))
    grad_start = grad_mid + grad_start_norm
    grad_table = jnp.einsum("tk,td->kd", onehot, grad_start, precision=HIGHEST_PRECISION)
    sums = jnp.concatenate(
        [
            grad_table,
            jnp.stack([grad_gain_one, grad_bias_one, grad_gain_two, grad_bias_two]),
        ],
        axis=0,
    )
    sums, (qkv_shard,) = sum_everywhere(sums, [qkv_sum])
    sum_qkv = jnp.transpose(qkv_shard)
    sum_up = jnp.transpose(up_shard)
    return (
        output,
        grad_start.reshape(tokens.shape),
        sums[:TYPES],
        sums[TYPES],
        sums[TYPES + 1],
        sum_qkv.astype(F32),
        out_sum.astype(F32),
        sums[TYPES + 2],
        sums[TYPES + 3],
        sum_up.astype(F32),
        sum_down.astype(F32),
    )


def solution(mesh):
    placed = (
        P("dp", "seq", None),
        P("dp", "seq"),
        P("dp"),
        P(None, "seq"),
        P("seq"),
        P("seq"),
        P("dp", "seq"),
        P("dp", "seq"),
        P("seq"),
        P("seq"),
        P("dp", "seq"),
        P("seq", "dp"),
        P("dp", "seq", None),
    )
    fits = mesh.shape["dp"] == 8 and mesh.shape["seq"] == 4
    return jax.shard_map(
        grouped_shards if fits else plain_shards,
        mesh=mesh,
        in_specs=placed,
        out_specs=(
            P("dp", "seq", None),
            P("dp", "seq", None),
            P(None, ("dp", "seq")),
            P(("dp", "seq")),
            P(("dp", "seq")),
            P("dp", "seq"),
            P("dp", "seq"),
            P(("dp", "seq")),
            P(("dp", "seq")),
            P("dp", "seq"),
            P("seq", "dp"),
        ),
        check_vma=False,
    )
```

```python
import math

import jax
import jax.numpy as jnp
from jax import lax
from jax.experimental import pallas as pl
from jax.experimental.pallas import tpu as pltpu
from jax.sharding import PartitionSpec as P

HEADS = 16
HEAD_DIM = 128
TYPES = 4


EPS = 1e-05
NEGATIVE = -1e30
HIGHEST_PRECISION = lax.Precision.HIGHEST


def layer_norm(hidden, gain, bias):
    average = jnp.mean(hidden, axis=-1, keepdims=True)
    centered = hidden - average
    variance = jnp.mean(centered * centered, axis=-1, keepdims=True)
    return centered * lax.rsqrt(variance + EPS) * gain + bias


def gelu_tanh(value):
    inner = math.sqrt(2.0 / math.pi) * (value + 0.044715 * value * value * value)
    return 0.5 * value * (1.0 + jnp.tanh(inner))


def key_allowed(first, count, full_len, view_flag):
    query_pos = first + jnp.arange(count, dtype=jnp.int32)
    key_pos = jnp.arange(full_len, dtype=jnp.int32)
    causal = key_pos[None, :] <= query_pos[:, None]
    seen = jnp.logical_or(view_flag == 1, key_pos % (full_len // 2) < full_len // 4)
    return jnp.logical_and(causal, seen[None, :])


def scores_of(query, keys, allowed, scale):
    plain = jnp.einsum("qhd,khd->hqk", query, keys, preferred_element_type=jnp.float32) * scale
    return jnp.where(allowed[None], plain, NEGATIVE)


def to_heads(values_in):
    return lax.all_to_all(values_in, "seq", split_axis=2, concat_axis=1, tiled=True)


def to_tokens(values_in):
    return lax.all_to_all(values_in, "seq", split_axis=1, concat_axis=2, tiled=True)


def plain_shards(
    tokens,
    token_types,
    view_mask,
    type_table,
    ln1_gain,
    ln1_bias,
    w_qkv,
    w_out,
    ln2_gain,
    ln2_bias,
    w_up,
    w_down,
    cotangent,
):
    seq_count, local_len, width = tokens.shape
    groups = lax.axis_size("seq")
    full_len = local_len * groups
    row_count = seq_count * local_len
    local_heads = HEADS // groups
    scale = 1.0 / math.sqrt(HEAD_DIM)
    block = min(512, full_len)
    f32 = jnp.float32
    bf16 = jnp.bfloat16
    out_part, table, gain_one, bias_one, gain_two, bias_two = (
        lax.all_gather(w_out, "seq", axis=1, tiled=True),
        lax.all_gather(type_table, "seq", axis=1, tiled=True),
        lax.all_gather(ln1_gain, "seq", axis=0, tiled=True),
        lax.all_gather(ln1_bias, "seq", axis=0, tiled=True),
        lax.all_gather(ln2_gain, "seq", axis=0, tiled=True),
        lax.all_gather(ln2_bias, "seq", axis=0, tiled=True),
    )
    qkv_full, out_full, up_full, down_full = (
        lax.all_gather(w_qkv, "dp", axis=0, tiled=True),
        lax.all_gather(out_part, "dp", axis=0, tiled=True),
        lax.all_gather(w_up, "dp", axis=0, tiled=True),
        lax.all_gather(w_down, "dp", axis=1, tiled=True),
    )
    onehot = (
        token_types.reshape(row_count)[:, None] == jnp.arange(TYPES, dtype=jnp.int32)[None, :]
    ).astype(f32)
    start_hidden = tokens.reshape(row_count, width).astype(f32) + jnp.dot(
        onehot, table.astype(f32), precision=HIGHEST_PRECISION
    )
    norm_one, pull_one = jax.vjp(
        layer_norm, start_hidden, gain_one.astype(f32), bias_one.astype(f32)
    )
    normed_one = norm_one.astype(bf16)
    normed_rows = lax.all_gather(
        normed_one.reshape(seq_count, local_len, width), "seq", axis=1, tiled=True
    )
    by_heads = jnp.einsum("std,de->ste", normed_rows, qkv_full, preferred_element_type=f32).astype(
        bf16
    )
    by_heads = by_heads.reshape(seq_count, full_len, local_heads, 3, HEAD_DIM)
    contexts = []
    kept_lse = []
    for index in range(seq_count):
        keys = by_heads[index, :, :, 1]
        values = by_heads[index, :, :, 2]
        context_blocks = []
        lse_blocks = []
        for first in range(0, full_len, block):
            query = by_heads[index, first : first + block, :, 0]
            allowed = key_allowed(first, block, full_len, view_mask[index])
            scores = scores_of(query, keys, allowed, scale)
            top = jnp.max(scores, axis=-1, keepdims=True)
            expd = jnp.exp(scores - top)
            total = jnp.sum(expd, axis=-1, keepdims=True)
            probs_low = (expd / total).astype(bf16)
            context_blocks.append(
                jnp.einsum("hqk,khd->qhd", probs_low, values, preferred_element_type=f32).astype(
                    bf16
                )
            )
            lse_blocks.append(top + jnp.log(total))
        contexts.append(jnp.concatenate(context_blocks, axis=0))
        kept_lse.append(lse_blocks)
    context_heads = jnp.stack(contexts)
    context_rows = to_tokens(context_heads).reshape(row_count, width)
    mid_hidden = start_hidden + jnp.dot(context_rows, out_full, preferred_element_type=f32)
    norm_two, pull_two = jax.vjp(layer_norm, mid_hidden, gain_two.astype(f32), bias_two.astype(f32))
    normed_two = norm_two.astype(bf16)
    cot_rows = cotangent.reshape(row_count, width)
    ffn_input, grad_rows = (
        lax.all_gather(normed_two, "seq", axis=0, tiled=True),
        lax.all_gather(cot_rows, "seq", axis=0, tiled=True),
    )
    up_value = jnp.dot(ffn_input, up_full, preferred_element_type=f32)
    activated, gelu_pull = jax.vjp(gelu_tanh, up_value)
    activated_low = activated.astype(bf16)
    piece = activated_low
    ffn_out = lax.psum_scatter(
        jnp.dot(piece, down_full, preferred_element_type=f32).astype(jnp.bfloat16),
        "seq",
        scatter_dimension=0,
        tiled=True,
    ).astype(jnp.float32)
    output = (mid_hidden + ffn_out).astype(bf16).reshape(seq_count, local_len, width)
    grad_down = jnp.einsum("ti,td->id", activated_low, grad_rows, preferred_element_type=f32)
    grad_act = jnp.einsum("td,id->ti", grad_rows, down_full, preferred_element_type=f32)
    grad_up_value = gelu_pull(grad_act)[0].astype(bf16)
    grad_up = jnp.einsum("td,ti->di", ffn_input, grad_up_value, preferred_element_type=f32)
    piece = grad_up_value
    grad_normed_two = lax.psum_scatter(
        jnp.einsum("ti,di->td", piece, up_full, preferred_element_type=f32).astype(jnp.bfloat16),
        "seq",
        scatter_dimension=0,
        tiled=True,
    ).astype(jnp.float32)
    grad_mid_norm, grad_gain_two, grad_bias_two = pull_two(grad_normed_two)
    grad_mid = cot_rows.astype(f32) + grad_mid_norm
    grad_mid_low = grad_mid.astype(bf16)
    grad_out_weight = jnp.einsum(
        "td,te->de", context_rows, grad_mid_low, preferred_element_type=f32
    )
    grad_context = jnp.einsum(
        "te,de->td", grad_mid_low, out_full, preferred_element_type=f32
    ).astype(bf16)
    grad_context = grad_context.reshape(seq_count, local_len, HEADS, HEAD_DIM)
    grad_by_heads = to_heads(grad_context)
    grad_parts = []
    for index in range(seq_count):
        keys = by_heads[index, :, :, 1]
        values = by_heads[index, :, :, 2]
        grad_keys = jnp.zeros(keys.shape, f32)
        grad_values = jnp.zeros(values.shape, f32)
        grad_query_blocks = []
        for number, first in enumerate(range(0, full_len, block)):
            query = by_heads[index, first : first + block, :, 0]
            allowed = key_allowed(first, block, full_len, view_mask[index])
            scores = scores_of(query, keys, allowed, scale)
            probs = jnp.exp(scores - kept_lse[index][number])
            probs_low = probs.astype(bf16)
            grad_block = grad_by_heads[index, first : first + block]
            grad_values = grad_values + jnp.einsum(
                "hqk,qhd->khd", probs_low, grad_block, preferred_element_type=f32
            )
            grad_probs = jnp.einsum("qhd,khd->hqk", grad_block, values, preferred_element_type=f32)
            weighted = jnp.sum(probs * grad_probs, axis=-1, keepdims=True)
            grad_scores = (probs * (grad_probs - weighted)).astype(bf16)
            grad_query_blocks.append(
                jnp.einsum("hqk,khd->qhd", grad_scores, keys, preferred_element_type=f32) * scale
            )
            grad_keys = (
                grad_keys
                + jnp.einsum("hqk,qhd->khd", grad_scores, query, preferred_element_type=f32) * scale
            )
        grad_parts.append(
            jnp.stack([jnp.concatenate(grad_query_blocks, axis=0), grad_keys, grad_values], axis=2)
        )
    grad_projected = jnp.stack(grad_parts).astype(bf16)
    columns = qkv_full.shape[1]
    grad_flat = grad_projected.reshape(seq_count, full_len, columns)
    grad_qkv_weight = jnp.einsum("std,ste->de", normed_rows, grad_flat, preferred_element_type=f32)
    position_major = jnp.transpose(grad_flat, (1, 0, 2)).reshape(full_len * seq_count, columns)
    piece = position_major
    summed_rows = lax.psum_scatter(
        jnp.einsum("te,de->td", piece, qkv_full, preferred_element_type=f32).astype(jnp.bfloat16),
        "seq",
        scatter_dimension=0,
        tiled=True,
    ).astype(jnp.float32)
    grad_normed_one = jnp.transpose(
        summed_rows.reshape(local_len, seq_count, width), (1, 0, 2)
    ).reshape(row_count, width)
    grad_start_norm, grad_gain_one, grad_bias_one = pull_one(grad_normed_one)
    grad_start = grad_mid + grad_start_norm
    input_grad = grad_start.reshape(seq_count, local_len, width)
    grad_table = jnp.einsum("tk,td->kd", onehot, grad_start, precision=HIGHEST_PRECISION)
    (
        sum_qkv,
        sum_out,
        sum_up,
        sum_down,
        sum_table,
        sum_gain_one,
        sum_bias_one,
        sum_gain_two,
        sum_bias_two,
    ) = (
        lax.psum_scatter(
            grad_qkv_weight.astype(jnp.bfloat16), "dp", scatter_dimension=0, tiled=True
        ).astype(jnp.float32),
        lax.psum_scatter(
            grad_out_weight.astype(jnp.bfloat16), "dp", scatter_dimension=0, tiled=True
        ).astype(jnp.float32),
        lax.psum_scatter(
            grad_up.astype(jnp.bfloat16), "dp", scatter_dimension=0, tiled=True
        ).astype(jnp.float32),
        lax.psum_scatter(
            grad_down.astype(jnp.bfloat16), "dp", scatter_dimension=1, tiled=True
        ).astype(jnp.float32),
        lax.psum_scatter(
            grad_table.astype(jnp.bfloat16), "dp", scatter_dimension=1, tiled=True
        ).astype(jnp.float32),
        lax.psum_scatter(
            grad_gain_one.astype(jnp.bfloat16), "dp", scatter_dimension=0, tiled=True
        ).astype(jnp.float32),
        lax.psum_scatter(
            grad_bias_one.astype(jnp.bfloat16), "dp", scatter_dimension=0, tiled=True
        ).astype(jnp.float32),
        lax.psum_scatter(
            grad_gain_two.astype(jnp.bfloat16), "dp", scatter_dimension=0, tiled=True
        ).astype(jnp.float32),
        lax.psum_scatter(
            grad_bias_two.astype(jnp.bfloat16), "dp", scatter_dimension=0, tiled=True
        ).astype(jnp.float32),
    )
    final_out, final_table, final_gain_one, final_bias_one, final_gain_two, final_bias_two = (
        lax.psum_scatter(
            sum_out.astype(jnp.bfloat16), "seq", scatter_dimension=1, tiled=True
        ).astype(jnp.float32),
        lax.psum_scatter(
            sum_table.astype(jnp.bfloat16), "seq", scatter_dimension=1, tiled=True
        ).astype(jnp.float32),
        lax.psum_scatter(
            sum_gain_one.astype(jnp.bfloat16), "seq", scatter_dimension=0, tiled=True
        ).astype(jnp.float32),
        lax.psum_scatter(
            sum_bias_one.astype(jnp.bfloat16), "seq", scatter_dimension=0, tiled=True
        ).astype(jnp.float32),
        lax.psum_scatter(
            sum_gain_two.astype(jnp.bfloat16), "seq", scatter_dimension=0, tiled=True
        ).astype(jnp.float32),
        lax.psum_scatter(
            sum_bias_two.astype(jnp.bfloat16), "seq", scatter_dimension=0, tiled=True
        ).astype(jnp.float32),
    )
    return (
        output,
        input_grad,
        final_table,
        final_gain_one,
        final_bias_one,
        sum_qkv,
        final_out,
        final_gain_two,
        final_bias_two,
        sum_up,
        sum_down,
    )


PLANE = 8
QUAD = 4
F32 = jnp.float32
BF16 = jnp.bfloat16
MESH_ID = pl.DeviceIdType.MESH
CORE, X_WAY, Y_WAY = 1, 2, 4
FAR_FIRST = (6, 7, 2, 3, 4, 5, 1)


def swap(value, mask):
    dp = lax.axis_size("dp")
    return lax.ppermute(value, "dp", [(i, i ^ mask) for i in range(dp)])


def after(value, *earlier):
    return lax.optimization_barrier((value, earlier))[0]


def at_plane(d, z):
    return dict(device_id=(d, z), device_id_type=MESH_ID)


class Moves:
    def __init__(self, send_sem, recv_sem, local_sem=None):
        self.sems = (send_sem, recv_sem, local_sem)
        self.count = [0, 0]
        self.open = []
        self.done = []

    def far(self, source, target, d, z, sends=None, receives=None, lands=None, own=None):
        number = self.count[0] if own is None else own
        self.count[0] += own is None

        def copy(landing):
            return pltpu.make_async_remote_copy(
                src_ref=source,
                dst_ref=target,
                send_sem=self.sems[0].at[number],
                recv_sem=self.sems[1].at[landing],
                **at_plane(d, z),
            )

        out = copy(number if lands is None else lands)
        when(sends, out.start)
        move = [(out, copy(number)), sends, receives, False]
        self.open.append(move)
        return move

    def here(self, source, target, sends=None):
        number = self.count[1]
        self.count[1] += 1
        copy = pltpu.make_async_copy(source, target, self.sems[2].at[number])
        when(sends, copy.start)
        move = [copy, sends, None, False]
        self.open.append(move)
        return move

    def landed(self, move):
        copy, sends, receives, done = move
        assert not done
        move[3] = True
        if isinstance(copy, tuple):
            when(receives, copy[1].wait_recv)
        else:
            when(sends, copy.wait)

    def sent(self, move):
        when(move[1], move[0][0].wait_send)
        self.done.append(id(move))

    def finish(self):
        for move in self.open:
            if not move[3]:
                self.landed(move)
            if isinstance(move[0], tuple) and id(move) not in self.done:
                self.sent(move)


def when(condition, do):
    if condition is None:
        do()
    else:
        pl.when(condition)(do)


def meet_all(masks, lines=True, peers=False):
    d = lax.axis_index("dp")
    z = lax.axis_index("seq")
    groups = lax.axis_size("seq")
    barrier = pltpu.get_barrier_semaphore()
    count = len(masks)
    for mask in masks:
        pl.semaphore_signal(barrier, inc=1, **at_plane(d ^ mask, z))
    if lines:
        count = count + groups - 1
        for step in range(1, groups):
            pl.semaphore_signal(barrier, inc=1, **at_plane(d, (z + step) % groups))
    if peers:
        for number in range(2):
            to_d, to_z, itself = peer_of(number)
            away = jnp.logical_not(itself)

            def signal(to_d=to_d, to_z=to_z):
                pl.semaphore_signal(barrier, inc=1, **at_plane(to_d, to_z))

            when(away, signal)
            count = count + jnp.where(itself, 0, 1)
    pl.semaphore_wait(barrier, count)


def peer_of(number):
    d = lax.axis_index("dp")
    z = lax.axis_index("seq")
    core = d & 1
    to_d = (d - core) + (z >> 1)
    to_z = 2 * core + number
    return to_d, to_z, jnp.logical_and(to_d == d, to_z == z)


def exchange_along_z(moves, number, source, target, base=None):
    z = lax.axis_index("seq")
    own = None if base is None else base + number
    base = moves.count[0] - number if base is None else base
    to_d, to_z, itself = peer_of(number)
    away = jnp.logical_not(itself)
    far = moves.far(source, target(z & 1), to_d, to_z, away, away, base + (z & 1), own)
    near = moves.here(source, target(z & 1), itself)
    return far, near


def all_landed(moves, landing):
    for move in landing:
        moves.landed(move)


def intake_kernel(small_ref, mark_ref, whole_ref, marks_ref, *sems):
    moves = Moves(*sems)
    d = lax.axis_index("dp")
    z = lax.axis_index("seq")
    groups = lax.axis_size("seq")
    meet_all(range(1, PLANE))
    moves.here(small_ref, whole_ref.at[z])
    for step in range(1, groups):
        moves.far(small_ref, whole_ref.at[z], d, (z + step) % groups)
    moves.here(mark_ref, marks_ref.at[0])
    for mask in range(1, PLANE):
        moves.far(mark_ref, marks_ref.at[mask], d ^ mask, z)
    moves.finish()


def spread_columns(moves, shard, half):
    d = lax.axis_index("dp")
    z = lax.axis_index("seq")
    part, width = shard.shape[0] // PLANE, shard.shape[1]
    target = half.at[:, pl.ds(pl.multiple_of(d * width, 128), width)]

    def rows(mask):
        return shard.at[pl.ds(pl.multiple_of((d ^ mask) * part, 64), part)]

    return [moves.here(rows(0), target)] + [
        moves.far(rows(mask), target, d ^ mask, z) for mask in FAR_FIRST
    ]


def kernel_call(
    kernel, inputs, outputs, far, here, number, name, traffic, spaces=None, scratch=(), late=()
):
    count = len(inputs)

    def body(*refs):
        kernel(*refs[:count], *refs[count + len(late) :])

    return pl.pallas_call(
        body,
        out_shape=outputs,
        in_specs=[pl.BlockSpec(memory_space=space) for space in spaces or [pltpu.VMEM] * count]
        + [pl.BlockSpec(memory_space=pl.ANY)] * len(late),
        out_specs=[pl.BlockSpec(memory_space=pl.ANY)] * len(outputs),
        scratch_shapes=[
            *scratch,
            pltpu.SemaphoreType.DMA((far,)),
            pltpu.SemaphoreType.DMA((far,)),
            pltpu.SemaphoreType.DMA((here,)),
        ],
        compiler_params=pltpu.CompilerParams(
            collective_id=number, has_side_effects=True, vmem_limit_bytes=56 * 1024 * 1024
        ),
        cost_estimate=pl.CostEstimate(
            flops=0, bytes_accessed=traffic * 3 * 1024 * 1024, transcendentals=0
        ),
        name=name,
    )(*inputs, *late)


def shaped(*shape):
    return jax.ShapeDtypeStruct(shape, BF16)


def intake(small, mark):
    groups = lax.axis_size("seq")
    return kernel_call(
        intake_kernel,
        [small, mark],
        [
            shaped(groups, *small.shape),
            jax.ShapeDtypeStruct((PLANE,) + mark.shape, mark.dtype),
        ],
        groups - 1 + PLANE - 1,
        2,
        1,
        "intake",
        10,
    )


def gather_rows(moves, rows_ref, chips_ref, others_ref, ready=None, pieces=2, passed=None):
    d = lax.axis_index("dp")
    z = lax.axis_index("seq")
    size = chips_ref.shape[1] // pieces
    parts = [pl.ds(number * size, size) for number in range(pieces)]
    order = [i + j for i in range(pieces // 2) for j in (0, pieces // 2)]

    def far(source, target, mask):
        return moves.far(source, target, d ^ mask, z)

    def keep(chip, move):
        if passed is not None:
            passed.setdefault(chip, []).append(move)

    if ready is None:
        moves.here(rows_ref, chips_ref.at[0])
    over_x = {}
    over_y = {}
    for number in order:
        part = parts[number]
        if ready is None:
            source = rows_ref.at[part]
        else:
            ready(number)
            source = chips_ref.at[0, part]
        over_x[number] = far(source, chips_ref.at[1, part], X_WAY)
        over_y[number] = far(source, chips_ref.at[2, part], Y_WAY)
        keep(0, far(source, others_ref.at[0, part], CORE))

    def pass_on(chip, number):
        part = parts[number]
        keep(chip, far(chips_ref.at[chip, part], others_ref.at[chip, part], CORE))

    corner = {}
    for number in order:
        yield
        part = parts[number]
        first = number < pieces // 2
        via, chip, mask = (over_y, 2, X_WAY) if first else (over_x, 1, Y_WAY)
        moves.landed(via[number])
        corner[number] = far(chips_ref.at[chip, part], chips_ref.at[3, part], mask)
        pass_on(chip, number)
        moves.landed((over_x if first else over_y)[number])
        pass_on(3 - chip, number)
    yield
    for number in order:
        moves.landed(corner[number])
        pass_on(3, number)


GATHER_COPIES = 14
FIRST_PIECES = 4


def gather_along_z(moves, shard_ref, place, target):
    d = lax.axis_index("dp")
    z = lax.axis_index("seq")
    own = moves.here(shard_ref, target.at[place(z)])
    arrivals = []
    for step in (2, -2, 1, -1):
        to, source = z + step, z - step
        inside = jnp.logical_and(to >= 0, to < 4)
        comes = jnp.logical_and(source >= 0, source < 4)
        arrivals.append(
            moves.far(shard_ref, target.at[place(z)], d, jnp.clip(to, 0, 3), inside, comes)
        )
    yield
    for arrival in arrivals:
        moves.landed(arrival)
    for end, via, to in ((0, 2, 3), (3, 1, 0)):
        arrivals.append(
            moves.far(target.at[place(end)], target.at[place(end)], d, to, z == via, z == to)
        )
    yield
    for arrival in arrivals[4:] + [own]:
        moves.landed(arrival)


Z_COPIES = 6


def first_kernel(rows_ref, qkv_ref, up_ref, down_ref, *refs):
    chips, others, heads, up_half, down_half, qkv_half = refs[:6]
    moves = Moves(*refs[6:])
    d = lax.axis_index("dp")
    core = d & 1
    half = rows_ref.shape[1]
    meet_all(range(1, PLANE), peers=True)
    size = 2 * half // FIRST_PIECES
    landing = {}
    for piece in range(FIRST_PIECES // 2):
        for number in range(2):
            landing[number * (FIRST_PIECES // 2) + piece] = exchange_along_z(
                moves,
                number,
                rows_ref.at[number, pl.ds(piece * size, size)],
                lambda at: chips.at[
                    0, pl.ds(pl.multiple_of(at * half + piece * size, size), size)
                ],
            )
    spread = spread_columns(moves, qkv_ref, qkv_half)
    spread_columns(moves, up_ref, up_half)
    spread_columns(moves, down_ref, down_half)
    all_landed(moves, spread)

    def place(at):
        own = (at >> 1) == core
        return jnp.where(own, (at & 1) * 2 + core, 4 + (at & 1))

    qkv = gather_along_z(moves, qkv_half, place, heads)
    next(qkv)
    rows = gather_rows(
        moves,
        None,
        chips,
        others,
        lambda number: all_landed(moves, landing[number]),
        FIRST_PIECES,
    )
    for _ in range(FIRST_PIECES):
        next(rows)
    next(qkv)
    next(rows)
    next(qkv, None)
    z = lax.axis_index("seq")
    for number in range(2):
        moves.far(heads.at[4 + number], heads.at[number * 2 + core], d ^ CORE, z)
    next(rows, None)
    moves.finish()


def first_gather(rows, qkv_shard, up_shard, down_shard, late):
    seqs, half, width = rows.shape
    part = qkv_shard.shape[0] // PLANE
    return kernel_call(
        first_kernel,
        [rows, qkv_shard, up_shard, down_shard],
        [
            shaped(4, seqs * half, width),
            shaped(4, seqs * half, width),
            shaped(6, part, width),
            shaped(up_shard.shape[0] // PLANE, width),
            shaped(down_shard.shape[0] // PLANE, width),
            shaped(part, width),
        ],
        7 * FIRST_PIECES + Z_COPIES + FIRST_PIECES + 2 + 3 * (PLANE - 1),
        4 + FIRST_PIECES,
        2,
        "first_gather",
        110,
        late=late,
    )[:5]


def gather_kernel(
    rows_ref,
    held_ref,
    weights_ref,
    chips,
    others,
    held_others,
    chips_out,
    others_out,
    weights,
    blocks_held,
    results_held,
    weights_sem,
    blocks_sem,
    results_sem,
    *sems,
):
    moves = Moves(*sems)
    d = lax.axis_index("dp")
    z = lax.axis_index("seq")
    count = rows_ref.shape[0]
    blocks = Slots(blocks_held, blocks_sem)
    results = Slots(results_held, results_sem)
    weights_in = pltpu.make_async_copy(weights_ref, weights, weights_sem)
    weights_in.start()
    meet_all((CORE, X_WAY, Y_WAY), lines=False)
    passed = {}
    done = []

    def multiply(source, target, chip, block=None):
        slot = len(done) % 2
        done.append(chip)
        if block is None:
            blocks.load(slot, source.at[chip])
            block = blocks.wait(slot)
        result = results.wait(slot)

        @pl.loop(0, count // 256)
        def _(i):
            at = pl.ds(pl.multiple_of(i * 256, 256), 256)
            result[at, :] = lax.dot_general(
                block[at, :], weights[...], (((1,), (1,)), ((), ())), preferred_element_type=F32
            )

        results.store(slot, target.at[pl.ds(chip * count, count)])

    def multiply_others(chip):
        all_landed(moves, passed[chip])
        multiply(others, others_out, chip)

    steps = gather_rows(moves, rows_ref, chips, others, passed=passed)
    next(steps)
    moves.far(held_ref, held_others, d ^ CORE, z)
    weights_in.wait()
    multiply(None, chips_out, 0, rows_ref)
    multiply_others(0)
    next(steps)
    next(steps)
    for chip in (1, 2):
        multiply(chips, chips_out, chip)
    for chip in (1, 2):
        multiply_others(chip)
    next(steps, None)
    multiply(chips, chips_out, 3)
    multiply_others(3)
    for slot in range(2):
        results.wait(slot)
    moves.finish()


def gather_multiply(rows, held, weights, number):
    count, width = rows.shape
    units = weights.shape[0]
    product = jax.ShapeDtypeStruct((4 * count, units), F32)
    chips, others, held_others, chips_out, others_out = kernel_call(
        gather_kernel,
        [rows, held, weights],
        [shaped(4, count, width), shaped(4, count, width), shaped(*held.shape), product, product],
        GATHER_COPIES + 1,
        1,
        number,
        "gather_multiply",
        80,
        [pltpu.VMEM, pl.ANY, pl.ANY],
        [
            pltpu.VMEM((units, width), BF16),
            pltpu.VMEM((2, count, width), BF16),
            pltpu.VMEM((2, count, units), F32),
            pltpu.SemaphoreType.DMA(()),
            pltpu.SemaphoreType.DMA((2,)),
            pltpu.SemaphoreType.DMA((2,)),
        ],
    )
    rows = [part.reshape(4 * count, width) for part in (chips, others)]
    return rows, held_others, (chips_out, others_out)


def add_rows(target, start, sources, count, step=64):
    @pl.loop(0, count // step)
    def _(i):
        total = None
        for ref, offset in sources:
            piece = ref[pl.ds(pl.multiple_of(offset + i * step, step), step), :].astype(F32)
            total = piece if total is None else total + piece
        target[pl.ds(pl.multiple_of(start + i * step, step), step), :] = total.astype(target.dtype)


CHIP_ORDER = (3, 1, 2, 0)


def scatter_rows(moves, fill, last, own, got, far, near, done):
    d = lax.axis_index("dp")
    z = lax.axis_index("seq")
    half = own.shape[1] // 2
    first, second = pl.ds(0, half), pl.ds(half, half)

    def send_to(source, target, mask):
        return moves.far(source, target, d ^ mask, z)

    ready = fill(send_to)
    yield
    ready(0)
    add_rows(own.at[0], 0, [(own.at[0], 0), (got.at[0], 0)], half)
    to_x = send_to(own.at[0, first], far.at[0], X_WAY)
    add_rows(own.at[0], half, [(own.at[0], half), (got.at[0], half)], half)
    to_y = send_to(own.at[0, second], far.at[1], Y_WAY)
    ready(1)
    add_rows(own.at[1], 0, [(own.at[1], 0), (got.at[1], 0)], half)
    x_first = send_to(own.at[1, first], near.at[0, first], X_WAY)
    ready(2)
    yield
    moves.landed(to_x)
    add_rows(own.at[2], 0, [(own.at[2], 0), (got.at[2], 0), (far.at[0], 0)], half)
    y_first = send_to(own.at[2, first], near.at[1, first], Y_WAY)
    add_rows(own.at[2], half, [(own.at[2], half), (got.at[2], half)], half)
    y_second = send_to(own.at[2, second], near.at[1, second], Y_WAY)
    moves.landed(to_y)
    add_rows(own.at[1], half, [(own.at[1], half), (got.at[1], half), (far.at[1], 0)], half)
    x_second = send_to(own.at[1, second], near.at[0, second], X_WAY)
    ready(3)
    yield
    for number, arrivals in ((0, (x_first, y_first)), (1, (x_second, y_second))):
        all_landed(moves, arrivals)
        start = number * half
        add_rows(
            done,
            start,
            [(own.at[3], start), (got.at[3], start), (near.at[0], start), (near.at[1], start)],
            half,
        )
        last(number)
    for move in (to_x, to_y, x_first, x_second, y_first, y_second):
        moves.sent(move)


SCATTER_COPIES = 10


def sum_rows(target, sources, step=64):
    @pl.loop(0, target.shape[0] // step)
    def _(i):
        at = pl.ds(pl.multiple_of(i * step, step), step)
        total = sources[0][at, :].astype(F32)
        for ref in sources[1:]:
            total = total + ref[at, :].astype(F32)
        target[at, :] = total.astype(target.dtype)


def sum_along_line(moves, piece, got, target):
    d = lax.axis_index("dp")
    z = lax.axis_index("seq")
    groups = lax.axis_size("seq")
    arrivals = []
    for step in range(1, groups):
        to = (z + step) % groups
        arrivals.append(moves.far(piece(to), got.at[step - 1], d, to))
    yield
    all_landed(moves, arrivals)
    sum_rows(target, [piece(z)] + [got.at[step] for step in range(groups - 1)])


class Slots:
    def __init__(self, places, sems):
        self.places = places
        self.sems = sems
        self.copies = {}

    def load(self, slot, source):
        self.copies[slot] = pltpu.make_async_copy(source, self.places.at[slot], self.sems.at[slot])
        self.copies[slot].start()

    def store(self, slot, target):
        self.copies[slot] = pltpu.make_async_copy(self.places.at[slot], target, self.sems.at[slot])
        self.copies[slot].start()

    def wait(self, slot):
        if slot in self.copies:
            self.copies.pop(slot).wait()
        return self.places.at[slot]


def scatter_products(
    moves, sources, held, rows_in, weights_in, stage, side, last, follow=None, also=None
):
    count = held[0].shape[1]
    blocks = [(1, c) for c in CHIP_ORDER] + [(0, c) for c in CHIP_ORDER]

    def fill(send_to):
        def load(number):
            which, c = blocks[number]
            rows_in.load(number % 2, sources[which].at[pl.ds(c * count, count)])

        load(0)
        matrix = weights_in.wait(side)
        from_core = []
        for number, (which, c) in enumerate(blocks):
            if number + 1 < len(blocks):
                load(number + 1)
            if which == 1 and number >= 2:
                moves.sent(from_core[number - 2])
            place = stage.at[number % 2] if which == 1 else held[0].at[number - 4]
            block = rows_in.wait(number % 2)

            @pl.loop(0, count // 256)
            def _(i):
                at = pl.ds(pl.multiple_of(i * 256, 256), 256)
                place[at, :] = jnp.dot(
                    block[at, :], matrix[...], preferred_element_type=F32
                ).astype(BF16)
                if also is not None:
                    also(which, c, block, i)

            if which == 1:
                from_core.append(send_to(place, held[1].at[number], CORE))
        if follow is not None:
            follow()
        moves.sent(from_core[2])
        moves.sent(from_core[3])
        return lambda i: moves.landed(from_core[i])

    return scatter_rows(moves, fill, last, *held)


def last_kernel(
    chips_ref,
    others_ref,
    weights_ref,
    out_ref,
    held_ref,
    grad_ref,
    out_sum_ref,
    shard_ref,
    own,
    got,
    far,
    near,
    done,
    stage,
    rows_held,
    weights_held,
    out_got,
    out_sum,
    rows_sem,
    weights_sem,
    *sems,
):
    moves = Moves(*sems)
    rows_in = Slots(rows_held, rows_sem)
    weights_in = Slots(weights_held, weights_sem)
    columns = out_sum.shape[1]
    half, width = own.shape[2] // 2, own.shape[3]
    for side in range(2):
        weights_in.load(side, weights_ref.at[:, pl.ds(side * width, width)])
    meet_all(range(1, PLANE), peers=True)
    out = sum_along_line(
        moves,
        lambda at: out_ref.at[:, pl.ds(pl.multiple_of(at * columns, 128), columns)],
        out_got,
        out_sum,
    )
    next(out)

    def scatter(side):
        base = []

        def last(number):
            if number == 0:
                base.append(moves.count[0])
                moves.count[0] += 2
            exchange_along_z(
                moves,
                number,
                done.at[side, pl.ds(number * half, half)],
                lambda at: grad_ref.at[at, :, pl.ds(side * width, width)],
                base[0],
            )

        held = [ref.at[side] for ref in (own, got, far, near, done)]
        return scatter_products(
            moves, (chips_ref, others_ref), held, rows_in, weights_in, stage, side, last
        )

    low, high = scatter(0), scatter(1)
    next(low)
    next(low)
    next(high)
    next(low)
    next(high)
    next(out, None)
    moves.here(out_sum, out_sum_ref)
    next(low, None)
    next(high)
    unite_columns(moves, held_ref, shard_ref)
    next(high, None)
    moves.finish()


def last_scatter(parts, weights, out_grad, held, shape):
    total, units = parts[0].shape
    width = weights.shape[1]
    count, half = total // 4, width // 2
    groups = lax.axis_size("seq")
    rows, columns = out_grad.shape[0], width // groups
    sizes = ((4, count, half), (4, count, half), (2, count // 2, half), (2, count, half))
    return kernel_call(
        last_kernel,
        [*parts, weights, out_grad, held],
        [
            shaped(*shape),
            shaped(rows, columns),
            shaped(held.shape[0] * PLANE, width // PLANE),
        ],
        2 * SCATTER_COPIES + 4 + groups - 1 + PLANE - 1,
        6,
        7,
        "last_scatter",
        100,
        [pl.ANY, pl.ANY, pl.ANY, pltpu.VMEM, pltpu.VMEM],
        [pltpu.VMEM((2,) + size, BF16) for size in sizes + ((count, half),)]
        + [
            pltpu.VMEM((2, count, half), BF16),
            pltpu.VMEM((2, count, units), BF16),
            pltpu.VMEM((2, units, half), BF16),
            pltpu.VMEM((groups - 1, rows, columns), BF16),
            pltpu.VMEM((rows, columns), BF16),
            pltpu.SemaphoreType.DMA((2,)),
            pltpu.SemaphoreType.DMA((2,)),
        ],
    )


def feed_kernel(
    grad_chips,
    grad_others,
    act_chips,
    act_others,
    up_ref,
    down_ref,
    rows_chips,
    rows_others,
    cot_chips,
    cot_others,
    norm_ref,
    out_ref,
    up_parts_ref,
    down_grad_ref,
    left,
    rows_held,
    weights_held,
    own,
    got,
    far,
    near,
    done,
    stage,
    stream_held,
    result_held,
    rows_sem,
    weights_sem,
    stream_sem,
    result_sem,
    free_sem,
    send_sem,
    recv_sem,
    local_sem,
):
    moves = Moves(send_sem, recv_sem, local_sem)
    d = lax.axis_index("dp")
    z = lax.axis_index("seq")
    rows_in = Slots(rows_held, rows_sem)
    weights_in = Slots(weights_held, weights_sem)
    stream = Slots(stream_held, stream_sem)
    results = Slots(result_held, result_sem)
    count, width = own.shape[2], own.shape[3]
    columns = stream_held.shape[2]
    def load_weights(weights, side):
        weights_in.load(side, weights.at[:, pl.ds(side * width, width)])

    def scatter(sources, side, target, follow, keep):
        held = [ref.at[side] for ref in (own, got, far, near, done)]

        def transposed(which, c, block, i):
            tokens = pl.ds(pl.multiple_of(c * count + i * 256, 256), 256)
            for unit in range(0, block.shape[1], 256):
                left[which, unit : unit + 256, tokens] = jnp.transpose(
                    block[pl.ds(pl.multiple_of(i * 256, 256), 256), unit : unit + 256]
                )

        def last(number):
            if number == 1:
                moves.here(held[4], target.at[:, pl.ds(side * width, width)])

        return scatter_products(
            moves,
            sources,
            held,
            rows_in,
            weights_in,
            stage,
            side,
            last,
            follow,
            transposed if keep else None,
        )

    def end(work, side):
        next(work, None)
        all_landed(moves, moves.open[-1:])
        for mask in (CORE, X_WAY, Y_WAY):
            pl.semaphore_signal(free_sem.at[side], inc=1, **at_plane(d ^ mask, z))

    def weight_grad(rights, place):
        chunks = rights[0].shape[1] // columns
        gone = {}

        def load(chunk):
            for side in range(2):
                stream.load(
                    2 * (chunk % 2) + side, rights[side].at[:, pl.ds(chunk * columns, columns)]
                )

        load(0)
        for chunk in range(chunks):
            if chunk + 1 < chunks:
                load(chunk + 1)
            first, second = (stream.wait(2 * (chunk % 2) + side) for side in range(2))
            result = results.wait(chunk % 2)
            for move in gone.pop(chunk % 2, ()):
                moves.sent(move)

            @pl.loop(0, result.shape[0] // 256)
            def _(i):
                at = pl.ds(pl.multiple_of(i * 256, 256), 256)
                total = jnp.dot(left[0, at, :], first[...], preferred_element_type=F32)
                total += jnp.dot(left[1, at, :], second[...], preferred_element_type=F32)
                result[at, :] = total.astype(BF16)

            gone[chunk % 2] = place(result, chunk)
            yield
        for copies in gone.values():
            for move in copies:
                moves.sent(move)

    groups = lax.axis_size("seq")
    part = up_parts_ref.shape[1]

    def to_line(result, chunk):
        target = up_parts_ref.at[:, :, pl.ds(chunk * columns, columns)]
        copies = []
        for step in range(1, groups):
            to = (z + step) % groups
            piece = result.at[pl.ds(pl.multiple_of(to * part, 256), part)]
            copies.append(moves.far(piece, target.at[step], d, to))
        piece = result.at[pl.ds(pl.multiple_of(z * part, 256), part)]
        results.copies[chunk % 2] = pltpu.make_async_copy(
            piece, target.at[0], results.sems.at[chunk % 2]
        )
        results.copies[chunk % 2].start()
        return copies

    def to_memory(result, chunk):
        results.store(chunk % 2, down_grad_ref.at[:, pl.ds(chunk * columns, columns)])
        return ()

    def steps(work, number):
        for _ in range(number):
            next(work, None)

    nothing = lambda: None
    load_weights(up_ref, 0)
    load_weights(up_ref, 1)
    meet_all((CORE, X_WAY, Y_WAY))
    grads = (grad_chips, grad_others)
    acts = (act_chips, act_others)
    norm_low = scatter(grads, 0, norm_ref, lambda: load_weights(down_ref, 0), True)
    norm_high = scatter(grads, 1, norm_ref, lambda: load_weights(down_ref, 1), False)
    out_low = scatter(acts, 0, out_ref, nothing, False)
    out_high = scatter(acts, 1, out_ref, nothing, True)
    up_work = weight_grad((rows_chips, rows_others), to_line)
    down_work = weight_grad((cot_chips, cot_others), to_memory)
    next(norm_low)
    next(norm_low)
    steps(up_work, 3)
    next(norm_low)
    next(norm_high)
    next(norm_high)
    steps(up_work, 3)
    end(norm_low, 0)
    next(norm_high)
    pl.semaphore_wait(free_sem.at[0], 3)
    next(out_low)
    next(out_low)
    steps(up_work, 3)
    end(norm_high, 1)
    next(out_low)
    pl.semaphore_wait(free_sem.at[1], 3)
    next(out_high)
    next(out_high)
    steps(down_work, 4)
    next(out_low, None)
    next(out_high)
    steps(down_work, 5)
    next(out_high, None)
    for slot in range(2):
        results.wait(slot)
    moves.finish()


def feed_back(grads, acts, up_full, down_full, rows, cots):
    total, units = grads[0].shape
    width = up_full.shape[1]
    count = total // 4
    half = width // 2
    columns = 256
    copies = 4 * SCATTER_COPIES + 3 * width // columns
    groups = lax.axis_size("seq")
    ins = [*grads, *acts, up_full, down_full, *rows, *cots]
    return pl.pallas_call(
        feed_kernel,
        out_shape=[shaped(count, width)] * 2
        + [shaped(groups, units // groups, width), shaped(units, width)],
        in_specs=[pl.BlockSpec(memory_space=pl.ANY)] * len(ins),
        out_specs=[pl.BlockSpec(memory_space=pl.ANY)] * 4,
        scratch_shapes=[
            pltpu.VMEM((2, units, total), BF16),
            pltpu.VMEM((2, count, units), BF16),
            pltpu.VMEM((2, units, half), BF16),
            pltpu.VMEM((2, 4, count, half), BF16),
            pltpu.VMEM((2, 4, count, half), BF16),
            pltpu.VMEM((2, 2, count // 2, half), BF16),
            pltpu.VMEM((2, 2, count, half), BF16),
            pltpu.VMEM((2, count, half), BF16),
            pltpu.VMEM((2, count, half), BF16),
            pltpu.VMEM((4, total, columns), BF16),
            pltpu.VMEM((2, units, columns), BF16),
            pltpu.SemaphoreType.DMA((2,)),
            pltpu.SemaphoreType.DMA((2,)),
            pltpu.SemaphoreType.DMA((4,)),
            pltpu.SemaphoreType.DMA((2,)),
            pltpu.SemaphoreType.REGULAR((2,)),
            pltpu.SemaphoreType.DMA((copies,)),
            pltpu.SemaphoreType.DMA((copies,)),
            pltpu.SemaphoreType.DMA((4,)),
        ],
        compiler_params=pltpu.CompilerParams(
            collective_id=6, has_side_effects=True, vmem_limit_bytes=62 * 1024 * 1024
        ),
        cost_estimate=pl.CostEstimate(
            flops=8 * 2 * total * units * width, bytes_accessed=160 * 3 * 1024 * 1024, transcendentals=0
        ),
        name="feed_back",
    )(*ins)


def unite_columns(moves, half_ref, shard_ref):
    d = lax.axis_index("dp")
    z = lax.axis_index("seq")
    part, width = half_ref.shape[0], shard_ref.shape[1]
    target = shard_ref.at[pl.ds(pl.multiple_of(d * part, 64), part)]

    def columns(mask):
        return half_ref.at[:, pl.ds(pl.multiple_of((d ^ mask) * width, 128), width)]

    moves.here(columns(0), target)
    for mask in FAR_FIRST:
        moves.far(columns(mask), target, d ^ mask, z)


def along_z(value):
    return lax.all_gather(value, "seq", axis=0, tiled=True)


def sum_along_z(grad):
    return lax.psum_scatter(grad, "seq", scatter_dimension=0, tiled=True)


def shared_heads(grad):
    heads = HEADS // PLANE
    held = grad.reshape(heads, 2, -1, grad.shape[-1])
    second = lax.axis_index("dp") % 2 == 1
    keep = jnp.where(second, held[:, 1], held[:, 0])
    other = swap(jnp.where(second, held[:, 0], held[:, 1]), CORE)
    whole = jnp.concatenate([jnp.where(second, other, keep), jnp.where(second, keep, other)])
    return whole.reshape(-1, grad.shape[-1])


def chips_gather(rows, second):
    half = rows.shape[0] // 2
    x_rows = swap(rows, X_WAY)
    y_rows = swap(rows, Y_WAY)
    corner_first = swap(after(y_rows[:half], second), X_WAY)
    corner_second = swap(after(x_rows[half:], second), Y_WAY)
    return jnp.concatenate([rows, x_rows, y_rows, corner_first, corner_second])


class Scatter:
    def __init__(self, chips, others):
        self.chips = chips
        self.got = swap(others, CORE)
        self.count = chips.shape[0] // 4

    def both(self, start, size):
        return sum(part[start : start + size].astype(F32) for part in (self.chips, self.got))

    def corners(self, tied):
        half = self.count // 2
        self.got, tied = lax.optimization_barrier((self.got, tied))
        at = 3 * self.count
        self.far = (
            swap(self.both(at, half).astype(BF16), X_WAY),
            swap(self.both(at + half, half).astype(BF16), Y_WAY),
        )
        self.near = (
            swap(self.both(self.count, half).astype(BF16), X_WAY),
            swap(self.both(2 * self.count + half, half).astype(BF16), Y_WAY),
        )
        return tied

    def sides(self, tied):
        half = self.count // 2
        self.far, self.near, tied = lax.optimization_barrier((self.far, self.near, tied))
        x_second = self.both(self.count + half, half) + self.far[1].astype(F32)
        y_first = self.both(2 * self.count, half) + self.far[0].astype(F32)
        self.last = swap(x_second.astype(BF16), X_WAY), swap(y_first.astype(BF16), Y_WAY)
        return tied

    def ends(self, tied):
        self.last, tied = lax.optimization_barrier((self.last, tied))
        return tied

    def result(self):
        half = self.count // 2
        first = self.both(0, half) + self.near[0].astype(F32) + self.last[1].astype(F32)
        second = self.both(half, half) + self.last[0].astype(F32) + self.near[1].astype(F32)
        return jnp.concatenate([first, second])


def place_of(mask):
    return (mask & 1) * (PLANE // 2) + (mask >> 1)


def column_of(holder, member, number):
    head = (2 * (member & 1) + number) * (PLANE // 2) + (member >> 1)
    place = place_of(holder ^ (head >> 1))
    return pl.ds(pl.multiple_of((2 * place + (head & 1)) * HEAD_DIM, HEAD_DIM), HEAD_DIM)


def meet_heads(masks):
    d = lax.axis_index("dp")
    z = lax.axis_index("seq")
    core = d & 1
    groups = lax.axis_size("seq")
    inside = (z >> 1) == core
    barrier = pltpu.get_barrier_semaphore()

    def greet(to_d, to_z, maybe_itself):
        def signal():
            pl.semaphore_signal(barrier, inc=1, **at_plane(to_d, to_z))

        when(jnp.logical_or(to_d != d, to_z != z) if maybe_itself else None, signal)

    for line in range(PLANE // 2):
        for to_z in range(groups):
            greet(((d >> 1) ^ line) * 2 + (z >> 1), to_z, line == 0)
    for mask in range(PLANE):
        for j in range(2):
            greet(d ^ mask, 2 * core + j, mask == 0)
    for mask in masks:
        greet(d ^ mask, z, False)
    pl.semaphore_wait(barrier, 4 * PLANE + len(masks) - jnp.where(inside, 2, 0))


def contexts_home_kernel(chip_ref, other_ref, rows_ref, out_ref, out_chips, out_others, *sems):
    moves = Moves(*sems)
    d = lax.axis_index("dp")
    z = lax.axis_index("seq")
    core = d & 1
    heads = HEADS // PLANE
    half = out_ref.shape[1]
    meet_heads((CORE, X_WAY, Y_WAY))
    comes = []
    for j in range(2):
        comes += [2 * core + j != z] * heads + [None] * ((PLANE - 1) * heads)
    for line in (3, 1, 2, 0):
        to_d = ((d >> 1) ^ line) * 2 + (z >> 1)
        for slot, source in ((0, chip_ref), (1, other_ref)):
            for part in range(2):
                to_z = 2 * (core ^ slot) + part
                itself = jnp.logical_and(to_d == d, to_z == z)
                for number in range(heads):
                    here = source.at[
                        line, pl.ds(part * half, half), pl.ds(number * HEAD_DIM, HEAD_DIM)
                    ]
                    there = out_ref.at[z & 1, :, column_of(to_d, d, number)]
                    moves.far(
                        here,
                        there,
                        to_d,
                        to_z,
                        jnp.logical_not(itself) if line == 0 else None,
                        comes[moves.count[0]],
                        ((z & 1) * PLANE + (d ^ to_d)) * heads + number,
                    )
                    if line == 0:
                        moves.here(here, there, itself)
    for _ in gather_rows(moves, rows_ref, out_chips, out_others):
        pass
    moves.finish()


def contexts_home(context, out_rows):
    lines, rows, columns = context[0].shape
    count, width = out_rows.shape
    heads = HEADS // PLANE
    out, chips, others = kernel_call(
        contexts_home_kernel,
        [*context, out_rows],
        [
            shaped(2, rows // 2, width),
            shaped(4, count, width),
            shaped(4, count, width),
        ],
        2 * PLANE * heads + GATHER_COPIES,
        4 * heads + 1,
        3,
        "contexts_home",
        60,
    )
    chips, others = (part.reshape(-1, width) for part in (chips, others))
    return out.reshape(rows, width), chips, others


def gradients_out_kernel(count, in_ref, *refs):
    sums, out_ref, shards = refs[:count], refs[count], refs[count + 1 : 2 * count + 1]
    moves = Moves(*refs[2 * count + 1 :])
    d = lax.axis_index("dp")
    z = lax.axis_index("seq")
    core = d & 1
    heads = HEADS // PLANE
    half = in_ref.shape[1]
    meet_heads(range(1, PLANE))
    comes = []
    for side in range(2):
        for line in range(PLANE // 2):
            for part in range(2):
                itself = jnp.logical_and((z >> 1) == core, 2 * (core ^ side) + part == z)
                comes += [jnp.logical_not(itself) if line == 0 else None] * heads
    for mask in FAR_FIRST + (0,):
        for j in range(2):
            to_d = d ^ mask
            to_z = 2 * core + j
            line = mask >> 1
            side = (to_d & 1) ^ (z >> 1)
            for number in range(heads):
                here = in_ref.at[j, :, column_of(d, to_d, number)]
                there = out_ref.at[
                    side,
                    line,
                    pl.ds(pl.multiple_of((z & 1) * half, half), half),
                    pl.ds(number * HEAD_DIM, HEAD_DIM),
                ]
                moves.far(
                    here,
                    there,
                    to_d,
                    to_z,
                    to_z != z if mask == 0 else None,
                    comes[moves.count[0]],
                    ((side * (PLANE // 2) + line) * 2 + (z & 1)) * heads + number,
                )
                if mask == 0:
                    moves.here(here, there, to_z == z)
    for held, shard in zip(sums, shards):
        unite_columns(moves, held, shard)
    moves.finish()


def gradients_out(grad, sums, late):
    rows, width = grad.shape
    heads = HEADS // PLANE
    count = len(sums)
    return kernel_call(
        lambda *refs: gradients_out_kernel(count, *refs),
        [grad.reshape(2, rows // 2, width), *sums],
        [shaped(2, PLANE // 2, rows, heads * HEAD_DIM)]
        + [shaped(s.shape[0] * PLANE, s.shape[1] // PLANE) for s in sums],
        2 * PLANE * heads + count * (PLANE - 1),
        2 * heads + count,
        4,
        "gradients_out",
        50,
        late=late,
    )


SEQS = 4


def masked_scores(left, right, first_row, first_column, row_axis, flag, full_len):
    plain = lax.dot_general(
        left, right, (((1,), (1,)), ((), ())), preferred_element_type=F32
    ) * (1.0 / math.sqrt(HEAD_DIM))
    rows = first_row + lax.broadcasted_iota(jnp.int32, plain.shape, row_axis)
    columns = first_column + lax.broadcasted_iota(jnp.int32, plain.shape, 1 - row_axis)
    seen = jnp.logical_or(flag == 1, columns % (full_len // 2) < full_len // 4)
    return jnp.where(jnp.logical_and(columns <= rows, seen), plain, NEGATIVE)


def attend_kernel(half, block, core, flag, qkv, context, lse):
    for part in range(2):
        here = part ^ core
        for first in range(0, half, block):
            query = qkv[here][0, first : first + block, :HEAD_DIM]
            spans = [(here, part, first + block)]
            if part == 1:
                spans = [(core, 0, half)] + spans
            scores = []
            for slot, place, length in spans:
                keys = qkv[slot][0, :length, HEAD_DIM : 2 * HEAD_DIM]
                scores.append(
                    masked_scores(
                        query, keys, part * half + first, place * half, 0, flag, 2 * half
                    )
                )
            top = jnp.max(scores[0], axis=-1, keepdims=True)
            for more in scores[1:]:
                top = jnp.maximum(top, jnp.max(more, axis=-1, keepdims=True))
            expd = [jnp.exp(piece - top) for piece in scores]
            total = sum(jnp.sum(piece, axis=-1, keepdims=True) for piece in expd)
            result = 0.0
            for (slot, _, length), piece in zip(spans, expd):
                values = qkv[slot][0, :length, 2 * HEAD_DIM :]
                result = result + jnp.dot(
                    (piece / total).astype(BF16), values, preferred_element_type=F32
                )
            context[here][0, first : first + block, :] = result.astype(BF16)
            wide = jnp.broadcast_to(top + jnp.log(total), (block, HEAD_DIM))
            lse[here][0, 0, :, first : first + block] = jnp.transpose(wide)[:8]


def attend(qkv, flags, heads):
    half = qkv[0].shape[1]
    spot = lambda s, h: (s, 0, h)

    def kernel(flags_ref, *refs):
        for core in range(2):

            @pl.when(flags_ref[SEQS] == core)
            def _():
                flag = flags_ref[pl.program_id(0)]
                attend_kernel(half, half // 2, core, flag, refs[:2], refs[2:4], refs[4:])

    out = pl.pallas_call(
        kernel,
        grid=(SEQS, heads),
        in_specs=[pl.BlockSpec(memory_space=pltpu.SMEM)]
        + [pl.BlockSpec((1, half, 3 * HEAD_DIM), spot)] * 2,
        out_specs=[pl.BlockSpec((1, half, HEAD_DIM), spot)] * 2
        + [pl.BlockSpec((1, 1, 8, half), lambda s, h: (s, h, 0, 0))] * 2,
        out_shape=[jax.ShapeDtypeStruct((SEQS, half, heads * HEAD_DIM), BF16)] * 2
        + [jax.ShapeDtypeStruct((SEQS, heads, 8, half), F32)] * 2,
        cost_estimate=pl.CostEstimate(
            flops=48 * heads * half * half * HEAD_DIM,
            bytes_accessed=64 * heads * half * HEAD_DIM,
            transcendentals=16 * heads * half * half,
        ),
        name="attend",
    )(flags, *qkv)
    return out[:2], out[2:]


def attend_back_kernel(half, block, core, flag, qkv, grads, lse, out, grad_keys, grad_values):
    scale = 1.0 / math.sqrt(HEAD_DIM)
    grad_keys[...] = jnp.zeros_like(grad_keys)
    grad_values[...] = jnp.zeros_like(grad_values)
    for part in range(2):
        here = part ^ core
        for first in range(0, half, block):
            query = qkv[here][0, first : first + block, :HEAD_DIM]
            grad = grads[here, 0, first : first + block, :]
            level = lse[here][0, 0, 0:1, first : first + block]
            spans = [(here, part, first + block)]
            if part == 1:
                spans = [(core, 0, half)] + spans
            held = []
            weighted = 0.0
            for slot, place, length in spans:
                keys = qkv[slot][0, :length, HEAD_DIM : 2 * HEAD_DIM]
                values = qkv[slot][0, :length, 2 * HEAD_DIM :]
                scores = masked_scores(
                    keys, query, part * half + first, place * half, 1, flag, 2 * half
                )
                probs = jnp.exp(scores - level)
                grad_values[place, :length, :] += jnp.dot(
                    probs.astype(BF16), grad, preferred_element_type=F32
                )
                grad_probs = lax.dot_general(
                    values, grad, (((1,), (1,)), ((), ())), preferred_element_type=F32
                )
                weighted = weighted + jnp.sum(probs * grad_probs, axis=0, keepdims=True)
                held.append((probs, grad_probs, keys))
            grad_query = 0.0
            for (_, place, length), (probs, grad_probs, keys) in zip(spans, held):
                grad_scores = (probs * (grad_probs - weighted)).astype(BF16)
                grad_keys[place, :length, :] += jnp.dot(
                    grad_scores, query, preferred_element_type=F32
                )
                grad_query = grad_query + lax.dot_general(
                    grad_scores, keys, (((0,), (0,)), ((), ())), preferred_element_type=F32
                )
            out[here][0, first : first + block, :HEAD_DIM] = (grad_query * scale).astype(BF16)
    for part in range(2):
        target = out[part ^ core]
        target[0, :, HEAD_DIM : 2 * HEAD_DIM] = (grad_keys[part] * scale).astype(BF16)
        target[0, :, 2 * HEAD_DIM :] = grad_values[part].astype(BF16)


def attend_back(qkv, grads, lse, flags, heads):
    half = qkv[0].shape[1]
    spot = lambda s, h: (s, 0, h)

    def kernel(flags_ref, *refs):
        for core in range(2):

            @pl.when(flags_ref[SEQS] == core)
            def _():
                flag = flags_ref[pl.program_id(0)]
                attend_back_kernel(
                    half, half // 2, core, flag, refs[:2], refs[2], refs[3:5], refs[5:7], *refs[7:]
                )

    return pl.pallas_call(
        kernel,
        grid=(SEQS, heads),
        in_specs=[pl.BlockSpec(memory_space=pltpu.SMEM)]
        + [pl.BlockSpec((1, half, 3 * HEAD_DIM), spot)] * 2
        + [pl.BlockSpec((2, 1, half, HEAD_DIM), lambda s, h: (0, s, 0, h))]
        + [pl.BlockSpec((1, 1, 8, half), lambda s, h: (s, h, 0, 0))] * 2,
        out_specs=[pl.BlockSpec((1, half, 3 * HEAD_DIM), spot)] * 2,
        out_shape=[jax.ShapeDtypeStruct(qkv[0].shape, BF16)] * 2,
        scratch_shapes=[
            pltpu.VMEM((2, half, HEAD_DIM), F32),
            pltpu.VMEM((2, half, HEAD_DIM), F32),
        ],
        cost_estimate=pl.CostEstimate(
            flops=128 * heads * half * half * HEAD_DIM,
            bytes_accessed=128 * heads * half * HEAD_DIM,
            transcendentals=16 * heads * half * half,
        ),
        name="attend_back",
    )(flags, *qkv, grads, *lse)


def sum_everywhere_kernel(number, in_ref, *refs):
    held, out_ref, shards = refs[:number], refs[number], refs[number + 1 : 2 * number + 1]
    got = refs[2 * number + 1]
    moves = Moves(*refs[2 * number + 2 :])
    d = lax.axis_index("dp")
    z = lax.axis_index("seq")
    groups = lax.axis_size("seq")
    count = in_ref.shape[0]
    me = d * groups + z
    barrier = pltpu.get_barrier_semaphore()
    for step in range(1, count):
        to = (me + step) % count
        pl.semaphore_signal(barrier, inc=1, **at_plane(to // groups, to % groups))
    pl.semaphore_wait(barrier, count - 1)
    arrivals = []
    for step in range(1, count):
        to = (me + step) % count
        arrivals.append(moves.far(in_ref.at[to], got.at[step - 1], to // groups, to % groups))
    for held_ref, shard_ref in zip(held, shards):
        unite_columns(moves, held_ref, shard_ref)
    total = in_ref[me]
    for step, arrival in enumerate(arrivals):
        moves.landed(arrival)
        total = total + got[step]
    out_ref[...] = total
    moves.finish()


def sum_everywhere(sums, held):
    count = lax.axis_size("dp") * lax.axis_size("seq")
    kinds, width = sums.shape
    piece = width // count
    lanes = 128
    pieces = jnp.transpose(sums.reshape(kinds, count, piece), (1, 0, 2))
    pieces = pieces.reshape(count, kinds * piece // lanes, lanes)
    number = len(held)
    far = count - 1 + number * (PLANE - 1)
    summed, *shards = pl.pallas_call(
        lambda *refs: sum_everywhere_kernel(number, *refs),
        out_shape=[jax.ShapeDtypeStruct(pieces.shape[1:], F32)]
        + [shaped(h.shape[0] * PLANE, h.shape[1] // PLANE) for h in held],
        in_specs=[pl.BlockSpec(memory_space=pltpu.VMEM)] * (1 + number),
        out_specs=[pl.BlockSpec(memory_space=pltpu.VMEM)]
        + [pl.BlockSpec(memory_space=pl.ANY)] * number,
        scratch_shapes=[
            pltpu.VMEM((count - 1,) + pieces.shape[1:], F32),
            pltpu.SemaphoreType.DMA((far,)),
            pltpu.SemaphoreType.DMA((far,)),
            pltpu.SemaphoreType.DMA((number,)),
        ],
        compiler_params=pltpu.CompilerParams(collective_id=0, has_side_effects=True),
        cost_estimate=pl.CostEstimate(
            flops=0, bytes_accessed=40 * 1024 * 1024, transcendentals=0
        ),
        name="sum_everywhere",
    )(pieces, *held)
    return summed.reshape(kinds, piece), shards


def grouped_shards(
    tokens,
    token_types,
    view_mask,
    type_table,
    ln1_gain,
    ln1_bias,
    w_qkv,
    w_out,
    ln2_gain,
    ln2_bias,
    w_up,
    w_down,
    cotangent,
):
    seq_count, local_len, width = tokens.shape
    groups = lax.axis_size("seq")
    rows = seq_count * local_len
    heads = HEADS // PLANE
    d = lax.axis_index("dp")
    z = lax.axis_index("seq")

    small = jnp.concatenate(
        [type_table, jnp.stack([ln1_gain, ln1_bias, ln2_gain, ln2_bias])], axis=0
    )
    mark = jnp.broadcast_to(view_mask[:, None, None], (seq_count, 4, 128)).reshape(8, 128)
    out_columns = along_z(jnp.transpose(w_out))
    small, marks = intake(small, mark)
    small = jnp.swapaxes(small, 0, 1).reshape(2 * TYPES, width).astype(F32)
    table = small[:TYPES]
    gain_one, bias_one, gain_two, bias_two = (small[TYPES + i] for i in range(4))
    marks = lax.dynamic_index_in_dim(marks[:, ::4, 0], z & 1, 1, keepdims=False)
    marks = lax.dynamic_index_in_dim(
        marks.reshape(SEQS, 2), (d & 1) ^ (z >> 1), 1, keepdims=False
    )
    flags = jnp.concatenate([marks, (d & 1)[None]])

    types = token_types.reshape(rows)
    onehot = (types[:, None] == jnp.arange(TYPES, dtype=jnp.int32)[None, :]).astype(F32)
    start_hidden = tokens.reshape(rows, width).astype(F32) + jnp.dot(
        onehot, table, precision=HIGHEST_PRECISION
    )
    cot = cotangent.reshape(rows, width)
    norm_one, pull_one = jax.vjp(layer_norm, start_hidden, gain_one, bias_one)
    chips, others, qkv_full, up_half, down_half = first_gather(
        norm_one.astype(BF16).reshape(tokens.shape),
        jnp.transpose(w_qkv),
        jnp.transpose(w_up),
        w_down,
        [out_columns],
    )
    up_full = along_z(up_half)
    down_full = along_z(down_half)
    normed = [part.reshape(4 * rows, width) for part in (chips, others)]
    qkv_full = qkv_full[:4].reshape(-1, width)
    qkv = [
        jnp.einsum("td,ed->te", part, qkv_full, preferred_element_type=F32)
        .astype(BF16)
        .reshape(SEQS, rows, 3 * heads * HEAD_DIM)
        for part in normed
    ]
    context, lse = attend(qkv, flags, heads)
    context_rows, out_chips, out_others = contexts_home(context, jnp.transpose(out_columns))
    cot_chips = chips_gather(after(cot, chips), context)
    mid_hidden = (
        start_hidden
        + jnp.dot(context_rows[:, : width // 2], out_chips, preferred_element_type=F32)
        + jnp.dot(context_rows[:, width // 2 :], out_others, preferred_element_type=F32)
    )
    norm_two, pull_two = jax.vjp(layer_norm, mid_hidden, gain_two, bias_two)
    ffn_input, cot_others, ups = gather_multiply(
        norm_two.astype(BF16), cot_chips, up_full, 5
    )
    cot_chips, ups = lax.optimization_barrier((cot_chips, ups))
    cots = (cot_chips, cot_others)
    def weight_grad(left, right):
        return sum(
            jnp.einsum("ti,td->id", a, b, preferred_element_type=F32)
            for a, b in zip(left, right)
        ).astype(BF16)

    acts = []
    grad_ups = []
    for cot_part, up_value in zip(cots, ups):
        grad_act = jnp.einsum("td,id->ti", cot_part, down_full, preferred_element_type=F32)
        activated, gelu_pull = jax.vjp(gelu_tanh, up_value)
        acts.append(activated.astype(BF16))
        grad_ups.append(gelu_pull(grad_act)[0].astype(BF16))
    grad_normed_two, ffn_out, up_parts, down_grad = feed_back(
        grad_ups, acts, up_full, down_full, ffn_input, cots
    )
    up_sum = jnp.sum(up_parts.astype(F32), axis=0).astype(BF16)
    grad_normed_two = grad_normed_two.astype(F32)
    grad_mid_norm, grad_gain_two, grad_bias_two = pull_two(grad_normed_two)
    grad_mid = cot.astype(F32) + grad_mid_norm
    grad_mid_low = grad_mid.astype(BF16)
    grad_context = jnp.concatenate(
        [
            jnp.einsum("te,de->td", grad_mid_low, part, preferred_element_type=F32).astype(BF16)
            for part in (out_chips, out_others)
        ],
        axis=1,
    )
    output = (mid_hidden + ffn_out.astype(F32)).astype(BF16).reshape(tokens.shape)
    grad_out_weight = [
        jnp.einsum("td,te->de", part, grad_mid_low, preferred_element_type=F32).astype(BF16)
        for part in jnp.split(context_rows, 2, axis=1)
    ]
    out_scatter = Scatter(*grad_out_weight)
    grad_by_heads, up_shard = gradients_out(grad_context, [up_sum], [])
    grad_by_heads, down_grad = lax.optimization_barrier((grad_by_heads, down_grad))
    down_sum = sum_along_z(down_grad)
    grad_by_heads = out_scatter.corners(grad_by_heads)
    grad_qkv = attend_back(qkv, grad_by_heads, lse, flags, heads)
    grad_qkv = [part.reshape(SEQS * rows, 3 * heads * HEAD_DIM) for part in grad_qkv]
    grad_qkv = out_scatter.sides(grad_qkv)
    late_grad = out_scatter.ends(grad_qkv[1])
    qkv_grad = shared_heads(weight_grad((grad_qkv[0], late_grad), normed))
    qkv_sum = sum_along_z(qkv_grad)
    grad_normed_one, out_sum, sum_down = last_scatter(
        grad_qkv, qkv_full, out_scatter.result().astype(BF16), down_sum, tokens.shape
    )
    grad_normed_one = grad_normed_one.astype(F32)
    grad_start_norm, grad_gain_one, grad_bias_one = pull_one(grad_normed_one.reshape(rows, width))
    grad_start = grad_mid + grad_start_norm
    grad_table = jnp.einsum("tk,td->kd", onehot, grad_start, precision=HIGHEST_PRECISION)
    sums = jnp.concatenate(
        [
            grad_table,
            jnp.stack([grad_gain_one, grad_bias_one, grad_gain_two, grad_bias_two]),
        ],
        axis=0,
    )
    sums, (qkv_shard,) = sum_everywhere(sums, [qkv_sum])
    sum_qkv = jnp.transpose(qkv_shard)
    sum_up = jnp.transpose(up_shard)
    return (
        output,
        grad_start.reshape(tokens.shape),
        sums[:TYPES],
        sums[TYPES],
        sums[TYPES + 1],
        sum_qkv.astype(F32),
        out_sum.astype(F32),
        sums[TYPES + 2],
        sums[TYPES + 3],
        sum_up.astype(F32),
        sum_down.astype(F32),
    )


def solution(mesh):
    placed = (
        P("dp", "seq", None),
        P("dp", "seq"),
        P("dp"),
        P(None, "seq"),
        P("seq"),
        P("seq"),
        P("dp", "seq"),
        P("dp", "seq"),
        P("seq"),
        P("seq"),
        P("dp", "seq"),
        P("seq", "dp"),
        P("dp", "seq", None),
    )
    fits = mesh.shape["dp"] == 8 and mesh.shape["seq"] == 4
    return jax.shard_map(
        grouped_shards if fits else plain_shards,
        mesh=mesh,
        in_specs=placed,
        out_specs=(
            P("dp", "seq", None),
            P("dp", "seq", None),
            P(None, ("dp", "seq")),
            P(("dp", "seq")),
            P(("dp", "seq")),
            P("dp", "seq"),
            P("dp", "seq"),
            P(("dp", "seq")),
            P(("dp", "seq")),
            P("dp", "seq"),
            P("seq", "dp"),
        ),
        check_vma=False,
    )
```

```python
import math

import jax
import jax.numpy as jnp
from jax import lax
from jax.experimental import pallas as pl
from jax.experimental.pallas import tpu as pltpu
from jax.sharding import PartitionSpec as P

HEADS = 16
HEAD_DIM = 128
TYPES = 4


EPS = 1e-05
NEGATIVE = -1e30
HIGHEST_PRECISION = lax.Precision.HIGHEST


def layer_norm(hidden, gain, bias):
    average = jnp.mean(hidden, axis=-1, keepdims=True)
    centered = hidden - average
    variance = jnp.mean(centered * centered, axis=-1, keepdims=True)
    return centered * lax.rsqrt(variance + EPS) * gain + bias


def gelu_tanh(value):
    inner = math.sqrt(2.0 / math.pi) * (value + 0.044715 * value * value * value)
    return 0.5 * value * (1.0 + jnp.tanh(inner))


def key_allowed(first, count, full_len, view_flag):
    query_pos = first + jnp.arange(count, dtype=jnp.int32)
    key_pos = jnp.arange(full_len, dtype=jnp.int32)
    causal = key_pos[None, :] <= query_pos[:, None]
    seen = jnp.logical_or(view_flag == 1, key_pos % (full_len // 2) < full_len // 4)
    return jnp.logical_and(causal, seen[None, :])


def scores_of(query, keys, allowed, scale):
    plain = jnp.einsum("qhd,khd->hqk", query, keys, preferred_element_type=jnp.float32) * scale
    return jnp.where(allowed[None], plain, NEGATIVE)


def to_heads(values_in):
    return lax.all_to_all(values_in, "seq", split_axis=2, concat_axis=1, tiled=True)


def to_tokens(values_in):
    return lax.all_to_all(values_in, "seq", split_axis=1, concat_axis=2, tiled=True)


def plain_shards(
    tokens,
    token_types,
    view_mask,
    type_table,
    ln1_gain,
    ln1_bias,
    w_qkv,
    w_out,
    ln2_gain,
    ln2_bias,
    w_up,
    w_down,
    cotangent,
):
    seq_count, local_len, width = tokens.shape
    groups = lax.axis_size("seq")
    full_len = local_len * groups
    row_count = seq_count * local_len
    local_heads = HEADS // groups
    scale = 1.0 / math.sqrt(HEAD_DIM)
    block = min(512, full_len)
    f32 = jnp.float32
    bf16 = jnp.bfloat16
    out_part, table, gain_one, bias_one, gain_two, bias_two = (
        lax.all_gather(w_out, "seq", axis=1, tiled=True),
        lax.all_gather(type_table, "seq", axis=1, tiled=True),
        lax.all_gather(ln1_gain, "seq", axis=0, tiled=True),
        lax.all_gather(ln1_bias, "seq", axis=0, tiled=True),
        lax.all_gather(ln2_gain, "seq", axis=0, tiled=True),
        lax.all_gather(ln2_bias, "seq", axis=0, tiled=True),
    )
    qkv_full, out_full, up_full, down_full = (
        lax.all_gather(w_qkv, "dp", axis=0, tiled=True),
        lax.all_gather(out_part, "dp", axis=0, tiled=True),
        lax.all_gather(w_up, "dp", axis=0, tiled=True),
        lax.all_gather(w_down, "dp", axis=1, tiled=True),
    )
    onehot = (
        token_types.reshape(row_count)[:, None] == jnp.arange(TYPES, dtype=jnp.int32)[None, :]
    ).astype(f32)
    start_hidden = tokens.reshape(row_count, width).astype(f32) + jnp.dot(
        onehot, table.astype(f32), precision=HIGHEST_PRECISION
    )
    norm_one, pull_one = jax.vjp(
        layer_norm, start_hidden, gain_one.astype(f32), bias_one.astype(f32)
    )
    normed_one = norm_one.astype(bf16)
    normed_rows = lax.all_gather(
        normed_one.reshape(seq_count, local_len, width), "seq", axis=1, tiled=True
    )
    by_heads = jnp.einsum("std,de->ste", normed_rows, qkv_full, preferred_element_type=f32).astype(
        bf16
    )
    by_heads = by_heads.reshape(seq_count, full_len, local_heads, 3, HEAD_DIM)
    contexts = []
    kept_lse = []
    for index in range(seq_count):
        keys = by_heads[index, :, :, 1]
        values = by_heads[index, :, :, 2]
        context_blocks = []
        lse_blocks = []
        for first in range(0, full_len, block):
            query = by_heads[index, first : first + block, :, 0]
            allowed = key_allowed(first, block, full_len, view_mask[index])
            scores = scores_of(query, keys, allowed, scale)
            top = jnp.max(scores, axis=-1, keepdims=True)
            expd = jnp.exp(scores - top)
            total = jnp.sum(expd, axis=-1, keepdims=True)
            probs_low = (expd / total).astype(bf16)
            context_blocks.append(
                jnp.einsum("hqk,khd->qhd", probs_low, values, preferred_element_type=f32).astype(
                    bf16
                )
            )
            lse_blocks.append(top + jnp.log(total))
        contexts.append(jnp.concatenate(context_blocks, axis=0))
        kept_lse.append(lse_blocks)
    context_heads = jnp.stack(contexts)
    context_rows = to_tokens(context_heads).reshape(row_count, width)
    mid_hidden = start_hidden + jnp.dot(context_rows, out_full, preferred_element_type=f32)
    norm_two, pull_two = jax.vjp(layer_norm, mid_hidden, gain_two.astype(f32), bias_two.astype(f32))
    normed_two = norm_two.astype(bf16)
    cot_rows = cotangent.reshape(row_count, width)
    ffn_input, grad_rows = (
        lax.all_gather(normed_two, "seq", axis=0, tiled=True),
        lax.all_gather(cot_rows, "seq", axis=0, tiled=True),
    )
    up_value = jnp.dot(ffn_input, up_full, preferred_element_type=f32)
    activated, gelu_pull = jax.vjp(gelu_tanh, up_value)
    activated_low = activated.astype(bf16)
    piece = activated_low
    ffn_out = lax.psum_scatter(
        jnp.dot(piece, down_full, preferred_element_type=f32).astype(jnp.bfloat16),
        "seq",
        scatter_dimension=0,
        tiled=True,
    ).astype(jnp.float32)
    output = (mid_hidden + ffn_out).astype(bf16).reshape(seq_count, local_len, width)
    grad_down = jnp.einsum("ti,td->id", activated_low, grad_rows, preferred_element_type=f32)
    grad_act = jnp.einsum("td,id->ti", grad_rows, down_full, preferred_element_type=f32)
    grad_up_value = gelu_pull(grad_act)[0].astype(bf16)
    grad_up = jnp.einsum("td,ti->di", ffn_input, grad_up_value, preferred_element_type=f32)
    piece = grad_up_value
    grad_normed_two = lax.psum_scatter(
        jnp.einsum("ti,di->td", piece, up_full, preferred_element_type=f32).astype(jnp.bfloat16),
        "seq",
        scatter_dimension=0,
        tiled=True,
    ).astype(jnp.float32)
    grad_mid_norm, grad_gain_two, grad_bias_two = pull_two(grad_normed_two)
    grad_mid = cot_rows.astype(f32) + grad_mid_norm
    grad_mid_low = grad_mid.astype(bf16)
    grad_out_weight = jnp.einsum(
        "td,te->de", context_rows, grad_mid_low, preferred_element_type=f32
    )
    grad_context = jnp.einsum(
        "te,de->td", grad_mid_low, out_full, preferred_element_type=f32
    ).astype(bf16)
    grad_context = grad_context.reshape(seq_count, local_len, HEADS, HEAD_DIM)
    grad_by_heads = to_heads(grad_context)
    grad_parts = []
    for index in range(seq_count):
        keys = by_heads[index, :, :, 1]
        values = by_heads[index, :, :, 2]
        grad_keys = jnp.zeros(keys.shape, f32)
        grad_values = jnp.zeros(values.shape, f32)
        grad_query_blocks = []
        for number, first in enumerate(range(0, full_len, block)):
            query = by_heads[index, first : first + block, :, 0]
            allowed = key_allowed(first, block, full_len, view_mask[index])
            scores = scores_of(query, keys, allowed, scale)
            probs = jnp.exp(scores - kept_lse[index][number])
            probs_low = probs.astype(bf16)
            grad_block = grad_by_heads[index, first : first + block]
            grad_values = grad_values + jnp.einsum(
                "hqk,qhd->khd", probs_low, grad_block, preferred_element_type=f32
            )
            grad_probs = jnp.einsum("qhd,khd->hqk", grad_block, values, preferred_element_type=f32)
            weighted = jnp.sum(probs * grad_probs, axis=-1, keepdims=True)
            grad_scores = (probs * (grad_probs - weighted)).astype(bf16)
            grad_query_blocks.append(
                jnp.einsum("hqk,khd->qhd", grad_scores, keys, preferred_element_type=f32) * scale
            )
            grad_keys = (
                grad_keys
                + jnp.einsum("hqk,qhd->khd", grad_scores, query, preferred_element_type=f32) * scale
            )
        grad_parts.append(
            jnp.stack([jnp.concatenate(grad_query_blocks, axis=0), grad_keys, grad_values], axis=2)
        )
    grad_projected = jnp.stack(grad_parts).astype(bf16)
    columns = qkv_full.shape[1]
    grad_flat = grad_projected.reshape(seq_count, full_len, columns)
    grad_qkv_weight = jnp.einsum("std,ste->de", normed_rows, grad_flat, preferred_element_type=f32)
    position_major = jnp.transpose(grad_flat, (1, 0, 2)).reshape(full_len * seq_count, columns)
    piece = position_major
    summed_rows = lax.psum_scatter(
        jnp.einsum("te,de->td", piece, qkv_full, preferred_element_type=f32).astype(jnp.bfloat16),
        "seq",
        scatter_dimension=0,
        tiled=True,
    ).astype(jnp.float32)
    grad_normed_one = jnp.transpose(
        summed_rows.reshape(local_len, seq_count, width), (1, 0, 2)
    ).reshape(row_count, width)
    grad_start_norm, grad_gain_one, grad_bias_one = pull_one(grad_normed_one)
    grad_start = grad_mid + grad_start_norm
    input_grad = grad_start.reshape(seq_count, local_len, width)
    grad_table = jnp.einsum("tk,td->kd", onehot, grad_start, precision=HIGHEST_PRECISION)
    (
        sum_qkv,
        sum_out,
        sum_up,
        sum_down,
        sum_table,
        sum_gain_one,
        sum_bias_one,
        sum_gain_two,
        sum_bias_two,
    ) = (
        lax.psum_scatter(
            grad_qkv_weight.astype(jnp.bfloat16), "dp", scatter_dimension=0, tiled=True
        ).astype(jnp.float32),
        lax.psum_scatter(
            grad_out_weight.astype(jnp.bfloat16), "dp", scatter_dimension=0, tiled=True
        ).astype(jnp.float32),
        lax.psum_scatter(
            grad_up.astype(jnp.bfloat16), "dp", scatter_dimension=0, tiled=True
        ).astype(jnp.float32),
        lax.psum_scatter(
            grad_down.astype(jnp.bfloat16), "dp", scatter_dimension=1, tiled=True
        ).astype(jnp.float32),
        lax.psum_scatter(
            grad_table.astype(jnp.bfloat16), "dp", scatter_dimension=1, tiled=True
        ).astype(jnp.float32),
        lax.psum_scatter(
            grad_gain_one.astype(jnp.bfloat16), "dp", scatter_dimension=0, tiled=True
        ).astype(jnp.float32),
        lax.psum_scatter(
            grad_bias_one.astype(jnp.bfloat16), "dp", scatter_dimension=0, tiled=True
        ).astype(jnp.float32),
        lax.psum_scatter(
            grad_gain_two.astype(jnp.bfloat16), "dp", scatter_dimension=0, tiled=True
        ).astype(jnp.float32),
        lax.psum_scatter(
            grad_bias_two.astype(jnp.bfloat16), "dp", scatter_dimension=0, tiled=True
        ).astype(jnp.float32),
    )
    final_out, final_table, final_gain_one, final_bias_one, final_gain_two, final_bias_two = (
        lax.psum_scatter(
            sum_out.astype(jnp.bfloat16), "seq", scatter_dimension=1, tiled=True
        ).astype(jnp.float32),
        lax.psum_scatter(
            sum_table.astype(jnp.bfloat16), "seq", scatter_dimension=1, tiled=True
        ).astype(jnp.float32),
        lax.psum_scatter(
            sum_gain_one.astype(jnp.bfloat16), "seq", scatter_dimension=0, tiled=True
        ).astype(jnp.float32),
        lax.psum_scatter(
            sum_bias_one.astype(jnp.bfloat16), "seq", scatter_dimension=0, tiled=True
        ).astype(jnp.float32),
        lax.psum_scatter(
            sum_gain_two.astype(jnp.bfloat16), "seq", scatter_dimension=0, tiled=True
        ).astype(jnp.float32),
        lax.psum_scatter(
            sum_bias_two.astype(jnp.bfloat16), "seq", scatter_dimension=0, tiled=True
        ).astype(jnp.float32),
    )
    return (
        output,
        input_grad,
        final_table,
        final_gain_one,
        final_bias_one,
        sum_qkv,
        final_out,
        final_gain_two,
        final_bias_two,
        sum_up,
        sum_down,
    )


PLANE = 8
QUAD = 4
F32 = jnp.float32
BF16 = jnp.bfloat16
MESH_ID = pl.DeviceIdType.MESH
CORE, X_WAY, Y_WAY = 1, 2, 4
FAR_FIRST = (6, 7, 2, 3, 4, 5, 1)


def swap(value, mask):
    dp = lax.axis_size("dp")
    return lax.ppermute(value, "dp", [(i, i ^ mask) for i in range(dp)])


def after(value, *earlier):
    return lax.optimization_barrier((value, earlier))[0]


def at_plane(d, z):
    return dict(device_id=(d, z), device_id_type=MESH_ID)


class Moves:
    def __init__(self, send_sem, recv_sem, local_sem=None):
        self.sems = (send_sem, recv_sem, local_sem)
        self.count = [0, 0]
        self.open = []
        self.done = []

    def far(self, source, target, d, z, sends=None, receives=None, lands=None, own=None):
        number = self.count[0] if own is None else own
        self.count[0] += own is None

        def copy(landing):
            return pltpu.make_async_remote_copy(
                src_ref=source,
                dst_ref=target,
                send_sem=self.sems[0].at[number],
                recv_sem=self.sems[1].at[landing],
                **at_plane(d, z),
            )

        out = copy(number if lands is None else lands)
        when(sends, out.start)
        move = [(out, copy(number)), sends, receives, False]
        self.open.append(move)
        return move

    def here(self, source, target, sends=None):
        number = self.count[1]
        self.count[1] += 1
        copy = pltpu.make_async_copy(source, target, self.sems[2].at[number])
        when(sends, copy.start)
        move = [copy, sends, None, False]
        self.open.append(move)
        return move

    def landed(self, move):
        copy, sends, receives, done = move
        assert not done
        move[3] = True
        if isinstance(copy, tuple):
            when(receives, copy[1].wait_recv)
        else:
            when(sends, copy.wait)

    def sent(self, move):
        when(move[1], move[0][0].wait_send)
        self.done.append(id(move))

    def finish(self):
        for move in self.open:
            if not move[3]:
                self.landed(move)
            if isinstance(move[0], tuple) and id(move) not in self.done:
                self.sent(move)


def when(condition, do):
    if condition is None:
        do()
    else:
        pl.when(condition)(do)


def meet_all(masks, lines=True, peers=False):
    d = lax.axis_index("dp")
    z = lax.axis_index("seq")
    groups = lax.axis_size("seq")
    barrier = pltpu.get_barrier_semaphore()
    count = len(masks)
    for mask in masks:
        pl.semaphore_signal(barrier, inc=1, **at_plane(d ^ mask, z))
    if lines:
        count = count + groups - 1
        for step in range(1, groups):
            pl.semaphore_signal(barrier, inc=1, **at_plane(d, (z + step) % groups))
    if peers:
        for number in range(2):
            to_d, to_z, itself = peer_of(number)
            away = jnp.logical_not(itself)

            def signal(to_d=to_d, to_z=to_z):
                pl.semaphore_signal(barrier, inc=1, **at_plane(to_d, to_z))

            when(away, signal)
            count = count + jnp.where(itself, 0, 1)
    pl.semaphore_wait(barrier, count)


def peer_of(number):
    d = lax.axis_index("dp")
    z = lax.axis_index("seq")
    core = d & 1
    to_d = (d - core) + (z >> 1)
    to_z = 2 * core + number
    return to_d, to_z, jnp.logical_and(to_d == d, to_z == z)


def exchange_along_z(moves, number, source, target, base=None):
    z = lax.axis_index("seq")
    own = None if base is None else base + number
    base = moves.count[0] - number if base is None else base
    to_d, to_z, itself = peer_of(number)
    away = jnp.logical_not(itself)
    far = moves.far(source, target(z & 1), to_d, to_z, away, away, base + (z & 1), own)
    near = moves.here(source, target(z & 1), itself)
    return far, near


def all_landed(moves, landing):
    for move in landing:
        moves.landed(move)


def intake_kernel(small_ref, mark_ref, whole_ref, marks_ref, *sems):
    moves = Moves(*sems)
    d = lax.axis_index("dp")
    z = lax.axis_index("seq")
    groups = lax.axis_size("seq")
    meet_all(range(1, PLANE))
    moves.here(small_ref, whole_ref.at[z])
    for step in range(1, groups):
        moves.far(small_ref, whole_ref.at[z], d, (z + step) % groups)
    moves.here(mark_ref, marks_ref.at[0])
    for mask in range(1, PLANE):
        moves.far(mark_ref, marks_ref.at[mask], d ^ mask, z)
    moves.finish()


def spread_columns(moves, shard, half):
    d = lax.axis_index("dp")
    z = lax.axis_index("seq")
    part, width = shard.shape[0] // PLANE, shard.shape[1]
    target = half.at[:, pl.ds(pl.multiple_of(d * width, 128), width)]

    def rows(mask):
        return shard.at[pl.ds(pl.multiple_of((d ^ mask) * part, 64), part)]

    return [moves.here(rows(0), target)] + [
        moves.far(rows(mask), target, d ^ mask, z) for mask in FAR_FIRST
    ]


def kernel_call(
    kernel, inputs, outputs, far, here, number, name, traffic, spaces=None, scratch=(), late=()
):
    count = len(inputs)

    def body(*refs):
        kernel(*refs[:count], *refs[count + len(late) :])

    return pl.pallas_call(
        body,
        out_shape=outputs,
        in_specs=[pl.BlockSpec(memory_space=space) for space in spaces or [pltpu.VMEM] * count]
        + [pl.BlockSpec(memory_space=pl.ANY)] * len(late),
        out_specs=[pl.BlockSpec(memory_space=pl.ANY)] * len(outputs),
        scratch_shapes=[
            *scratch,
            pltpu.SemaphoreType.DMA((far,)),
            pltpu.SemaphoreType.DMA((far,)),
            pltpu.SemaphoreType.DMA((here,)),
        ],
        compiler_params=pltpu.CompilerParams(
            collective_id=number, has_side_effects=True, vmem_limit_bytes=56 * 1024 * 1024
        ),
        cost_estimate=pl.CostEstimate(
            flops=0, bytes_accessed=traffic * 3 * 1024 * 1024, transcendentals=0
        ),
        name=name,
    )(*inputs, *late)


def shaped(*shape):
    return jax.ShapeDtypeStruct(shape, BF16)


def intake(small, mark):
    groups = lax.axis_size("seq")
    return kernel_call(
        intake_kernel,
        [small, mark],
        [
            shaped(groups, *small.shape),
            jax.ShapeDtypeStruct((PLANE,) + mark.shape, mark.dtype),
        ],
        groups - 1 + PLANE - 1,
        2,
        1,
        "intake",
        10,
    )


def gather_rows(moves, rows_ref, chips_ref, others_ref, ready=None, pieces=2, passed=None):
    d = lax.axis_index("dp")
    z = lax.axis_index("seq")
    size = chips_ref.shape[1] // pieces
    parts = [pl.ds(number * size, size) for number in range(pieces)]
    order = [i + j for i in range(pieces // 2) for j in (0, pieces // 2)]

    def far(source, target, mask):
        return moves.far(source, target, d ^ mask, z)

    def keep(chip, move):
        if passed is not None:
            passed.setdefault(chip, []).append(move)

    if ready is None:
        moves.here(rows_ref, chips_ref.at[0])
    over_x = {}
    over_y = {}
    for number in order:
        part = parts[number]
        if ready is None:
            source = rows_ref.at[part]
        else:
            ready(number)
            source = chips_ref.at[0, part]
        over_x[number] = far(source, chips_ref.at[1, part], X_WAY)
        over_y[number] = far(source, chips_ref.at[2, part], Y_WAY)
        keep(0, far(source, others_ref.at[0, part], CORE))

    def pass_on(chip, number):
        part = parts[number]
        keep(chip, far(chips_ref.at[chip, part], others_ref.at[chip, part], CORE))

    corner = {}
    for number in order:
        yield
        part = parts[number]
        first = number < pieces // 2
        via, chip, mask = (over_y, 2, X_WAY) if first else (over_x, 1, Y_WAY)
        moves.landed(via[number])
        corner[number] = far(chips_ref.at[chip, part], chips_ref.at[3, part], mask)
        pass_on(chip, number)
        moves.landed((over_x if first else over_y)[number])
        pass_on(3 - chip, number)
    yield
    for number in order:
        moves.landed(corner[number])
        pass_on(3, number)


GATHER_COPIES = 14
FIRST_PIECES = 4


def gather_along_z(moves, shard_ref, place, target):
    d = lax.axis_index("dp")
    z = lax.axis_index("seq")
    own = moves.here(shard_ref, target.at[place(z)])
    arrivals = []
    for step in (2, -2, 1, -1):
        to, source = z + step, z - step
        inside = jnp.logical_and(to >= 0, to < 4)
        comes = jnp.logical_and(source >= 0, source < 4)
        arrivals.append(
            moves.far(shard_ref, target.at[place(z)], d, jnp.clip(to, 0, 3), inside, comes)
        )
    yield
    for arrival in arrivals:
        moves.landed(arrival)
    for end, via, to in ((0, 2, 3), (3, 1, 0)):
        arrivals.append(
            moves.far(target.at[place(end)], target.at[place(end)], d, to, z == via, z == to)
        )
    yield
    for arrival in arrivals[4:] + [own]:
        moves.landed(arrival)


Z_COPIES = 6


def first_kernel(rows_ref, qkv_ref, up_ref, down_ref, *refs):
    chips, others, heads, up_half, down_half, qkv_half = refs[:6]
    moves = Moves(*refs[6:])
    d = lax.axis_index("dp")
    core = d & 1
    half = rows_ref.shape[1]
    meet_all(range(1, PLANE), peers=True)
    size = 2 * half // FIRST_PIECES
    landing = {}
    for piece in range(FIRST_PIECES // 2):
        for number in range(2):
            landing[number * (FIRST_PIECES // 2) + piece] = exchange_along_z(
                moves,
                number,
                rows_ref.at[number, pl.ds(piece * size, size)],
                lambda at: chips.at[
                    0, pl.ds(pl.multiple_of(at * half + piece * size, size), size)
                ],
            )
    spread = spread_columns(moves, qkv_ref, qkv_half)
    spread_columns(moves, up_ref, up_half)
    spread_columns(moves, down_ref, down_half)
    all_landed(moves, spread)

    def place(at):
        own = (at >> 1) == core
        return jnp.where(own, (at & 1) * 2 + core, 4 + (at & 1))

    qkv = gather_along_z(moves, qkv_half, place, heads)
    next(qkv)
    rows = gather_rows(
        moves,
        None,
        chips,
        others,
        lambda number: all_landed(moves, landing[number]),
        FIRST_PIECES,
    )
    for _ in range(FIRST_PIECES):
        next(rows)
    next(qkv)
    next(rows)
    next(qkv, None)
    z = lax.axis_index("seq")
    for number in range(2):
        moves.far(heads.at[4 + number], heads.at[number * 2 + core], d ^ CORE, z)
    next(rows, None)
    moves.finish()


def first_gather(rows, qkv_shard, up_shard, down_shard, late):
    seqs, half, width = rows.shape
    part = qkv_shard.shape[0] // PLANE
    return kernel_call(
        first_kernel,
        [rows, qkv_shard, up_shard, down_shard],
        [
            shaped(4, seqs * half, width),
            shaped(4, seqs * half, width),
            shaped(6, part, width),
            shaped(up_shard.shape[0] // PLANE, width),
            shaped(down_shard.shape[0] // PLANE, width),
            shaped(part, width),
        ],
        7 * FIRST_PIECES + Z_COPIES + FIRST_PIECES + 2 + 3 * (PLANE - 1),
        4 + FIRST_PIECES,
        2,
        "first_gather",
        110,
        late=late,
    )[:5]


def gather_kernel(
    rows_ref,
    held_ref,
    weights_ref,
    chips,
    others,
    held_others,
    chips_out,
    others_out,
    weights,
    blocks_held,
    results_held,
    weights_sem,
    blocks_sem,
    results_sem,
    *sems,
):
    moves = Moves(*sems)
    d = lax.axis_index("dp")
    z = lax.axis_index("seq")
    count = rows_ref.shape[0]
    blocks = Slots(blocks_held, blocks_sem)
    results = Slots(results_held, results_sem)
    weights_in = pltpu.make_async_copy(weights_ref, weights, weights_sem)
    weights_in.start()
    meet_all((CORE, X_WAY, Y_WAY), lines=False)
    passed = {}
    done = []

    def multiply(source, target, chip, block=None):
        slot = len(done) % 2
        done.append(chip)
        if block is None:
            blocks.load(slot, source.at[chip])
            block = blocks.wait(slot)
        result = results.wait(slot)

        @pl.loop(0, count // 256)
        def _(i):
            at = pl.ds(pl.multiple_of(i * 256, 256), 256)
            result[at, :] = lax.dot_general(
                block[at, :], weights[...], (((1,), (1,)), ((), ())), preferred_element_type=F32
            )

        results.store(slot, target.at[pl.ds(chip * count, count)])

    def multiply_others(chip):
        all_landed(moves, passed[chip])
        multiply(others, others_out, chip)

    steps = gather_rows(moves, rows_ref, chips, others, passed=passed)
    next(steps)
    moves.far(held_ref, held_others, d ^ CORE, z)
    weights_in.wait()
    multiply(None, chips_out, 0, rows_ref)
    multiply_others(0)
    next(steps)
    next(steps)
    for chip in (1, 2):
        multiply(chips, chips_out, chip)
    for chip in (1, 2):
        multiply_others(chip)
    next(steps, None)
    multiply(chips, chips_out, 3)
    multiply_others(3)
    for slot in range(2):
        results.wait(slot)
    moves.finish()


def gather_multiply(rows, held, weights, number):
    count, width = rows.shape
    units = weights.shape[0]
    product = jax.ShapeDtypeStruct((4 * count, units), F32)
    chips, others, held_others, chips_out, others_out = kernel_call(
        gather_kernel,
        [rows, held, weights],
        [shaped(4, count, width), shaped(4, count, width), shaped(*held.shape), product, product],
        GATHER_COPIES + 1,
        1,
        number,
        "gather_multiply",
        80,
        [pltpu.VMEM, pl.ANY, pl.ANY],
        [
            pltpu.VMEM((units, width), BF16),
            pltpu.VMEM((2, count, width), BF16),
            pltpu.VMEM((2, count, units), F32),
            pltpu.SemaphoreType.DMA(()),
            pltpu.SemaphoreType.DMA((2,)),
            pltpu.SemaphoreType.DMA((2,)),
        ],
    )
    rows = [part.reshape(4 * count, width) for part in (chips, others)]
    return rows, held_others, (chips_out, others_out)


def add_rows(target, start, sources, count, step=64):
    @pl.loop(0, count // step)
    def _(i):
        total = None
        for ref, offset in sources:
            piece = ref[pl.ds(pl.multiple_of(offset + i * step, step), step), :].astype(F32)
            total = piece if total is None else total + piece
        target[pl.ds(pl.multiple_of(start + i * step, step), step), :] = total.astype(target.dtype)


CHIP_ORDER = (3, 1, 2, 0)


def scatter_rows(moves, fill, last, own, got, far, near, done):
    d = lax.axis_index("dp")
    z = lax.axis_index("seq")
    half = own.shape[1] // 2
    first, second = pl.ds(0, half), pl.ds(half, half)

    def send_to(source, target, mask):
        return moves.far(source, target, d ^ mask, z)

    ready = fill(send_to)
    yield
    ready(0)
    add_rows(own.at[0], 0, [(own.at[0], 0), (got.at[0], 0)], half)
    to_x = send_to(own.at[0, first], far.at[0], X_WAY)
    add_rows(own.at[0], half, [(own.at[0], half), (got.at[0], half)], half)
    to_y = send_to(own.at[0, second], far.at[1], Y_WAY)
    ready(1)
    add_rows(own.at[1], 0, [(own.at[1], 0), (got.at[1], 0)], half)
    x_first = send_to(own.at[1, first], near.at[0, first], X_WAY)
    ready(2)
    yield
    moves.landed(to_x)
    add_rows(own.at[2], 0, [(own.at[2], 0), (got.at[2], 0), (far.at[0], 0)], half)
    y_first = send_to(own.at[2, first], near.at[1, first], Y_WAY)
    add_rows(own.at[2], half, [(own.at[2], half), (got.at[2], half)], half)
    y_second = send_to(own.at[2, second], near.at[1, second], Y_WAY)
    moves.landed(to_y)
    add_rows(own.at[1], half, [(own.at[1], half), (got.at[1], half), (far.at[1], 0)], half)
    x_second = send_to(own.at[1, second], near.at[0, second], X_WAY)
    ready(3)
    yield
    for number, arrivals in ((0, (x_first, y_first)), (1, (x_second, y_second))):
        all_landed(moves, arrivals)
        start = number * half
        add_rows(
            done,
            start,
            [(own.at[3], start), (got.at[3], start), (near.at[0], start), (near.at[1], start)],
            half,
        )
        last(number)
    for move in (to_x, to_y, x_first, x_second, y_first, y_second):
        moves.sent(move)


SCATTER_COPIES = 10


def sum_rows(target, sources, step=64):
    @pl.loop(0, target.shape[0] // step)
    def _(i):
        at = pl.ds(pl.multiple_of(i * step, step), step)
        total = sources[0][at, :].astype(F32)
        for ref in sources[1:]:
            total = total + ref[at, :].astype(F32)
        target[at, :] = total.astype(target.dtype)


def sum_along_line(moves, piece, got, target):
    d = lax.axis_index("dp")
    z = lax.axis_index("seq")
    groups = lax.axis_size("seq")
    arrivals = []
    for step in range(1, groups):
        to = (z + step) % groups
        arrivals.append(moves.far(piece(to), got.at[step - 1], d, to))
    yield
    all_landed(moves, arrivals)
    sum_rows(target, [piece(z)] + [got.at[step] for step in range(groups - 1)])


class Slots:
    def __init__(self, places, sems):
        self.places = places
        self.sems = sems
        self.copies = {}

    def load(self, slot, source):
        self.copies[slot] = pltpu.make_async_copy(source, self.places.at[slot], self.sems.at[slot])
        self.copies[slot].start()

    def store(self, slot, target):
        self.copies[slot] = pltpu.make_async_copy(self.places.at[slot], target, self.sems.at[slot])
        self.copies[slot].start()

    def wait(self, slot):
        if slot in self.copies:
            self.copies.pop(slot).wait()
        return self.places.at[slot]


def scatter_products(
    moves, sources, held, rows_in, weights_in, stage, side, last, follow=None, also=None
):
    count = held[0].shape[1]
    blocks = [(1, c) for c in CHIP_ORDER] + [(0, c) for c in CHIP_ORDER]

    def fill(send_to):
        def load(number):
            which, c = blocks[number]
            rows_in.load(number % 2, sources[which].at[pl.ds(c * count, count)])

        load(0)
        matrix = weights_in.wait(side)
        from_core = []
        for number, (which, c) in enumerate(blocks):
            if number + 1 < len(blocks):
                load(number + 1)
            if which == 1 and number >= 2:
                moves.sent(from_core[number - 2])
            place = stage.at[number % 2] if which == 1 else held[0].at[number - 4]
            block = rows_in.wait(number % 2)

            @pl.loop(0, count // 256)
            def _(i):
                at = pl.ds(pl.multiple_of(i * 256, 256), 256)
                place[at, :] = jnp.dot(
                    block[at, :], matrix[...], preferred_element_type=F32
                ).astype(BF16)
                if also is not None:
                    also(which, c, block, i)

            if which == 1:
                from_core.append(send_to(place, held[1].at[number], CORE))
        if follow is not None:
            follow()
        moves.sent(from_core[2])
        moves.sent(from_core[3])
        return lambda i: moves.landed(from_core[i])

    return scatter_rows(moves, fill, last, *held)


def last_kernel(
    chips_ref,
    others_ref,
    weights_ref,
    out_ref,
    held_ref,
    grad_ref,
    out_sum_ref,
    shard_ref,
    own,
    got,
    far,
    near,
    done,
    stage,
    rows_held,
    weights_held,
    out_got,
    out_sum,
    rows_sem,
    weights_sem,
    *sems,
):
    moves = Moves(*sems)
    rows_in = Slots(rows_held, rows_sem)
    weights_in = Slots(weights_held, weights_sem)
    columns = out_sum.shape[1]
    half, width = own.shape[2] // 2, own.shape[3]
    for side in range(2):
        weights_in.load(side, weights_ref.at[:, pl.ds(side * width, width)])
    meet_all(range(1, PLANE), peers=True)
    out = sum_along_line(
        moves,
        lambda at: out_ref.at[:, pl.ds(pl.multiple_of(at * columns, 128), columns)],
        out_got,
        out_sum,
    )
    next(out)

    def scatter(side):
        base = []

        def last(number):
            if number == 0:
                base.append(moves.count[0])
                moves.count[0] += 2
            exchange_along_z(
                moves,
                number,
                done.at[side, pl.ds(number * half, half)],
                lambda at: grad_ref.at[at, :, pl.ds(side * width, width)],
                base[0],
            )

        held = [ref.at[side] for ref in (own, got, far, near, done)]
        return scatter_products(
            moves, (chips_ref, others_ref), held, rows_in, weights_in, stage, side, last
        )

    low, high = scatter(0), scatter(1)
    next(low)
    next(low)
    next(high)
    next(low)
    next(high)
    next(out, None)
    moves.here(out_sum, out_sum_ref)
    next(low, None)
    next(high)
    unite_columns(moves, held_ref, shard_ref)
    next(high, None)
    moves.finish()


def last_scatter(parts, weights, out_grad, held, shape):
    total, units = parts[0].shape
    width = weights.shape[1]
    count, half = total // 4, width // 2
    groups = lax.axis_size("seq")
    rows, columns = out_grad.shape[0], width // groups
    sizes = ((4, count, half), (4, count, half), (2, count // 2, half), (2, count, half))
    return kernel_call(
        last_kernel,
        [*parts, weights, out_grad, held],
        [
            shaped(*shape),
            shaped(rows, columns),
            shaped(held.shape[0] * PLANE, width // PLANE),
        ],
        2 * SCATTER_COPIES + 4 + groups - 1 + PLANE - 1,
        6,
        7,
        "last_scatter",
        100,
        [pl.ANY, pl.ANY, pl.ANY, pltpu.VMEM, pltpu.VMEM],
        [pltpu.VMEM((2,) + size, BF16) for size in sizes + ((count, half),)]
        + [
            pltpu.VMEM((2, count, half), BF16),
            pltpu.VMEM((2, count, units), BF16),
            pltpu.VMEM((2, units, half), BF16),
            pltpu.VMEM((groups - 1, rows, columns), BF16),
            pltpu.VMEM((rows, columns), BF16),
            pltpu.SemaphoreType.DMA((2,)),
            pltpu.SemaphoreType.DMA((2,)),
        ],
    )


def feed_kernel(
    grad_chips,
    grad_others,
    act_chips,
    act_others,
    up_ref,
    down_ref,
    rows_chips,
    rows_others,
    cot_chips,
    cot_others,
    norm_ref,
    out_ref,
    up_parts_ref,
    down_grad_ref,
    left,
    rows_held,
    weights_held,
    own,
    got,
    far,
    near,
    done,
    stage,
    stream_held,
    result_held,
    rows_sem,
    weights_sem,
    stream_sem,
    result_sem,
    free_sem,
    send_sem,
    recv_sem,
    local_sem,
):
    moves = Moves(send_sem, recv_sem, local_sem)
    d = lax.axis_index("dp")
    z = lax.axis_index("seq")
    rows_in = Slots(rows_held, rows_sem)
    weights_in = Slots(weights_held, weights_sem)
    stream = Slots(stream_held, stream_sem)
    results = Slots(result_held, result_sem)
    count, width = own.shape[2], own.shape[3]
    columns = stream_held.shape[2]
    def load_weights(weights, side):
        weights_in.load(side, weights.at[:, pl.ds(side * width, width)])

    def scatter(sources, side, target, follow, keep):
        held = [ref.at[side] for ref in (own, got, far, near, done)]

        def transposed(which, c, block, i):
            tokens = pl.ds(pl.multiple_of(c * count + i * 256, 256), 256)
            for unit in range(0, block.shape[1], 256):
                left[which, unit : unit + 256, tokens] = jnp.transpose(
                    block[pl.ds(pl.multiple_of(i * 256, 256), 256), unit : unit + 256]
                )

        def last(number):
            if number == 1:
                moves.here(held[4], target.at[:, pl.ds(side * width, width)])

        return scatter_products(
            moves,
            sources,
            held,
            rows_in,
            weights_in,
            stage,
            side,
            last,
            follow,
            transposed if keep else None,
        )

    def end(work, side):
        next(work, None)
        all_landed(moves, moves.open[-1:])
        for mask in (CORE, X_WAY, Y_WAY):
            pl.semaphore_signal(free_sem.at[side], inc=1, **at_plane(d ^ mask, z))

    def weight_grad(rights, place, base, slots):
        chunks = rights[0].shape[1] // columns

        def load(chunk):
            for side in range(2):
                stream.load(
                    2 * (chunk % 2) + side, rights[side].at[:, pl.ds(chunk * columns, columns)]
                )

        load(0)
        for chunk in range(chunks):
            if chunk + 1 < chunks:
                load(chunk + 1)
            first, second = (stream.wait(2 * (chunk % 2) + side) for side in range(2))
            slot = base + chunk % slots
            result = results.wait(slot)

            @pl.loop(0, result.shape[0] // 256)
            def _(i):
                at = pl.ds(pl.multiple_of(i * 256, 256), 256)
                total = jnp.dot(left[0, at, :], first[...], preferred_element_type=F32)
                total += jnp.dot(left[1, at, :], second[...], preferred_element_type=F32)
                result[at, :] = total.astype(BF16)

            place(slot, result, chunk)
            yield

    groups = lax.axis_size("seq")
    part = up_parts_ref.shape[1]

    def to_line(slot, result, chunk):
        target = up_parts_ref.at[:, :, pl.ds(chunk * columns, columns)]
        for step in range(1, groups):
            to = (z + step) % groups
            piece = result.at[pl.ds(pl.multiple_of(to * part, 256), part)]
            moves.far(piece, target.at[step], d, to)
        piece = result.at[pl.ds(pl.multiple_of(z * part, 256), part)]
        results.copies[slot] = pltpu.make_async_copy(piece, target.at[0], results.sems.at[slot])
        results.copies[slot].start()

    def to_memory(slot, result, chunk):
        results.store(slot, down_grad_ref.at[:, pl.ds(chunk * columns, columns)])

    def steps(work, number):
        for _ in range(number):
            next(work, None)

    nothing = lambda: None
    load_weights(up_ref, 0)
    load_weights(up_ref, 1)
    meet_all((CORE, X_WAY, Y_WAY))
    grads = (grad_chips, grad_others)
    acts = (act_chips, act_others)
    norm_low = scatter(grads, 0, norm_ref, lambda: load_weights(down_ref, 0), True)
    norm_high = scatter(grads, 1, norm_ref, lambda: load_weights(down_ref, 1), False)
    out_low = scatter(acts, 0, out_ref, nothing, False)
    out_high = scatter(acts, 1, out_ref, nothing, True)
    line_slots = result_held.shape[0] - 2
    up_work = weight_grad((rows_chips, rows_others), to_line, 0, line_slots)
    down_work = weight_grad((cot_chips, cot_others), to_memory, line_slots, 2)
    next(norm_low)
    next(norm_low)
    steps(up_work, 3)
    next(norm_low)
    next(norm_high)
    next(norm_high)
    steps(up_work, 3)
    end(norm_low, 0)
    next(norm_high)
    pl.semaphore_wait(free_sem.at[0], 3)
    next(out_low)
    next(out_low)
    steps(up_work, 3)
    end(norm_high, 1)
    next(out_low)
    pl.semaphore_wait(free_sem.at[1], 3)
    next(out_high)
    next(out_high)
    steps(down_work, 4)
    next(out_low, None)
    next(out_high)
    steps(down_work, 5)
    next(out_high, None)
    for slot in range(line_slots + 2):
        results.wait(slot)
    moves.finish()


def feed_back(grads, acts, up_full, down_full, rows, cots):
    total, units = grads[0].shape
    width = up_full.shape[1]
    count = total // 4
    half = width // 2
    columns = 256
    copies = 4 * SCATTER_COPIES + 3 * width // columns
    groups = lax.axis_size("seq")
    ins = [*grads, *acts, up_full, down_full, *rows, *cots]
    return pl.pallas_call(
        feed_kernel,
        out_shape=[shaped(count, width)] * 2
        + [shaped(groups, units // groups, width), shaped(units, width)],
        in_specs=[pl.BlockSpec(memory_space=pl.ANY)] * len(ins),
        out_specs=[pl.BlockSpec(memory_space=pl.ANY)] * 4,
        scratch_shapes=[
            pltpu.VMEM((2, units, total), BF16),
            pltpu.VMEM((2, count, units), BF16),
            pltpu.VMEM((2, units, half), BF16),
            pltpu.VMEM((2, 4, count, half), BF16),
            pltpu.VMEM((2, 4, count, half), BF16),
            pltpu.VMEM((2, 2, count // 2, half), BF16),
            pltpu.VMEM((2, 2, count, half), BF16),
            pltpu.VMEM((2, count, half), BF16),
            pltpu.VMEM((2, count, half), BF16),
            pltpu.VMEM((4, total, columns), BF16),
            pltpu.VMEM((width // columns + 2, units, columns), BF16),
            pltpu.SemaphoreType.DMA((2,)),
            pltpu.SemaphoreType.DMA((2,)),
            pltpu.SemaphoreType.DMA((4,)),
            pltpu.SemaphoreType.DMA((width // columns + 2,)),
            pltpu.SemaphoreType.REGULAR((2,)),
            pltpu.SemaphoreType.DMA((copies,)),
            pltpu.SemaphoreType.DMA((copies,)),
            pltpu.SemaphoreType.DMA((4,)),
        ],
        compiler_params=pltpu.CompilerParams(
            collective_id=6, has_side_effects=True, vmem_limit_bytes=62 * 1024 * 1024
        ),
        cost_estimate=pl.CostEstimate(
            flops=8 * 2 * total * units * width, bytes_accessed=160 * 3 * 1024 * 1024, transcendentals=0
        ),
        name="feed_back",
    )(*ins)


def unite_columns(moves, half_ref, shard_ref):
    d = lax.axis_index("dp")
    z = lax.axis_index("seq")
    part, width = half_ref.shape[0], shard_ref.shape[1]
    target = shard_ref.at[pl.ds(pl.multiple_of(d * part, 64), part)]

    def columns(mask):
        return half_ref.at[:, pl.ds(pl.multiple_of((d ^ mask) * width, 128), width)]

    moves.here(columns(0), target)
    for mask in FAR_FIRST:
        moves.far(columns(mask), target, d ^ mask, z)


def along_z(value):
    return lax.all_gather(value, "seq", axis=0, tiled=True)


def sum_along_z(grad):
    return lax.psum_scatter(grad, "seq", scatter_dimension=0, tiled=True)


def shared_heads(grad):
    heads = HEADS // PLANE
    held = grad.reshape(heads, 2, -1, grad.shape[-1])
    second = lax.axis_index("dp") % 2 == 1
    keep = jnp.where(second, held[:, 1], held[:, 0])
    other = swap(jnp.where(second, held[:, 0], held[:, 1]), CORE)
    whole = jnp.concatenate([jnp.where(second, other, keep), jnp.where(second, keep, other)])
    return whole.reshape(-1, grad.shape[-1])


def chips_gather(rows, second):
    half = rows.shape[0] // 2
    x_rows = swap(rows, X_WAY)
    y_rows = swap(rows, Y_WAY)
    corner_first = swap(after(y_rows[:half], second), X_WAY)
    corner_second = swap(after(x_rows[half:], second), Y_WAY)
    return jnp.concatenate([rows, x_rows, y_rows, corner_first, corner_second])


class Scatter:
    def __init__(self, chips, others):
        self.chips = chips
        self.got = swap(others, CORE)
        self.count = chips.shape[0] // 4

    def both(self, start, size):
        return sum(part[start : start + size].astype(F32) for part in (self.chips, self.got))

    def corners(self, tied):
        half = self.count // 2
        self.got, tied = lax.optimization_barrier((self.got, tied))
        at = 3 * self.count
        self.far = (
            swap(self.both(at, half).astype(BF16), X_WAY),
            swap(self.both(at + half, half).astype(BF16), Y_WAY),
        )
        self.near = (
            swap(self.both(self.count, half).astype(BF16), X_WAY),
            swap(self.both(2 * self.count + half, half).astype(BF16), Y_WAY),
        )
        return tied

    def sides(self, tied):
        half = self.count // 2
        self.far, self.near, tied = lax.optimization_barrier((self.far, self.near, tied))
        x_second = self.both(self.count + half, half) + self.far[1].astype(F32)
        y_first = self.both(2 * self.count, half) + self.far[0].astype(F32)
        self.last = swap(x_second.astype(BF16), X_WAY), swap(y_first.astype(BF16), Y_WAY)
        return tied

    def ends(self, tied):
        self.last, tied = lax.optimization_barrier((self.last, tied))
        return tied

    def result(self):
        half = self.count // 2
        first = self.both(0, half) + self.near[0].astype(F32) + self.last[1].astype(F32)
        second = self.both(half, half) + self.last[0].astype(F32) + self.near[1].astype(F32)
        return jnp.concatenate([first, second])


def place_of(mask):
    return (mask & 1) * (PLANE // 2) + (mask >> 1)


def column_of(holder, member, number):
    head = (2 * (member & 1) + number) * (PLANE // 2) + (member >> 1)
    place = place_of(holder ^ (head >> 1))
    return pl.ds(pl.multiple_of((2 * place + (head & 1)) * HEAD_DIM, HEAD_DIM), HEAD_DIM)


def meet_heads(masks):
    d = lax.axis_index("dp")
    z = lax.axis_index("seq")
    core = d & 1
    groups = lax.axis_size("seq")
    inside = (z >> 1) == core
    barrier = pltpu.get_barrier_semaphore()

    def greet(to_d, to_z, maybe_itself):
        def signal():
            pl.semaphore_signal(barrier, inc=1, **at_plane(to_d, to_z))

        when(jnp.logical_or(to_d != d, to_z != z) if maybe_itself else None, signal)

    for line in range(PLANE // 2):
        for to_z in range(groups):
            greet(((d >> 1) ^ line) * 2 + (z >> 1), to_z, line == 0)
    for mask in range(PLANE):
        for j in range(2):
            greet(d ^ mask, 2 * core + j, mask == 0)
    for mask in masks:
        greet(d ^ mask, z, False)
    pl.semaphore_wait(barrier, 4 * PLANE + len(masks) - jnp.where(inside, 2, 0))


def contexts_home_kernel(chip_ref, other_ref, rows_ref, out_ref, out_chips, out_others, *sems):
    moves = Moves(*sems)
    d = lax.axis_index("dp")
    z = lax.axis_index("seq")
    core = d & 1
    heads = HEADS // PLANE
    half = out_ref.shape[1]
    meet_heads((CORE, X_WAY, Y_WAY))
    comes = []
    for j in range(2):
        comes += [2 * core + j != z] * heads + [None] * ((PLANE - 1) * heads)
    for line in (3, 1, 2, 0):
        to_d = ((d >> 1) ^ line) * 2 + (z >> 1)
        for slot, source in ((0, chip_ref), (1, other_ref)):
            for part in range(2):
                to_z = 2 * (core ^ slot) + part
                itself = jnp.logical_and(to_d == d, to_z == z)
                for number in range(heads):
                    here = source.at[
                        line, pl.ds(part * half, half), pl.ds(number * HEAD_DIM, HEAD_DIM)
                    ]
                    there = out_ref.at[z & 1, :, column_of(to_d, d, number)]
                    moves.far(
                        here,
                        there,
                        to_d,
                        to_z,
                        jnp.logical_not(itself) if line == 0 else None,
                        comes[moves.count[0]],
                        ((z & 1) * PLANE + (d ^ to_d)) * heads + number,
                    )
                    if line == 0:
                        moves.here(here, there, itself)
    for _ in gather_rows(moves, rows_ref, out_chips, out_others):
        pass
    moves.finish()


def contexts_home(context, out_rows):
    lines, rows, columns = context[0].shape
    count, width = out_rows.shape
    heads = HEADS // PLANE
    out, chips, others = kernel_call(
        contexts_home_kernel,
        [*context, out_rows],
        [
            shaped(2, rows // 2, width),
            shaped(4, count, width),
            shaped(4, count, width),
        ],
        2 * PLANE * heads + GATHER_COPIES,
        4 * heads + 1,
        3,
        "contexts_home",
        60,
    )
    chips, others = (part.reshape(-1, width) for part in (chips, others))
    return out.reshape(rows, width), chips, others


def gradients_out_kernel(count, in_ref, *refs):
    sums, out_ref, shards = refs[:count], refs[count], refs[count + 1 : 2 * count + 1]
    moves = Moves(*refs[2 * count + 1 :])
    d = lax.axis_index("dp")
    z = lax.axis_index("seq")
    core = d & 1
    heads = HEADS // PLANE
    half = in_ref.shape[1]
    meet_heads(range(1, PLANE))
    comes = []
    for side in range(2):
        for line in range(PLANE // 2):
            for part in range(2):
                itself = jnp.logical_and((z >> 1) == core, 2 * (core ^ side) + part == z)
                comes += [jnp.logical_not(itself) if line == 0 else None] * heads
    for mask in FAR_FIRST + (0,):
        for j in range(2):
            to_d = d ^ mask
            to_z = 2 * core + j
            line = mask >> 1
            side = (to_d & 1) ^ (z >> 1)
            for number in range(heads):
                here = in_ref.at[j, :, column_of(d, to_d, number)]
                there = out_ref.at[
                    side,
                    line,
                    pl.ds(pl.multiple_of((z & 1) * half, half), half),
                    pl.ds(number * HEAD_DIM, HEAD_DIM),
                ]
                moves.far(
                    here,
                    there,
                    to_d,
                    to_z,
                    to_z != z if mask == 0 else None,
                    comes[moves.count[0]],
                    ((side * (PLANE // 2) + line) * 2 + (z & 1)) * heads + number,
                )
                if mask == 0:
                    moves.here(here, there, to_z == z)
    for held, shard in zip(sums, shards):
        unite_columns(moves, held, shard)
    moves.finish()


def gradients_out(grad, sums, late):
    rows, width = grad.shape
    heads = HEADS // PLANE
    count = len(sums)
    return kernel_call(
        lambda *refs: gradients_out_kernel(count, *refs),
        [grad.reshape(2, rows // 2, width), *sums],
        [shaped(2, PLANE // 2, rows, heads * HEAD_DIM)]
        + [shaped(s.shape[0] * PLANE, s.shape[1] // PLANE) for s in sums],
        2 * PLANE * heads + count * (PLANE - 1),
        2 * heads + count,
        4,
        "gradients_out",
        50,
        late=late,
    )


SEQS = 4


def masked_scores(left, right, first_row, first_column, row_axis, flag, full_len):
    plain = lax.dot_general(
        left, right, (((1,), (1,)), ((), ())), preferred_element_type=F32
    ) * (1.0 / math.sqrt(HEAD_DIM))
    rows = first_row + lax.broadcasted_iota(jnp.int32, plain.shape, row_axis)
    columns = first_column + lax.broadcasted_iota(jnp.int32, plain.shape, 1 - row_axis)
    seen = jnp.logical_or(flag == 1, columns % (full_len // 2) < full_len // 4)
    return jnp.where(jnp.logical_and(columns <= rows, seen), plain, NEGATIVE)


def attend_kernel(half, block, core, flag, qkv, context, lse):
    for part in range(2):
        here = part ^ core
        for first in range(0, half, block):
            query = qkv[here][0, first : first + block, :HEAD_DIM]
            spans = [(here, part, first + block)]
            if part == 1:
                spans = [(core, 0, half)] + spans
            scores = []
            for slot, place, length in spans:
                keys = qkv[slot][0, :length, HEAD_DIM : 2 * HEAD_DIM]
                scores.append(
                    masked_scores(
                        query, keys, part * half + first, place * half, 0, flag, 2 * half
                    )
                )
            top = jnp.max(scores[0], axis=-1, keepdims=True)
            for more in scores[1:]:
                top = jnp.maximum(top, jnp.max(more, axis=-1, keepdims=True))
            expd = [jnp.exp(piece - top) for piece in scores]
            total = sum(jnp.sum(piece, axis=-1, keepdims=True) for piece in expd)
            result = 0.0
            for (slot, _, length), piece in zip(spans, expd):
                values = qkv[slot][0, :length, 2 * HEAD_DIM :]
                result = result + jnp.dot(
                    (piece / total).astype(BF16), values, preferred_element_type=F32
                )
            context[here][0, first : first + block, :] = result.astype(BF16)
            wide = jnp.broadcast_to(top + jnp.log(total), (block, HEAD_DIM))
            lse[here][0, 0, :, first : first + block] = jnp.transpose(wide)[:8]


def attend(qkv, flags, heads):
    half = qkv[0].shape[1]
    spot = lambda s, h: (s, 0, h)

    def kernel(flags_ref, *refs):
        for core in range(2):

            @pl.when(flags_ref[SEQS] == core)
            def _():
                flag = flags_ref[pl.program_id(0)]
                attend_kernel(half, half // 2, core, flag, refs[:2], refs[2:4], refs[4:])

    out = pl.pallas_call(
        kernel,
        grid=(SEQS, heads),
        in_specs=[pl.BlockSpec(memory_space=pltpu.SMEM)]
        + [pl.BlockSpec((1, half, 3 * HEAD_DIM), spot)] * 2,
        out_specs=[pl.BlockSpec((1, half, HEAD_DIM), spot)] * 2
        + [pl.BlockSpec((1, 1, 8, half), lambda s, h: (s, h, 0, 0))] * 2,
        out_shape=[jax.ShapeDtypeStruct((SEQS, half, heads * HEAD_DIM), BF16)] * 2
        + [jax.ShapeDtypeStruct((SEQS, heads, 8, half), F32)] * 2,
        cost_estimate=pl.CostEstimate(
            flops=48 * heads * half * half * HEAD_DIM,
            bytes_accessed=64 * heads * half * HEAD_DIM,
            transcendentals=16 * heads * half * half,
        ),
        name="attend",
    )(flags, *qkv)
    return out[:2], out[2:]


def attend_back_kernel(half, block, core, flag, qkv, grads, lse, out, grad_keys, grad_values):
    scale = 1.0 / math.sqrt(HEAD_DIM)
    grad_keys[...] = jnp.zeros_like(grad_keys)
    grad_values[...] = jnp.zeros_like(grad_values)
    for part in range(2):
        here = part ^ core
        for first in range(0, half, block):
            query = qkv[here][0, first : first + block, :HEAD_DIM]
            grad = grads[here, 0, first : first + block, :]
            level = lse[here][0, 0, 0:1, first : first + block]
            spans = [(here, part, first + block)]
            if part == 1:
                spans = [(core, 0, half)] + spans
            held = []
            weighted = 0.0
            for slot, place, length in spans:
                keys = qkv[slot][0, :length, HEAD_DIM : 2 * HEAD_DIM]
                values = qkv[slot][0, :length, 2 * HEAD_DIM :]
                scores = masked_scores(
                    keys, query, part * half + first, place * half, 1, flag, 2 * half
                )
                probs = jnp.exp(scores - level)
                grad_values[place, :length, :] += jnp.dot(
                    probs.astype(BF16), grad, preferred_element_type=F32
                )
                grad_probs = lax.dot_general(
                    values, grad, (((1,), (1,)), ((), ())), preferred_element_type=F32
                )
                weighted = weighted + jnp.sum(probs * grad_probs, axis=0, keepdims=True)
                held.append((probs, grad_probs, keys))
            grad_query = 0.0
            for (_, place, length), (probs, grad_probs, keys) in zip(spans, held):
                grad_scores = (probs * (grad_probs - weighted)).astype(BF16)
                grad_keys[place, :length, :] += jnp.dot(
                    grad_scores, query, preferred_element_type=F32
                )
                grad_query = grad_query + lax.dot_general(
                    grad_scores, keys, (((0,), (0,)), ((), ())), preferred_element_type=F32
                )
            out[here][0, first : first + block, :HEAD_DIM] = (grad_query * scale).astype(BF16)
    for part in range(2):
        target = out[part ^ core]
        target[0, :, HEAD_DIM : 2 * HEAD_DIM] = (grad_keys[part] * scale).astype(BF16)
        target[0, :, 2 * HEAD_DIM :] = grad_values[part].astype(BF16)


def attend_back(qkv, grads, lse, flags, heads):
    half = qkv[0].shape[1]
    spot = lambda s, h: (s, 0, h)

    def kernel(flags_ref, *refs):
        for core in range(2):

            @pl.when(flags_ref[SEQS] == core)
            def _():
                flag = flags_ref[pl.program_id(0)]
                attend_back_kernel(
                    half, half // 2, core, flag, refs[:2], refs[2], refs[3:5], refs[5:7], *refs[7:]
                )

    return pl.pallas_call(
        kernel,
        grid=(SEQS, heads),
        in_specs=[pl.BlockSpec(memory_space=pltpu.SMEM)]
        + [pl.BlockSpec((1, half, 3 * HEAD_DIM), spot)] * 2
        + [pl.BlockSpec((2, 1, half, HEAD_DIM), lambda s, h: (0, s, 0, h))]
        + [pl.BlockSpec((1, 1, 8, half), lambda s, h: (s, h, 0, 0))] * 2,
        out_specs=[pl.BlockSpec((1, half, 3 * HEAD_DIM), spot)] * 2,
        out_shape=[jax.ShapeDtypeStruct(qkv[0].shape, BF16)] * 2,
        scratch_shapes=[
            pltpu.VMEM((2, half, HEAD_DIM), F32),
            pltpu.VMEM((2, half, HEAD_DIM), F32),
        ],
        cost_estimate=pl.CostEstimate(
            flops=128 * heads * half * half * HEAD_DIM,
            bytes_accessed=128 * heads * half * HEAD_DIM,
            transcendentals=16 * heads * half * half,
        ),
        name="attend_back",
    )(flags, *qkv, grads, *lse)


def sum_everywhere_kernel(number, in_ref, *refs):
    held, out_ref, shards = refs[:number], refs[number], refs[number + 1 : 2 * number + 1]
    got = refs[2 * number + 1]
    moves = Moves(*refs[2 * number + 2 :])
    d = lax.axis_index("dp")
    z = lax.axis_index("seq")
    groups = lax.axis_size("seq")
    count = in_ref.shape[0]
    me = d * groups + z
    barrier = pltpu.get_barrier_semaphore()
    for step in range(1, count):
        to = (me + step) % count
        pl.semaphore_signal(barrier, inc=1, **at_plane(to // groups, to % groups))
    pl.semaphore_wait(barrier, count - 1)
    arrivals = []
    for step in range(1, count):
        to = (me + step) % count
        arrivals.append(moves.far(in_ref.at[to], got.at[step - 1], to // groups, to % groups))
    for held_ref, shard_ref in zip(held, shards):
        unite_columns(moves, held_ref, shard_ref)
    total = in_ref[me]
    for step, arrival in enumerate(arrivals):
        moves.landed(arrival)
        total = total + got[step]
    out_ref[...] = total
    moves.finish()


def sum_everywhere(sums, held):
    count = lax.axis_size("dp") * lax.axis_size("seq")
    kinds, width = sums.shape
    piece = width // count
    lanes = 128
    pieces = jnp.transpose(sums.reshape(kinds, count, piece), (1, 0, 2))
    pieces = pieces.reshape(count, kinds * piece // lanes, lanes)
    number = len(held)
    far = count - 1 + number * (PLANE - 1)
    summed, *shards = pl.pallas_call(
        lambda *refs: sum_everywhere_kernel(number, *refs),
        out_shape=[jax.ShapeDtypeStruct(pieces.shape[1:], F32)]
        + [shaped(h.shape[0] * PLANE, h.shape[1] // PLANE) for h in held],
        in_specs=[pl.BlockSpec(memory_space=pltpu.VMEM)] * (1 + number),
        out_specs=[pl.BlockSpec(memory_space=pltpu.VMEM)]
        + [pl.BlockSpec(memory_space=pl.ANY)] * number,
        scratch_shapes=[
            pltpu.VMEM((count - 1,) + pieces.shape[1:], F32),
            pltpu.SemaphoreType.DMA((far,)),
            pltpu.SemaphoreType.DMA((far,)),
            pltpu.SemaphoreType.DMA((number,)),
        ],
        compiler_params=pltpu.CompilerParams(collective_id=0, has_side_effects=True),
        cost_estimate=pl.CostEstimate(
            flops=0, bytes_accessed=40 * 1024 * 1024, transcendentals=0
        ),
        name="sum_everywhere",
    )(pieces, *held)
    return summed.reshape(kinds, piece), shards


def grouped_shards(
    tokens,
    token_types,
    view_mask,
    type_table,
    ln1_gain,
    ln1_bias,
    w_qkv,
    w_out,
    ln2_gain,
    ln2_bias,
    w_up,
    w_down,
    cotangent,
):
    seq_count, local_len, width = tokens.shape
    groups = lax.axis_size("seq")
    rows = seq_count * local_len
    heads = HEADS // PLANE
    d = lax.axis_index("dp")
    z = lax.axis_index("seq")

    small = jnp.concatenate(
        [type_table, jnp.stack([ln1_gain, ln1_bias, ln2_gain, ln2_bias])], axis=0
    )
    mark = jnp.broadcast_to(view_mask[:, None, None], (seq_count, 4, 128)).reshape(8, 128)
    out_columns = along_z(jnp.transpose(w_out))
    small, marks = intake(small, mark)
    small = jnp.swapaxes(small, 0, 1).reshape(2 * TYPES, width).astype(F32)
    table = small[:TYPES]
    gain_one, bias_one, gain_two, bias_two = (small[TYPES + i] for i in range(4))
    marks = lax.dynamic_index_in_dim(marks[:, ::4, 0], z & 1, 1, keepdims=False)
    marks = lax.dynamic_index_in_dim(
        marks.reshape(SEQS, 2), (d & 1) ^ (z >> 1), 1, keepdims=False
    )
    flags = jnp.concatenate([marks, (d & 1)[None]])

    types = token_types.reshape(rows)
    onehot = (types[:, None] == jnp.arange(TYPES, dtype=jnp.int32)[None, :]).astype(F32)
    start_hidden = tokens.reshape(rows, width).astype(F32) + jnp.dot(
        onehot, table, precision=HIGHEST_PRECISION
    )
    cot = cotangent.reshape(rows, width)
    norm_one, pull_one = jax.vjp(layer_norm, start_hidden, gain_one, bias_one)
    chips, others, qkv_full, up_half, down_half = first_gather(
        norm_one.astype(BF16).reshape(tokens.shape),
        jnp.transpose(w_qkv),
        jnp.transpose(w_up),
        w_down,
        [out_columns],
    )
    up_full = along_z(up_half)
    down_full = along_z(down_half)
    normed = [part.reshape(4 * rows, width) for part in (chips, others)]
    qkv_full = qkv_full[:4].reshape(-1, width)
    qkv = [
        jnp.einsum("td,ed->te", part, qkv_full, preferred_element_type=F32)
        .astype(BF16)
        .reshape(SEQS, rows, 3 * heads * HEAD_DIM)
        for part in normed
    ]
    context, lse = attend(qkv, flags, heads)
    context_rows, out_chips, out_others = contexts_home(context, jnp.transpose(out_columns))
    cot_chips = chips_gather(after(cot, chips), context)
    mid_hidden = (
        start_hidden
        + jnp.dot(context_rows[:, : width // 2], out_chips, preferred_element_type=F32)
        + jnp.dot(context_rows[:, width // 2 :], out_others, preferred_element_type=F32)
    )
    norm_two, pull_two = jax.vjp(layer_norm, mid_hidden, gain_two, bias_two)
    ffn_input, cot_others, ups = gather_multiply(
        norm_two.astype(BF16), cot_chips, up_full, 5
    )
    cot_chips, ups = lax.optimization_barrier((cot_chips, ups))
    cots = (cot_chips, cot_others)
    def weight_grad(left, right):
        return sum(
            jnp.einsum("ti,td->id", a, b, preferred_element_type=F32)
            for a, b in zip(left, right)
        ).astype(BF16)

    acts = []
    grad_ups = []
    for cot_part, up_value in zip(cots, ups):
        grad_act = jnp.einsum("td,id->ti", cot_part, down_full, preferred_element_type=F32)
        activated, gelu_pull = jax.vjp(gelu_tanh, up_value)
        acts.append(activated.astype(BF16))
        grad_ups.append(gelu_pull(grad_act)[0].astype(BF16))
    grad_normed_two, ffn_out, up_parts, down_grad = feed_back(
        grad_ups, acts, up_full, down_full, ffn_input, cots
    )
    up_sum = jnp.sum(up_parts.astype(F32), axis=0).astype(BF16)
    grad_normed_two = grad_normed_two.astype(F32)
    grad_mid_norm, grad_gain_two, grad_bias_two = pull_two(grad_normed_two)
    grad_mid = cot.astype(F32) + grad_mid_norm
    grad_mid_low = grad_mid.astype(BF16)
    grad_context = jnp.concatenate(
        [
            jnp.einsum("te,de->td", grad_mid_low, part, preferred_element_type=F32).astype(BF16)
            for part in (out_chips, out_others)
        ],
        axis=1,
    )
    output = (mid_hidden + ffn_out.astype(F32)).astype(BF16).reshape(tokens.shape)
    grad_out_weight = [
        jnp.einsum("td,te->de", part, grad_mid_low, preferred_element_type=F32).astype(BF16)
        for part in jnp.split(context_rows, 2, axis=1)
    ]
    out_scatter = Scatter(*grad_out_weight)
    grad_by_heads, up_shard = gradients_out(grad_context, [up_sum], [])
    grad_by_heads, down_grad = lax.optimization_barrier((grad_by_heads, down_grad))
    down_sum = sum_along_z(down_grad)
    grad_by_heads = out_scatter.corners(grad_by_heads)
    grad_qkv = attend_back(qkv, grad_by_heads, lse, flags, heads)
    grad_qkv = [part.reshape(SEQS * rows, 3 * heads * HEAD_DIM) for part in grad_qkv]
    grad_qkv = out_scatter.sides(grad_qkv)
    late_grad = out_scatter.ends(grad_qkv[1])
    qkv_grad = shared_heads(weight_grad((grad_qkv[0], late_grad), normed))
    qkv_sum = sum_along_z(qkv_grad)
    grad_normed_one, out_sum, sum_down = last_scatter(
        grad_qkv, qkv_full, out_scatter.result().astype(BF16), down_sum, tokens.shape
    )
    grad_normed_one = grad_normed_one.astype(F32)
    grad_start_norm, grad_gain_one, grad_bias_one = pull_one(grad_normed_one.reshape(rows, width))
    grad_start = grad_mid + grad_start_norm
    grad_table = jnp.einsum("tk,td->kd", onehot, grad_start, precision=HIGHEST_PRECISION)
    sums = jnp.concatenate(
        [
            grad_table,
            jnp.stack([grad_gain_one, grad_bias_one, grad_gain_two, grad_bias_two]),
        ],
        axis=0,
    )
    sums, (qkv_shard,) = sum_everywhere(sums, [qkv_sum])
    sum_qkv = jnp.transpose(qkv_shard)
    sum_up = jnp.transpose(up_shard)
    return (
        output,
        grad_start.reshape(tokens.shape),
        sums[:TYPES],
        sums[TYPES],
        sums[TYPES + 1],
        sum_qkv.astype(F32),
        out_sum.astype(F32),
        sums[TYPES + 2],
        sums[TYPES + 3],
        sum_up.astype(F32),
        sum_down.astype(F32),
    )


def solution(mesh):
    placed = (
        P("dp", "seq", None),
        P("dp", "seq"),
        P("dp"),
        P(None, "seq"),
        P("seq"),
        P("seq"),
        P("dp", "seq"),
        P("dp", "seq"),
        P("seq"),
        P("seq"),
        P("dp", "seq"),
        P("seq", "dp"),
        P("dp", "seq", None),
    )
    fits = mesh.shape["dp"] == 8 and mesh.shape["seq"] == 4
    return jax.shard_map(
        grouped_shards if fits else plain_shards,
        mesh=mesh,
        in_specs=placed,
        out_specs=(
            P("dp", "seq", None),
            P("dp", "seq", None),
            P(None, ("dp", "seq")),
            P(("dp", "seq")),
            P(("dp", "seq")),
            P("dp", "seq"),
            P("dp", "seq"),
            P(("dp", "seq")),
            P(("dp", "seq")),
            P("dp", "seq"),
            P("seq", "dp"),
        ),
        check_vma=False,
    )
```
